32 devices in a mesh: outer: 2 (over y), local: 4 (over x, core), tensor: 4 (over z).
Axes of the slice: x: 2, y: 2, z: 4, core: 2. Of those that a mesh axis runs over, the one named last changes fastest.
Arguments:
- tokens: bfloat16 [32, 512, 768], P(('outer', 'local')), may hold values from -6 to 6
- segments: int32 [32, 512], P(('outer', 'local')), may hold values from 0 to 3, never falling along the last dimension, each value on 1 to 256 neighbouring positions
- w_qkv: bfloat16 [3, 768, 768], P(None, None, 'tensor'), may hold values from -0.21875 to 0.21875
- b_qv: float32 [2, 12, 64], P(None, 'tensor'), may hold values from -3 to 3
- w_out: bfloat16 [768, 768], P('tensor'), may hold values from -1.75 to 1.75
- w_in: bfloat16 [768, 3072], P(None, 'tensor'), may hold values from -0.21875 to 0.21875
- b_inner: float32 [48, 64], P('tensor'), may hold values from -3 to 3
- w_down: bfloat16 [3072, 768], P('tensor'), may hold values from -0.109375 to 0.109375
- gains: float32 [2, 768], replicated, may hold values from 0.1 to 1.9
- shifts: float32 [4, 768], replicated, may hold values from -3 to 3
- cotangent: bfloat16 [32, 512, 768], P(('outer', 'local')), may hold values from -6 to 6
Outputs:
- output: bfloat16 [32, 512, 768], P(('outer', 'local'))
- grad_tokens: float32 [32, 512, 768], P(('outer', 'local'))
- grad_w_qkv: float32 [3, 768, 768], P(None, 'local', 'tensor')
- grad_b_qv: float32 [2, 12, 64], P(None, 'tensor', 'local')
- grad_w_out: float32 [768, 768], P('tensor', 'local')
- grad_w_in: float32 [768, 3072], P('local', 'tensor')
- grad_b_inner: float32 [48, 64], P('tensor', 'local')
- grad_w_down: float32 [3072, 768], P('tensor', 'local')
- grad_gains: float32 [2, 768], P(None, 'local')
- grad_shifts: float32 [4, 768], P(None, 'local')
The draws below stay inside these ranges and needn't reach their ends.
Inputs may be any that keep to these rules, and one draw needn't show every extreme that they name: `segments`: in each row the document numbers never fall; each document holds 1 to 256 tokens and some document holds exactly 256.
All inputs are finite; a program needn't handle non-finite values.
Results may differ from the reference program's by a relative error of at most 0.015.
Values may be sent and summed in bfloat16 or wider, within the bound.
No kernel may reach another device: no remote copies, remote signals or barrier semaphores. Data moves between devices by JAX's collectives and lax.ppermute only.
A program may use at most 192 MiB of HBM per device.

```python
import math
import jax
import jax.numpy as jnp
import numpy as np
from jax import lax

D = 768
HEADS = 12
HD = 64
FF = 3072
LEN = 512
DOCS = 4
SEQS = 32


def block_levels(stream_key, shape, pieces, least, top_value):
    def one(axis_at, parts):
        steps = jax.random.uniform(jax.random.fold_in(jax.random.fold_in(stream_key, 6), axis_at), (parts,), jnp.float32, least / len(pieces), top_value / len(pieces))
        return jnp.repeat(jnp.exp(steps), shape[axis_at] // parts).reshape((-1,) + (1,) * (len(shape) - axis_at - 1))

    factor_of = one(*pieces[0])
    for cut in pieces[1:]:
        factor_of = factor_of * one(*cut)
    return factor_of


def length_profile(number_of, total, most, skew):
    weights = [(1 << 20) // math.isqrt(standing ** skew) + 1 for standing in range(2, number_of + 1)]
    spare, counts = total - most - (number_of - 1), [1] * (number_of - 1)
    while spare > 0:
        free = [i for i in range(number_of - 1) if counts[i] < most]
        mass, remaining = sum([weights[i] for i in free]), spare
        for i in free:
            addition = min(most - counts[i], max(1, remaining * weights[i] // mass), spare)
            counts[i] = counts[i] + addition
            spare = spare - addition
    return np.array([most] + counts)


def uneven_parts(own_key, count, total, bound, lean):
    if count == 2:
        one = jax.random.randint(own_key, (), max(1, total - bound), min(bound, total - 1) + 1)
        return jnp.stack([one, total - one])
    lengths = jnp.asarray(length_profile(count, total, bound, lean), jnp.int32)
    pairs = (count - 1) // 2
    donor, sink = lengths[1:1 + 2 * pairs:2], lengths[2:2 + 2 * pairs:2]
    slack = jnp.minimum(donor - 1, bound - sink)
    moved = jax.random.randint(jax.random.fold_in(own_key, 1), (pairs,), 0, 1 << 20) % (slack + 1)
    lengths = lengths.at[1:1 + 2 * pairs:2].set(donor - moved).at[2:2 + 2 * pairs:2].set(sink + moved)
    return lengths[jax.random.permutation(jax.random.fold_in(own_key, 2), count)]


def scatter_about(own_key, dims, scale, limit, shards=(), kind=jnp.bfloat16):
    drawn = scale * jax.random.normal(own_key, dims, jnp.float32)
    if shards:
        drawn = drawn * block_levels(own_key, dims, shards, -0.22, 0.18)
    return jnp.clip(drawn, -limit, limit).astype(kind)


def setup_inputs(seed: int = 0) -> dict:
    seeds = jax.random.split(jax.random.key(seed), 12)
    return {
        "tokens": scatter_about(seeds[0], (SEQS, LEN, D), 1.0, 6.0, ((0, 8),)),
        "segments": jax.vmap(lambda own: jnp.searchsorted(jnp.cumsum(uneven_parts(own, DOCS, LEN, LEN // 2, 0)), jnp.arange(LEN), side="right"))(jax.random.split(seeds[1], SEQS)).reshape((SEQS, LEN)).astype(jnp.int32),
        "w_qkv": scatter_about(seeds[2], (3, D, D), D ** -0.5, 0.21875, ((2, 4),)),
        "b_qv": scatter_about(seeds[3], (2, HEADS, HD), 0.5, 3.0, ((1, 4),), jnp.float32),
        "w_out": scatter_about(seeds[4], (D, D), (D * 8 // LEN) ** -0.5, 1.75, ((0, 4),)),
        "w_in": scatter_about(seeds[5], (D, FF), D ** -0.5, 0.21875, ((1, 4),)),
        "b_inner": scatter_about(seeds[6], (FF // HD, HD), 0.5, 3.0, ((0, 4),), jnp.float32),
        "w_down": scatter_about(seeds[7], (FF, D), FF ** -0.5, 0.109375, ((0, 4),)),
        "gains": jnp.clip(1.0 + 0.18 * jax.random.normal(seeds[8], (2, D), jnp.float32), 0.1, 1.9),
        "shifts": scatter_about(seeds[9], (4, D), 0.5, 3.0, (), jnp.float32),
        "cotangent": scatter_about(seeds[10], (SEQS, LEN, D), 1.0, 6.0, ((0, 8),)),
    }


EPSILON = 1e-12
MASKED = -1e+30

@jax.custom_vjp
def low(v):
    return lax.optimization_barrier(v.astype(jnp.bfloat16)).astype(jnp.float32)

@jax.custom_vjp
def low_back(v):
    return v

def low_keep(v):
    return (low(v), None)

def low_pass(kept, grad):
    return (grad,)

def back_keep(v):
    return (v, None)

def back_low(kept, grad):
    return (low(grad),)
low.defvjp(low_keep, low_pass)
low_back.defvjp(back_keep, back_low)

def matmul(left, right):
    return jnp.dot(left, right, precision=lax.Precision.HIGHEST)

def layer_norm(values, gain, shift):
    centre = values - lax.optimization_barrier(jnp.mean(values, axis=-1, keepdims=True))
    variance = lax.optimization_barrier(jnp.mean(centre * centre, axis=-1, keepdims=True))
    return centre * lax.rsqrt(variance + EPSILON) * gain + shift

def forward(inputs, segments, w_qkv, b_qv, w_out, w_in, b_inner, w_down, gains, shifts):
    seq_count = inputs.shape[0]
    tok_rows = seq_count * LEN
    flat_tokens = inputs.reshape(tok_rows, D)
    queries = low(low_back(matmul(flat_tokens, w_qkv[0])) + b_qv[0].reshape(D))
    key_proj = low(low_back(matmul(flat_tokens, w_qkv[1])))
    values = low(low_back(matmul(flat_tokens, w_qkv[2])) + b_qv[1].reshape(D))
    head_shape = (seq_count, LEN, HEADS, HD)
    raw_scores = jnp.einsum('sqhe,skhe->shqk', queries.reshape(head_shape), key_proj.reshape(head_shape), precision=lax.Precision.HIGHEST)
    scores = low_back(raw_scores) * HD ** (-0.5)
    allowed = segments[:, None, :, None] == segments[:, None, None, :]
    probs = jax.nn.softmax(jnp.where(allowed, scores, MASKED), axis=-1)
    context = jnp.einsum('shqk,skhe->sqhe', low(probs), values.reshape(head_shape), precision=lax.Precision.HIGHEST)
    context = low(low_back(context.reshape(tok_rows, D)))
    attention = low_back(matmul(context, w_out))
    hidden1 = layer_norm(flat_tokens + attention + shifts[0], gains[0], shifts[1])
    pre_act = low_back(matmul(low(hidden1), w_in)) + b_inner.reshape(FF)
    activation = low(jax.nn.gelu(pre_act, approximate=False))
    feed = low_back(matmul(activation, w_down))
    result = layer_norm(hidden1 + feed + shifts[2], gains[1], shifts[3])
    return result.reshape(seq_count, LEN, D)

def reference(tokens, segments, w_qkv, b_qv, w_out, w_in, b_inner, w_down, gains, shifts, cotangent):
    group_size = math.gcd(SEQS, 8)
    group_count = SEQS // group_size
    weights = (w_qkv.astype(jnp.float32), b_qv.astype(jnp.float32), w_out.astype(jnp.float32), w_in.astype(jnp.float32), b_inner.astype(jnp.float32), w_down.astype(jnp.float32), gains.astype(jnp.float32), shifts.astype(jnp.float32))
    inputs = tokens.astype(jnp.float32).reshape(group_count, group_size, LEN, D)
    seg_groups = segments.reshape(group_count, group_size, LEN)
    cot_groups = cotangent.astype(jnp.float32).reshape(group_count, group_size, LEN, D)

    def scan_step(accum, scan_items):
        block_inputs, block_segments, block_cot = scan_items

        def closure(inputs_now, *params):
            return forward(inputs_now, block_segments, *params)
        result, pullback = jax.vjp(closure, block_inputs, *weights)
        gradients = pullback(block_cot)
        accum = tuple((earlier + update for earlier, update in zip(accum, gradients[1:])))
        return (accum, (result.astype(jnp.bfloat16), gradients[0]))
    zero_grads = tuple((jnp.zeros_like(weight) for weight in weights))
    accum, (outputs, grad_inputs) = lax.scan(scan_step, zero_grads, (inputs, seg_groups, cot_groups))
    return (outputs.reshape(SEQS, LEN, D), grad_inputs.reshape(SEQS, LEN, D), accum[0], accum[1], accum[2], accum[3], accum[4], accum[5], accum[6], accum[7])
```

```python
import math

import jax
import jax.numpy as jnp
from jax import lax
from jax.sharding import PartitionSpec as P

EPSILON = 1e-12
MASKED = -1e30
BF = jnp.bfloat16
F32 = jnp.float32


def normalize(values):
    centre = values - jnp.mean(values, axis=-1, keepdims=True)
    variance = jnp.mean(centre * centre, axis=-1, keepdims=True)
    recip = lax.rsqrt(variance + EPSILON)
    return (centre * recip, recip)


def norm_back(grad_norm, normed, recip):
    first = jnp.mean(grad_norm, axis=-1, keepdims=True)
    second = jnp.mean(grad_norm * normed, axis=-1, keepdims=True)
    return recip * (grad_norm - first - normed * second)


def gelu_slope(values):
    cumul = 0.5 * (1.0 + lax.erf(values * (1.0 / math.sqrt(2.0))))
    return cumul + values * jnp.exp(-0.5 * values * values) * (1.0 / math.sqrt(2.0 * math.pi))


def swap(value, axis, size, bit):
    return lax.ppermute(value, axis, [(i, i ^ bit) for i in range(size)])


def ordered(own, got, bit, axis):
    first = jnp.where(bit == 0, own, got)
    second = jnp.where(bit == 0, got, own)
    return jnp.stack([first, second], axis)


def line_gather(own, size):
    right = [None, lax.ppermute(own, "tensor", [(i, i + 1) for i in range(size - 1)])]
    left = [None, lax.ppermute(own, "tensor", [(i + 1, i) for i in range(size - 1)])]
    for step in range(2, size):
        right.append(lax.ppermute(right[-1], "tensor", [(i, i + 1) for i in range(step - 1, size - 1)]))
        left.append(lax.ppermute(left[-1], "tensor", [(i + 1, i) for i in range(size - step)]))
    place = lax.axis_index("tensor")
    return [own] + [jnp.where(place >= s, right[s], left[size - s]) for s in range(1, size)]


def make(sizes):
    n_outer, n_local, n_tensor = sizes["outer"], sizes["local"], sizes["tensor"]

    def local(tokens, segments, w_qkv, b_qv, w_out, w_in, b_inner, w_down, gains, shifts, cotangent):
        seq_count, seq_len, width = tokens.shape
        heads, head_size = b_qv.shape[1], b_qv.shape[2]
        head_cols = heads * head_size
        hidden_cols = w_in.shape[1]
        rows = seq_count * seq_len
        own_rows = rows // n_tensor
        own_seqs = seq_count // n_tensor
        scale = head_size ** (-0.5)
        z = lax.axis_index("tensor")
        l_index = lax.axis_index("local")
        core, x = l_index & 1, l_index >> 1
        o_index = lax.axis_index("outer")
        y = o_index & 1
        z_from = lambda s: jnp.mod(z - s, n_tensor)
        z_to = lambda s: jnp.mod(z + s, n_tensor)
        cyclic = lambda v, s: lax.ppermute(v, "tensor", [(i, (i + s) % n_tensor) for i in range(n_tensor)])

        def gather(pack):
            piece_rows = pack.shape[0] // 8
            piece = lax.dynamic_slice_in_dim(pack, (core * 4 + y * 2 + x) * piece_rows, piece_rows, 0)
            got = jnp.stack(line_gather(piece, n_tensor)[1:])
            half = width // 2
            a, b = got[..., :half], got[..., half:]
            a = ordered(a, swap(a, "local", n_local, 2), x, 1)
            b = ordered(b, swap(b, "outer", n_outer, 1), y, 1)
            a = ordered(a, swap(a, "outer", n_outer, 1), y, 1)
            b = ordered(b, swap(b, "local", n_local, 2), x, 2)
            both = jnp.concatenate([a, b], -1)
            both = ordered(both, swap(both, "local", n_local, 1), core, 1)
            both = both.reshape(n_tensor - 1, pack.shape[0], width)
            return jnp.concatenate([pack[None], both])

        qkv_rows = w_qkv.transpose(0, 2, 1).reshape(3 * head_cols, width)
        out_all = gather(w_out)
        in_all = gather(w_in)
        down_all = gather(w_down)
        qkv_all = gather(qkv_rows).reshape(n_tensor, 3, head_cols, width)
        biases = jnp.concatenate([b_inner.reshape(-1), b_qv.reshape(-1)])
        bias_all = jnp.stack([biases] + [cyclic(biases, s) for s in range(1, n_tensor)])
        b_inner_all = bias_all[:, :hidden_cols]
        b_qv_all = bias_all[:, hidden_cols:].reshape(n_tensor, 2, head_cols)

        flat_tokens = tokens.reshape(rows, width)
        projected = jnp.einsum("td,cdh->cth", flat_tokens, w_qkv, preferred_element_type=F32)
        shape = (seq_count, seq_len, heads, head_size)
        queries = (projected[0] + b_qv[0].reshape(-1)).astype(BF).reshape(shape)
        keys = projected[1].astype(BF).reshape(shape)
        values = (projected[2] + b_qv[1].reshape(-1)).astype(BF).reshape(shape)
        allowed = segments[:, None, :, None] == segments[:, None, None, :]
        scores = jnp.einsum("sqhe,skhe->shqk", queries, keys, preferred_element_type=F32)
        probs = jax.nn.softmax(jnp.where(allowed, scores * scale, MASKED), axis=-1).astype(BF)
        context = jnp.einsum("shqk,skhe->sqhe", probs, values, preferred_element_type=F32)
        context = context.astype(BF).reshape(n_tensor, own_rows, head_cols)
        pick = lambda v, i: lax.dynamic_index_in_dim(v, i, 0, keepdims=False)
        ctx = [pick(context, z)] + [cyclic(pick(context, z_to(s)), s) for s in range(1, n_tensor)]

        own_tokens = pick(tokens.reshape(n_tensor, own_rows, width), z)
        own_cot = pick(cotangent.reshape(n_tensor, own_rows, width), z).astype(F32)
        ctx_all = jnp.stack(ctx)
        attention = jnp.einsum("sth,shd->td", ctx_all, out_all, preferred_element_type=F32)
        norm_one, recip_one = normalize(own_tokens.astype(F32) + attention + shifts[0])
        hidden1 = norm_one * gains[0] + shifts[1]
        hidden_low = hidden1.astype(BF)
        pre_act = jnp.einsum("td,sdf->stf", hidden_low, in_all, preferred_element_type=F32)
        pre_act = pre_act + b_inner_all[:, None, :]
        activation = jax.nn.gelu(pre_act, approximate=False).astype(BF)
        feed = jnp.einsum("stf,sfd->td", activation, down_all, preferred_element_type=F32)
        norm_two, recip_two = normalize(hidden1 + feed + shifts[2])
        output_own = (norm_two * gains[1] + shifts[3]).astype(BF)

        def spread(own):
            parts = line_gather(own, n_tensor)
            whole = jnp.zeros((n_tensor,) + own.shape, own.dtype)
            for s in range(n_tensor):
                whole = lax.dynamic_update_index_in_dim(whole, parts[s], z_from(s), 0)
            return whole.reshape(seq_count, seq_len, width)

        output = spread(output_own)

        place = x * 4 + core * 2 + y

        def relative(value):
            blocks = value.T.reshape(8, width // 8, own_rows)
            return jnp.stack([pick(blocks, place ^ r) for r in range(8)])

        def scatter(left, right):
            part = left.reshape(2, 2, 2 * (width // 8), own_rows)
            mul = lambda v: jnp.einsum("xdt,stn->xsdn", v, right, preferred_element_type=F32)
            keep, send = mul(part[:, 0]), mul(part[:, 1]).astype(BF)
            total = keep + swap(send, "local", n_local, 1).astype(F32)
            total = total[0] + swap(total[1].astype(BF), "local", n_local, 2).astype(F32)
            half = width // 8
            total = total[:, :half] + swap(total[:, half:].astype(BF), "outer", n_outer, 1).astype(F32)
            mine = total[0]
            for s in range(1, n_tensor):
                mine = mine + cyclic(total[s].astype(BF), n_tensor - s).astype(F32)
            bit = 2
            while bit < n_outer:
                mine = mine + swap(mine.astype(BF), "outer", n_outer, bit).astype(F32)
                bit *= 2
            other = swap(mine.astype(BF), "outer", n_outer, 1).astype(F32)
            return ordered(mine, other, y, 0).reshape(2 * half, mine.shape[-1])

        grad_gain2 = jnp.sum(own_cot * norm_two, axis=0)
        grad_beta2 = jnp.sum(own_cot, axis=0)
        grad_r2 = norm_back(own_cot * gains[1], norm_two, recip_two)
        grad_bdown = jnp.sum(grad_r2, axis=0)
        grad_r2_low = grad_r2.astype(BF)
        done_wdown = scatter(relative(grad_r2_low), activation)
        grad_act = jnp.einsum("td,sfd->stf", grad_r2_low, down_all, preferred_element_type=F32)
        grad_pre = grad_act * gelu_slope(pre_act)
        grad_binner = jnp.sum(grad_pre, axis=1)
        grad_pre_low = grad_pre.astype(BF)
        done_win = scatter(relative(hidden_low), grad_pre_low)
        entry_ffn = jnp.einsum("stf,sdf->td", grad_pre_low, in_all, preferred_element_type=F32)
        grad_h1 = grad_r2 + entry_ffn
        grad_gain1 = jnp.sum(grad_h1 * norm_one, axis=0)
        grad_beta1 = jnp.sum(grad_h1, axis=0)
        grad_r1 = norm_back(grad_h1 * gains[0], norm_one, recip_one)
        grad_bout = jnp.sum(grad_r1, axis=0)
        grad_r1_low = grad_r1.astype(BF)
        done_wout = scatter(relative(grad_r1_low), ctx_all)
        grad_context = jnp.einsum("td,shd->sth", grad_r1_low, out_all, preferred_element_type=F32)
        all_heads = (n_tensor, own_seqs, seq_len, heads, head_size)
        grad_context = grad_context.astype(BF).reshape(all_heads)

        own_proj = jnp.einsum("td,schd->csth", own_tokens, qkv_all, preferred_element_type=F32)
        q = (own_proj[0] + b_qv_all[:, 0, None, :]).astype(BF).reshape(all_heads)
        k = own_proj[1].astype(BF).reshape(all_heads)
        v = (own_proj[2] + b_qv_all[:, 1, None, :]).astype(BF).reshape(all_heads)
        own_segments = pick(segments.reshape(n_tensor, own_seqs, seq_len), z)
        own_allowed = own_segments[None, :, None, :, None] == own_segments[None, :, None, None, :]
        own_scores = jnp.einsum("znqhe,znkhe->znhqk", q, k, preferred_element_type=F32)
        own_probs = jax.nn.softmax(jnp.where(own_allowed, own_scores * scale, MASKED), axis=-1)
        grad_probs = jnp.einsum("znqhe,znkhe->znhqk", grad_context, v, preferred_element_type=F32)
        inner = jnp.sum(own_probs * grad_probs, axis=-1, keepdims=True)
        grad_scores = (own_probs * (grad_probs - inner) * scale).astype(BF)
        grad_q = jnp.einsum("znhqk,znkhe->znqhe", grad_scores, k, preferred_element_type=F32)
        grad_k = jnp.einsum("znhqk,znqhe->znkhe", grad_scores, q, preferred_element_type=F32)
        grad_v = jnp.einsum("znhqk,znqhe->znkhe", own_probs.astype(BF), grad_context, preferred_element_type=F32)
        flat = lambda g: g.reshape(n_tensor, own_rows, head_cols)
        grad_bqv = jnp.stack([jnp.sum(flat(grad_q), 1), jnp.sum(flat(grad_v), 1)], 1)
        grad_proj = jnp.concatenate([flat(grad_q), flat(grad_k), flat(grad_v)], -1).astype(BF)
        qkv_cat = qkv_all.reshape(n_tensor, 3 * head_cols, width)
        entry_attn = jnp.einsum("sth,shd->td", grad_proj, qkv_cat, preferred_element_type=F32)
        grad_tokens = spread((grad_r1 + entry_attn).astype(BF)).astype(F32)
        done_wqkv = scatter(relative(own_tokens), grad_proj)

        slot_vec = jnp.concatenate([grad_binner, grad_bqv.reshape(n_tensor, -1)], 1)
        placed = jnp.zeros_like(slot_vec)
        for s in range(n_tensor):
            placed = lax.dynamic_update_index_in_dim(placed, slot_vec[s], z_from(s), 0)
        common = jnp.stack([grad_gain1, grad_gain2, grad_bout, grad_beta1, grad_bdown, grad_beta2])
        vectors = lax.psum(jnp.concatenate([placed.reshape(-1), common.reshape(-1)]), ("outer", "local", "tensor"))
        slot_sum = pick(vectors[: placed.size].reshape(placed.shape), z)
        common = vectors[placed.size :].reshape(common.shape)
        part = lambda v, n: lax.dynamic_slice_in_dim(v, l_index * (n // n_local), n // n_local, v.ndim - 1)
        binner = part(slot_sum[:hidden_cols].reshape(b_inner.shape), head_size)
        bqv = part(slot_sum[hidden_cols:].reshape(b_qv.shape), head_size)
        common = part(common, width)
        grad_wqkv = done_wqkv.reshape(width // n_local, 3, head_cols).transpose(1, 0, 2)
        return (
            output,
            grad_tokens,
            grad_wqkv,
            bqv,
            done_wout.T,
            done_win,
            binner,
            done_wdown.T,
            common[:2],
            common[2:],
        )

    return local


def solution(mesh):
    placed = (
        P(("outer", "local"), None, None),
        P(("outer", "local"), None),
        P(None, None, "tensor"),
        P(None, "tensor", None),
        P("tensor", None),
        P(None, "tensor"),
        P("tensor", None),
        P("tensor", None),
        P(),
        P(),
        P(("outer", "local"), None, None),
    )
    return jax.shard_map(
        make(dict(mesh.shape)),
        mesh=mesh,
        in_specs=placed,
        out_specs=(
            P(("outer", "local"), None, None),
            P(("outer", "local"), None, None),
            P(None, "local", "tensor"),
            P(None, "tensor", "local"),
            P("tensor", "local"),
            P("local", "tensor"),
            P("tensor", "local"),
            P("tensor", "local"),
            P(None, "local"),
            P(None, "local"),
        ),
        check_vma=False,
    )
```

```python
import functools
import math

import jax
import jax.numpy as jnp
from jax import lax
from jax.experimental import pallas as pl
from jax.experimental.pallas import tpu as pltpu
from jax.sharding import PartitionSpec as P

EPSILON = 1e-12
MASKED = -1e30
BF = jnp.bfloat16
F32 = jnp.float32
SHORT = pl.CostEstimate(flops=1000, bytes_accessed=1000, transcendentals=0)
ROWS_BY_ROWS = (((1,), (1,)), ((), ()))


def dot(left, right):
    return jnp.dot(left, right, preferred_element_type=F32)


def dot_t(left, right):
    return lax.dot_general(left, right, ROWS_BY_ROWS, preferred_element_type=F32)


def normalize(values):
    centre = values - jnp.mean(values, axis=-1, keepdims=True)
    variance = jnp.mean(centre * centre, axis=-1, keepdims=True)
    recip = lax.rsqrt(variance + EPSILON)
    return (centre * recip, recip)


def norm_back(grad_norm, normed, recip):
    first = jnp.mean(grad_norm, axis=-1, keepdims=True)
    second = jnp.mean(grad_norm * normed, axis=-1, keepdims=True)
    return recip * (grad_norm - first - normed * second)


def col_sum(value):
    return jnp.sum(value, axis=0, keepdims=True)


def softmax_columns(raw, allowed):
    scores = jnp.where(allowed, raw, MASKED)
    grown = jnp.exp(scores - jnp.max(scores, axis=0, keepdims=True))
    return grown, 1.0 / jnp.sum(grown, axis=0, keepdims=True)


def column(row):
    return jnp.broadcast_to(row, (8, row.shape[1])).T[:, :1]


def store_relative(out_ref, value, at_ref):
    flipped = value.T.astype(BF)
    block = flipped.shape[0] // 8
    for i in range(8):
        spot = (((i >> 1) & 1) ^ at_ref[0]) * 4 + ((i >> 2) ^ at_ref[1]) * 2 + ((i & 1) ^ at_ref[2])
        out_ref[pl.ds(pl.multiple_of(spot * block, block), block)] = flipped[i * block : (i + 1) * block]


def call(kernel, name, at, grid, in_specs, out_specs, out_shape, scratch=()):
    return pl.pallas_call(
        kernel,
        grid_spec=pltpu.PrefetchScalarGridSpec(
            num_scalar_prefetch=1, grid=grid, in_specs=in_specs, out_specs=out_specs, scratch_shapes=list(scratch)
        ),
        out_shape=out_shape,
        cost_estimate=SHORT,
        name=name,
    )


def const(*shape):
    return pl.BlockSpec(shape, lambda i, at: (0,) * len(shape))


def slot(*shape):
    return pl.BlockSpec((1, *shape), lambda i, at: (i,) + (0,) * len(shape))


def attend_kernel(heads, scale, at_ref, x_ref, w_ref, bias_ref, seg_ref, extra_ref, *out_refs):
    x = x_ref[0]
    size = w_ref.shape[1] // heads
    q_t = ((dot_t(w_ref[0], x) + column(bias_ref[0:1])).astype(BF) * scale).astype(BF)
    k = dot_t(x, w_ref[1]).astype(BF)
    v_t = (dot_t(w_ref[2], x) + column(bias_ref[1:2])).astype(BF)
    row = seg_ref[pl.ds(pl.program_id(0), 1)].astype(F32)
    allowed = column(row) == row
    parts = []
    for h in range(heads):
        at = slice(h * size, (h + 1) * size)
        grown, inv = softmax_columns(dot(k[:, at], q_t[at]), allowed)
        parts.append(dot(v_t[at], grown.astype(BF)) * inv)
    context = jnp.concatenate(parts, 0).T.astype(BF)
    count = len(out_refs)
    ahead = lax.rem(pl.program_id(0) + count - at_ref[3], count)
    for s, out_ref in enumerate(out_refs):
        @pl.when(ahead == s)
        def _():
            out_ref[: context.shape[0]] = context
            out_ref[context.shape[0] :] = extra_ref[...]


def attend(at, tokens, w_rows, bias, segments, heads, extra):
    seqs, length, width = tokens.shape
    cols = w_rows.shape[1]
    return call(
        functools.partial(attend_kernel, heads, (cols // heads) ** -0.5), "attend", at, (seqs,),
        [slot(length, width), const(3, cols, width), const(2, cols), const(seqs, length), const(*extra.shape)],
        [const(length + extra.shape[0], cols)] * seqs,
        [jax.ShapeDtypeStruct((length + extra.shape[0], cols), BF)] * seqs,
    )(at, tokens, w_rows, bias, segments, extra)


def fetch_copies(core, own_ref, mine_ref, theirs_ref, held, sems):
    slots = held.shape[0]
    copies = [[pltpu.make_async_copy(own_ref.at[c], held.at[0, c], sems.at[0, c]) for c in range(2)]]
    for s in range(1, slots):
        copies.append([
            pltpu.make_async_copy(mine_ref.at[:, s - 1], held.at[s, core], sems.at[s, 0]),
            pltpu.make_async_copy(theirs_ref.at[:, s - 1], held.at[s, 1 - core], sems.at[s, 1]),
        ])
    return copies


def fetch_slot(at_ref, refs, held, sems):
    step = pl.program_id(0)
    copies = fetch_copies(at_ref[0], *refs, held, sems)

    @pl.when(step == 0)
    def _():
        for pair in copies:
            for copy in pair:
                copy.start()

    for s, pair in enumerate(copies):
        @pl.when(step == s)
        def _():
            for copy in pair:
                copy.wait()

    return held[step].reshape(8 * held.shape[3], held.shape[4])


def pieces(weight):
    own, mine, theirs = weight
    piece = own.shape[0] // 8
    split = lambda v: v.reshape(4, -1, piece, own.shape[1])
    return own.reshape(2, 4, piece, own.shape[1]), split(mine), split(theirs)


def held_scratch(slots, weight):
    rows, width = weight[0].shape
    return [pltpu.VMEM((slots, 2, 4, rows // 8, width), BF), pltpu.SemaphoreType.DMA((slots, 2))]


def here(*shape):
    return pl.BlockSpec((1, *shape), lambda i, at: (at[3],) + (0,) * len(shape))


FAR = pl.BlockSpec(memory_space=pl.ANY)


def rise_kernel(slots, at_ref, *refs):
    ctx_refs = refs[:slots]
    (w_out_ref, x_ref, gains_ref, shifts_ref, own_ref, mine_ref, theirs_ref, bias_ref,
     hidden_ref, low_ref, norm_ref, recip_ref, act_ref, slope_ref, x_rel_ref, hidden_rel_ref, held, sems) = refs[slots:]
    step = pl.program_id(0)
    weight = fetch_slot(at_ref, (own_ref, mine_ref, theirs_ref), held, sems)

    @pl.when(step == 0)
    def _():
        rows = low_ref.shape[0]
        attention = dot(ctx_refs[0][:rows], w_out_ref[0])
        for s in range(1, slots):
            attention += dot(ctx_refs[s][:rows], w_out_ref[s])
        own = x_ref[0].astype(F32)
        norm, recip = normalize(own + attention + shifts_ref[0:1])
        hidden = norm * gains_ref[0:1] + shifts_ref[1:2]
        norm_ref[...] = norm
        recip_ref[...] = recip
        hidden_ref[...] = hidden
        low_ref[...] = hidden.astype(BF)
        store_relative(x_rel_ref, own, at_ref)
        store_relative(hidden_rel_ref, hidden, at_ref)

    pre = dot(low_ref[...], weight) + bias_ref[0]
    cumul = 0.5 * (1.0 + lax.erf(pre * (1.0 / math.sqrt(2.0))))
    act_ref[0] = (pre * cumul).astype(BF)
    slope_ref[0] = (cumul + pre * jnp.exp(-0.5 * pre * pre) * (1.0 / math.sqrt(2.0 * math.pi))).astype(BF)


def rise(at, ctx, w_out, x, gains, shifts, w_in, bias):
    slots, cols, rows = len(ctx), ctx[0].shape[1], x.shape[1]
    width, hidden = w_in[0].shape
    return call(
        functools.partial(rise_kernel, slots), "rise", at, (slots,),
        [const(*ctx[0].shape)] * slots
        + [
            const(slots, cols, width), here(rows, width), const(*gains.shape),
            const(*shifts.shape), FAR, FAR, FAR, slot(1, hidden),
        ],
        [
            const(rows, width), const(rows, width), const(rows, width), const(rows, 1),
            slot(rows, hidden), slot(rows, hidden), const(width, rows), const(width, rows),
        ],
        [
            jax.ShapeDtypeStruct((rows, width), F32),
            jax.ShapeDtypeStruct((rows, width), BF),
            jax.ShapeDtypeStruct((rows, width), F32),
            jax.ShapeDtypeStruct((rows, 1), F32),
            jax.ShapeDtypeStruct((slots, rows, hidden), BF),
            jax.ShapeDtypeStruct((slots, rows, hidden), BF),
            jax.ShapeDtypeStruct((width, rows), BF),
            jax.ShapeDtypeStruct((width, rows), BF),
        ],
        held_scratch(slots, w_in),
    )(at, *ctx, w_out, x, gains, shifts, *pieces(w_in), bias[:, None, :])


def store_parts(keep_ref, send_ref, x_first, first, whole):
    block, last = keep_ref.shape[2], first + whole.shape[1]
    low = whole.astype(BF)
    for i in range(4):
        spot = jnp.where(x_first, i, 3 - i) if i in (1, 2) else i
        keep_ref[spot, 0, :, first:last] = low[i * block : (i + 1) * block]
        send_ref[spot, 0, :, first:last] = low[(4 + i) * block : (5 + i) * block]


def fall_kernel(slots, at_ref, act_ref, own_ref, mine_ref, theirs_ref, hidden_ref, cot_ref, gains_ref, shifts_ref,
                out_ref, grad_ref, low_ref, vec_ref, keep_ref, send_ref, sum_ref, rel_ref, held, sems):
    s = pl.program_id(0)
    copies = fetch_copies(at_ref[0], own_ref, mine_ref, theirs_ref, held, sems)

    @pl.when(s == 0)
    def _():
        for pair in copies:
            for copy in pair:
                copy.start()

    for i, pair in enumerate(copies):
        @pl.when(s == i)
        def _():
            for copy in pair:
                copy.wait()
            share = dot(act_ref[0], held[i].reshape(8 * held.shape[3], held.shape[4]))
            if i:
                sum_ref[...] += share
            else:
                sum_ref[...] = share

    @pl.when(s == slots - 1)
    def _():
        norm, recip = normalize(hidden_ref[...] + sum_ref[...] + shifts_ref[2:3])
        out_ref[...] = (norm * gains_ref[1:2] + shifts_ref[3:4]).astype(BF)
        cot = cot_ref[0].astype(F32)
        grad = norm_back(cot * gains_ref[1:2], norm, recip)
        grad_ref[...] = grad
        low_ref[...] = grad.astype(BF)
        store_relative(rel_ref, grad, at_ref)
        vec_ref[0:1] = col_sum(cot * norm)
        vec_ref[1:2] = col_sum(grad)
        vec_ref[2:3] = col_sum(cot)

    @pl.when(s >= slots)
    def _():
        store_parts(keep_ref, send_ref, s - slots < slots // 2, 0, dot(rel_ref[...], act_ref[0]))


def part_specs(slots, block, cols, start=0):
    spec = pl.BlockSpec((4, 1, block, cols), lambda i, at: (0, lax.max(i - start, 0), 0, 0))
    return [spec] * 2, [jax.ShapeDtypeStruct((4, slots, block, cols), BF)] * 2


def fall(at, act, w_down, hidden, cot, gains, shifts):
    slots, rows, inner = act.shape
    width = w_down[0].shape[1]
    specs, shapes = part_specs(slots, width // 8, inner, slots)
    return call(
        functools.partial(fall_kernel, slots), "fall", at, (2 * slots,),
        [
            pl.BlockSpec((1, rows, inner), lambda i, at: (lax.rem(i, slots), 0, 0)), FAR, FAR, FAR, const(rows, width),
            here(rows, width), const(*gains.shape), const(*shifts.shape),
        ],
        [const(rows, width), const(rows, width), const(rows, width), const(3, width), *specs],
        [
            jax.ShapeDtypeStruct((rows, width), BF),
            jax.ShapeDtypeStruct((rows, width), F32),
            jax.ShapeDtypeStruct((rows, width), BF),
            jax.ShapeDtypeStruct((3, width), F32),
            *shapes,
        ],
        [pltpu.VMEM((rows, width), F32), pltpu.VMEM((width, rows), BF)] + held_scratch(slots, w_down),
    )(at, act, *pieces(w_down), hidden, cot, gains, shifts)


def back_kernel(slots, at_ref, grad2_ref, low2_ref, own2_ref, mine2_ref, theirs2_ref, slope_ref, own1_ref, mine1_ref,
                theirs1_ref, norm_ref, recip_ref, gains_ref, hidden_rel_ref, bias_ref, grad_ref, low_ref, rel_ref, vec_ref,
                keep_ref, send_ref, sum_ref, held2, sems2, held1, sems1):
    s = pl.program_id(0)
    w_down = fetch_slot(at_ref, (own2_ref, mine2_ref, theirs2_ref), held2, sems2)
    w_in = fetch_slot(at_ref, (own1_ref, mine1_ref, theirs1_ref), held1, sems1)
    pre = dot_t(low2_ref[...], w_down) * slope_ref[0].astype(F32)
    bias_ref[0] = col_sum(pre)
    pre_low = pre.astype(BF)
    store_parts(keep_ref, send_ref, s < slots // 2, 0, dot(hidden_rel_ref[...], pre_low))
    share = dot_t(pre_low, w_in)

    @pl.when(s == 0)
    def _():
        sum_ref[...] = share

    @pl.when(s > 0)
    def _():
        sum_ref[...] += share

    @pl.when(s == slots - 1)
    def _():
        norm = norm_ref[...]
        grad_h = grad2_ref[...] + sum_ref[...]
        grad = norm_back(grad_h * gains_ref[0:1], norm, recip_ref[...])
        grad_ref[...] = grad
        low_ref[...] = grad.astype(BF)
        store_relative(rel_ref, grad, at_ref)
        vec_ref[0:1] = col_sum(grad_h * norm)
        vec_ref[1:2] = col_sum(grad)
        vec_ref[2:3] = col_sum(grad_h)


def back(at, grad2, low2, w_down, slope, w_in, norm, recip, gains, hidden_rel):
    slots, rows, inner = slope.shape
    width = grad2.shape[1]
    specs, shapes = part_specs(slots, width // 8, inner)
    return call(
        functools.partial(back_kernel, slots), "back", at, (slots,),
        [
            const(rows, width), const(rows, width), FAR, FAR, FAR, slot(rows, inner), FAR, FAR, FAR,
            const(rows, width), const(rows, 1), const(*gains.shape), const(width, rows),
        ],
        [slot(1, inner), const(rows, width), const(rows, width), const(width, rows), const(3, width), *specs],
        [
            jax.ShapeDtypeStruct((slots, 1, inner), F32),
            jax.ShapeDtypeStruct((rows, width), F32),
            jax.ShapeDtypeStruct((rows, width), BF),
            jax.ShapeDtypeStruct((width, rows), BF),
            jax.ShapeDtypeStruct((3, width), F32),
            *shapes,
        ],
        [pltpu.VMEM((rows, width), F32)] + held_scratch(slots, w_down) + held_scratch(slots, w_in),
    )(at, grad2, low2, *pieces(w_down), slope, *pieces(w_in), norm, recip, gains, hidden_rel)


def attend_back_kernel(first, slots, heads, scale, at_ref, x_ref, low_ref, grad_ref, *refs):
    ctx_refs = refs[:slots]
    (own_ref, mine_ref, theirs_ref, bias_ref, w_out_ref, seg_ref, x_rel_ref, grad_rel_ref,
     vec_ref, tok_ref, keep_ref, send_ref, sum_ref, q_ref, k_ref, v_ref, proj_ref, held, sems) = refs[slots:]
    s = pl.program_id(0)
    half = mine_ref.shape[-1]
    mine_at = pl.ds(pl.multiple_of(at_ref[0] * half, half), half)
    theirs_at = pl.ds(pl.multiple_of((1 - at_ref[0]) * half, half), half)
    copies = []
    for i in range(slots):
        if first + i == 0:
            copies.append([
                pltpu.make_async_copy(own_ref.at[:2], held.at[i, :2], sems.at[i, 0]),
                pltpu.make_async_copy(own_ref.at[2:], held.at[i, 2:], sems.at[i, 1]),
            ])
        else:
            copies.append([
                pltpu.make_async_copy(mine_ref.at[:, first + i - 1], held.at[i, :, :, mine_at], sems.at[i, 0]),
                pltpu.make_async_copy(theirs_ref.at[:, first + i - 1], held.at[i, :, :, theirs_at], sems.at[i, 1]),
            ])

    @pl.when(s == 0)
    def _():
        for pair in copies:
            for copy in pair:
                copy.start()

    for i, pair in enumerate(copies):
        @pl.when(s == i)
        def _():
            for copy in pair:
                copy.wait()
            store_parts(
                keep_ref, send_ref, i < slots // 2, proj_ref.shape[1], dot(grad_rel_ref[...], ctx_refs[i][: x_ref.shape[1]])
            )

    x, low = x_ref[0], low_ref[...]
    cols = w_out_ref.shape[1]
    size = cols // heads
    weight = held[s].reshape(3, cols, x.shape[1])
    q_t = (dot_t(weight[0], x) + column(bias_ref[0, 0:1])).astype(BF)
    q_scaled = (q_t * scale).astype(BF)
    q = q_t.T
    k_t = dot_t(weight[1], x).astype(BF)
    k = k_t.T
    v = (dot_t(x, weight[2]) + bias_ref[0, 1:2]).astype(BF)
    gc_t = dot_t(w_out_ref[0], low).astype(BF)
    gc = gc_t.T
    row = seg_ref[pl.ds(at_ref[3], 1)].astype(F32)
    allowed = column(row) == row
    for h in range(heads):
        at = slice(h * size, (h + 1) * size)
        grown, inv = softmax_columns(dot(k[:, at], q_scaled[at]), allowed)
        probs = grown * inv
        grad_probs = dot(v[:, at], gc_t[at])
        inner = jnp.sum(probs * grad_probs, axis=0, keepdims=True)
        grad_scores = (probs * (grad_probs - inner) * scale).astype(BF)
        q_ref[at] = dot(k_t[at], grad_scores)
        k_ref[:, at] = dot(grad_scores, q[:, at])
        v_ref[:, at] = dot(probs.astype(BF), gc[:, at])
    grad_q = q_ref[...].T
    grad_v = v_ref[...]
    vec_ref[0, 0:1] = col_sum(grad_q)
    vec_ref[0, 1:2] = col_sum(grad_v)
    parts = [grad_q.astype(BF), k_ref[...].astype(BF), grad_v.astype(BF)]
    for c in range(3):
        proj_ref[:, c * cols : (c + 1) * cols] = parts[c]
    proj = proj_ref[...]
    share = dot(proj, weight.reshape(3 * cols, x.shape[1]))
    store_parts(keep_ref, send_ref, s < slots // 2, 0, dot(x_rel_ref[...], proj))

    @pl.when(s == 0)
    def _():
        sum_ref[...] = share + grad_ref[...]

    @pl.when(s > 0)
    def _():
        sum_ref[...] += share

    @pl.when(s == slots - 1)
    def _():
        tok_ref[...] = sum_ref[...].astype(tok_ref.dtype)


def attend_back(at, first, x, low, grad, ctx, w_qkv, bias, heads, w_out, segments, x_rel, grad_rel, kind):
    slots, cols = len(ctx), w_out.shape[1]
    rows, width = x.shape[1:]
    own, mine, theirs = w_qkv
    piece, half = mine.shape[-2:]
    split = lambda v: v.reshape(4, -1, piece, half)
    later = lambda *shape: pl.BlockSpec((1, *shape), lambda i, at: (i + first,) + (0,) * len(shape))
    specs, shapes = part_specs(slots, width // 8, 4 * cols)
    return call(
        functools.partial(attend_back_kernel, first, slots, heads, (cols // heads) ** -0.5), "attend_back", at, (slots,),
        [here(rows, width), const(rows, width), const(rows, width)]
        + [const(*ctx[0].shape)] * slots
        + [
            FAR, FAR, FAR, later(2, cols), later(cols, width), const(*segments.shape), const(width, rows), const(width, rows),
        ],
        [slot(2, cols), const(rows, width), *specs],
        [
            jax.ShapeDtypeStruct((slots, 2, cols), F32),
            jax.ShapeDtypeStruct((rows, width), kind),
            *shapes,
        ],
        [
            pltpu.VMEM((rows, width), F32), pltpu.VMEM((cols, rows), F32), pltpu.VMEM((rows, cols), F32),
            pltpu.VMEM((rows, cols), F32), pltpu.VMEM((rows, 3 * cols), BF),
            pltpu.VMEM((slots, 4, piece, width), BF), pltpu.SemaphoreType.DMA((slots, 2)),
        ],
    )(at, x, low, grad, *ctx, own.reshape(4, piece, width), split(mine), split(theirs), bias, w_out, segments, x_rel, grad_rel)


def place_kernel(slots, at_ref, *refs):
    sources, (out_ref, held, sems) = refs[:-3], refs[-3:]
    here = at_ref[3]

    def each(step, act):
        for s in range(slots):
            for source, wanted in ((s, here - step == s),) + (((slots - 1 + s, step - here == s),) if s else ()):
                @pl.when(wanted)
                def _():
                    act(pltpu.make_async_copy(sources[source], held.at[step], sems.at[step]))

    step = pl.program_id(0)

    @pl.when(step == 0)
    def _():
        for j in range(slots):
            each(j, lambda copy: copy.start())

    pltpu.make_async_copy(sources[0], held.at[step], sems.at[step]).wait()
    out_ref[0] = held[step].astype(out_ref.dtype)


def place(at, own, behind, ahead, kind):
    slots = len(behind) + 1
    values = [own, *behind, *ahead]
    return call(
        functools.partial(place_kernel, slots), "place", at, (slots,),
        [FAR] * len(values), slot(*own.shape),
        jax.ShapeDtypeStruct((slots, *own.shape), kind),
        [pltpu.VMEM((slots, *own.shape), own.dtype), pltpu.SemaphoreType.DMA((slots,))],
    )(at, *values)


def swap(value, axis, size, bit):
    return lax.ppermute(value, axis, [(i, i ^ bit) for i in range(size)])


def ordered(own, got, bit, axis):
    first = jnp.where(bit == 0, own, got)
    second = jnp.where(bit == 0, got, own)
    return jnp.stack([first, second], axis)


def in_three(value):
    high = value.astype(BF)
    rest = value - high.astype(F32)
    middle = rest.astype(BF)
    return jnp.stack([high, middle, (rest - middle.astype(F32)).astype(BF)])


class Order:
    def __init__(self):
        self.last = ()

    def hold(self, values, *waits):
        leaves, tree = jax.tree.flatten(values)
        held = lax.optimization_barrier((leaves, self.last, waits))[0]
        return jax.tree.unflatten(tree, held)

    def done(self, *values):
        self.last = tuple(values)

    def run(self, made, *waits):
        self.last = waits
        made = self.hold(made)
        self.last = tuple(jax.tree.leaves(made)[:1])
        return made


def make(sizes):
    n_outer, n_local, n_tensor = sizes["outer"], sizes["local"], sizes["tensor"]

    def local(tokens, segments, w_qkv, b_qv, w_out, w_in, b_inner, w_down, gains, shifts, cotangent):
        seq_count, seq_len, width = tokens.shape
        heads, head_size = b_qv.shape[1], b_qv.shape[2]
        head_cols = heads * head_size
        hidden_cols = w_in.shape[1]
        z = lax.axis_index("tensor")
        l_index = lax.axis_index("local")
        core, x = l_index & 1, l_index >> 1
        y = lax.axis_index("outer") & 1
        z_from = lambda s: jnp.mod(z - s, n_tensor)
        z_to = lambda s: jnp.mod(z + s, n_tensor)
        cyclic = lambda v, s: lax.ppermute(v, "tensor", [(i, (i + s) % n_tensor) for i in range(n_tensor)])
        pick = lambda v, i: lax.dynamic_index_in_dim(v, i, 0, keepdims=False)
        others = range(1, n_tensor)
        by_x = lambda v: swap(v, "local", n_local, 2)
        by_y = lambda v: swap(v, "outer", n_outer, 1)
        by_core = lambda v: swap(v, "local", n_local, 1)
        at = jnp.stack([core, x, y, z]).astype(jnp.int32)
        order = Order()
        hold, done, run = order.hold, order.done, order.run

        place8 = core * 4 + y * 2 + x
        half = width // 2

        def piece_of(weight):
            n = weight.shape[0] // 8
            return lax.dynamic_slice_in_dim(weight, place8 * n, n, 0)

        def halves(parts, rows):
            return jnp.stack([p[rows, :half] for p in parts]), jnp.stack([p[rows, half:] for p in parts])

        def plane_two(a, b, a1, b1):
            return ordered(a, a1, x, 0), ordered(b, b1, y, 0)

        def plane_three(a, b, a1, b1, rows):
            a, a1, b, b1 = (v[:, :, rows] for v in (a, a1, b, b1))
            return jnp.concatenate([ordered(a, a1, y, 0), ordered(b, b1, x, 1)], -1)

        qkv_rows = w_qkv.transpose(0, 2, 1)
        flat_qkv = qkv_rows.reshape(3 * head_cols, width)

        first = jnp.concatenate([piece_of(w_out), piece_of(w_in), piece_of(w_down)])
        first_z = [cyclic(first, s) for s in others]
        done(first)
        biases = jnp.concatenate([b_inner.reshape(-1), b_qv.reshape(-1)])
        bias_rows = -(-biases.size // head_cols)
        bias_pack = in_three(jnp.pad(hold(biases), (0, bias_rows * head_cols - biases.size)).reshape(bias_rows, head_cols))
        bias_pack = jnp.pad(bias_pack.reshape(3 * bias_rows, head_cols), ((0, -3 * bias_rows % 16), (0, 0)))

        context = attend(at, hold(tokens), qkv_rows, b_qv.reshape(2, head_cols), segments, heads, bias_pack)
        (ctx_own, *ctx_send), first_z = run((context, first_z))
        ctx_z = [cyclic(v, s) for v, s in zip(ctx_send, others)]
        cut, end = w_out.shape[0] // 8, (w_out.shape[0] + w_in.shape[0]) // 8
        a, b = halves(first_z, slice(0, end))
        a1, b1 = by_x(a), by_y(b)
        c, d = halves(first_z, slice(end, None))
        piece_qkv = lax.dynamic_slice(
            hold(flat_qkv), ((y * 2 + x) * (flat_qkv.shape[0] // 4), core * half), (flat_qkv.shape[0] // 4, half)
        )
        done(c, d, piece_qkv, a1, b1)
        a, b = plane_two(*hold((a, b, a1, b1)))
        a1, b1 = by_y(a), by_x(b)
        done(a, b, *ctx_z)
        ctx_z = hold(ctx_z)
        c1, d1 = by_x(hold(c)), by_y(hold(d))
        bias_got = jnp.stack([p[seq_len : seq_len + 3 * bias_rows] for p in ctx_z]).astype(F32)
        bias_got = bias_got.reshape(n_tensor - 1, 3, bias_rows * head_cols)
        bias_got = bias_got[:, 0] + bias_got[:, 1] + bias_got[:, 2]
        bias_all = jnp.concatenate([biases[None], bias_got[:, : biases.size]])
        b_inner_all = bias_all[:, :hidden_cols]
        b_qv_all = bias_all[:, hidden_cols:].reshape(n_tensor, 2, head_cols)
        done(b_inner_all, a1, b1)
        a, b, a1, b1 = hold((a, b, a1, b1))
        in_both = plane_three(a, b, a1, b1, slice(cut, None))
        in_core = by_core(in_both)
        out_both = plane_three(a, b, a1, b1, slice(0, cut))
        out_core = by_core(out_both)
        third_z = [cyclic(hold(piece_qkv), s) for s in others]
        done(in_both, out_both, c1, d1)
        c, d = plane_two(*hold((c, d, c1, d1)))
        c1, d1 = by_y(c), by_x(d)
        done(c, d, out_core, in_core)
        out_got = ordered(*hold((out_both, out_core)), core, 0).transpose(3, 0, 1, 2, 4, 5)
        out_all = jnp.concatenate([w_out[None], out_got.reshape(n_tensor - 1, *w_out.shape)])
        in_parts = (w_in, in_both, in_core)
        done(out_all, in_core)
        ctx = [ctx_own, *ctx_z]
        made = rise(at, hold(ctx), out_all, tokens, gains, shifts, in_parts, b_inner_all)
        made, c1, d1, third_z = run((made, c1, d1, third_z))
        hidden1, hidden_low, norm_one, recip_one, activation, slope, tokens_rel, hidden_rel = made
        down_both = plane_three(c, d, c1, d1, slice(None))
        down_core = by_core(down_both)
        e = jnp.stack(third_z)
        e1 = by_x(e)
        done(down_both, down_core, e)
        down_parts = (w_down, down_both, down_core)
        made = fall(at, hold(activation), down_parts, hidden1, cotangent, gains, shifts)
        made, e1 = run((made, e1))
        output_own, grad_r2, grad_r2_low, vec_two, keep1, send1 = made

        steps = [(i, i + 1) for i in range(n_tensor - 1)]
        back_steps = [(i + 1, i) for i in range(n_tensor - 1)]

        def hop(right, left, step):
            return (
                lax.ppermute(right, "tensor", steps[step:]),
                lax.ppermute(left, "tensor", back_steps[: len(steps) - step]),
            )

        block = width // 8

        class Part:
            def __init__(self, slots, *arrays):
                self.parts = [v[:, slots].reshape(2, 2, -1, *v.shape[2:]) for v in arrays]

            def total(self, *index):
                terms = [p[index].astype(F32) for p in self.parts]
                return functools.reduce(lambda u, v: u + v, terms).astype(BF)

            def take(self, got):
                self.parts = [p[0] for p in self.parts]
                self.parts.append(got.reshape(self.parts[0].shape))

            def totals(self):
                return [self.total(i) for i in range(self.parts[0].shape[0])]

        def pair_of(keep, got):
            count = keep.shape[1]
            return Part(slice(0, count // 2), keep, got), Part(slice(count // 2, count), keep, got)

        def plane(by_first, by_second):
            flying = []
            for move, group in ((by_x, by_first), (by_y, by_second)):
                sends = [p.total(1) for p in group]
                flat = jnp.concatenate([v.reshape(-1, *v.shape[-2:]) for v in sends])
                done(*order.last, flat)
                flying.append(move(flat))
            return flying

        def landed(flying, *groups):
            for flat, group in zip(flying, groups):
                first = 0
                for p in group:
                    size = math.prod(p.parts[0].shape[:-2]) // 2
                    p.take(flat[first : first + size])
                    first += size

        def z_units(total):
            return [cyclic(total[s], n_tensor - s) for s in others]

        def last_sum(mine, got):
            mine = mine.astype(F32)
            for v in got:
                mine = mine + v.astype(F32)
            bit = 2
            while bit < n_outer:
                mine = mine + swap(mine.astype(BF), "outer", n_outer, bit).astype(F32)
                bit *= 2
            return mine

        def whole_rows(mine, got):
            return ordered(mine, got.astype(F32), y, 0).reshape(2 * block, mine.shape[-1])

        out_1 = hop(output_own, output_own, 0)
        core1 = by_core(send1)
        e = ordered(e, e1, x, 0)
        e1 = by_y(e)
        done(e, core1)
        h1 = pair_of(*hold((keep1, core1)))
        flight = plane([h1[0]], [h1[1]])
        made = back(
            at, hold(grad_r2), grad_r2_low, down_parts, slope, in_parts, norm_one, recip_one, gains, hidden_rel
        )
        made, e1, out_1, flight = run((made, e1, out_1, flight))
        grad_binner, grad_r1, grad_r1_low, grad_r1_rel, vec_one, keep2, send2 = made
        out_2 = hop(*out_1, 1)
        core2 = by_core(send2)
        qkv_both = ordered(e, e1, y, 0)
        qkv_core = by_core(qkv_both)
        qkv_parts = (flat_qkv, qkv_both, qkv_core)
        landed(flight, [h1[0]], [h1[1]])
        done(qkv_both, core2)
        h2 = pair_of(*hold((keep2, core2)))
        groups = [h2[0], h1[1]], [h2[1], h1[0]]
        flight = plane(*groups)
        done(*order.last, qkv_core)
        two = n_tensor // 2
        made = attend_back(
            at, 0, tokens, hold(grad_r1_low), grad_r1, ctx[:two], qkv_parts, b_qv_all, heads, out_all, segments,
            tokens_rel, grad_r1_rel, F32,
        )
        made, out_2, flight = run((made, out_2, flight))
        bqv_a, tok_a, keep_a, send_a = made
        out_3 = hop(*out_2, 2)
        core_a = by_core(send_a)
        landed(flight, *groups)
        total1 = h1[0].totals() + h1[1].totals()
        done(*total1, core_a)
        ha = pair_of(*hold((keep_a, core_a)))
        groups = [ha[0], h2[1]], [ha[1], h2[0]]
        flight = plane(*groups)
        made = attend_back(
            at, two, tokens, hold(grad_r1_low), tok_a, ctx[two:], qkv_parts, b_qv_all, heads, out_all, segments,
            tokens_rel, grad_r1_rel, BF,
        )
        made, out_3, flight = run((made, out_3, flight))
        bqv_b, tok_own, keep_b, send_b = made
        tok_1 = hop(tok_own, tok_own, 0)
        core_b = by_core(send_b)
        landed(flight, *groups)
        grad_bqv = jnp.concatenate([bqv_a, bqv_b])

        slot_vec = jnp.concatenate([grad_binner.reshape(n_tensor, -1), grad_bqv.reshape(n_tensor, -1)], 1)
        placed = jnp.zeros_like(slot_vec)
        for s in range(n_tensor):
            placed = lax.dynamic_update_index_in_dim(placed, slot_vec[s], z_from(s), 0)
        common = jnp.stack([vec_one[0], vec_two[0], vec_one[1], vec_one[2], vec_two[1], vec_two[2]])
        vectors = [jnp.concatenate([placed.reshape(-1), common.reshape(-1)])]
        rounds = [
            (axis, size, 1 << i)
            for axis, size in (("local", n_local), ("outer", n_outer), ("tensor", n_tensor))
            for i in range(size.bit_length() - 1)
        ]

        def vector_round(count=1):
            for _ in range(count):
                if len(vectors) > 1:
                    vectors[:] = [vectors[0] + hold(vectors[1])]
                if rounds:
                    vectors.append(swap(vectors[0], *rounds.pop(0)))

        total2 = h2[0].totals() + h2[1].totals()
        total12 = [jnp.stack(pair) for pair in zip(total1, total2)]
        z12 = z_units(total12)
        done(*total12, core_b)
        hb = pair_of(*hold((keep_b, core_b)))
        groups = [hb[0], ha[1]], [hb[1], ha[0]]
        flight = plane(*groups)
        outs = hold((output_own, out_1, out_2, out_3))
        output = place(at, outs[0], [v[0] for v in outs[1:]], [v[1] for v in outs[1:]], BF)
        output, tok_1 = run((output.reshape(seq_count, seq_len, width), tok_1))
        tok_2 = hop(*tok_1, 1)
        vector_round()
        done(*order.last, *flight)
        landed(hold(flight), *groups)
        groups = [hb[1]], [hb[0]]
        flight = plane(*groups)
        done(*order.last, *z12, *vectors)
        mine12 = last_sum(total12[0], hold(z12))
        got12 = by_y(mine12.astype(BF))
        vector_round()
        done(mine12, *flight)
        landed(hold(flight), *groups)
        total3 = hold([t for part in (*ha, *hb) for t in part.totals()])
        z3 = z_units(total3)
        done(*total3, *tok_2, *vectors)
        tok_3 = hop(*hold(tok_2), 2)
        vector_round()
        done(got12, *vectors)
        vector_round()
        got12 = hold(got12)
        done_wdown = whole_rows(mine12[0], got12[0])
        done_win = whole_rows(mine12[1], got12[1])
        done(done_wdown, done_win, *z3)
        mine3 = last_sum(total3[0], hold(z3))
        got3 = by_y(mine3.astype(BF))
        done(mine3, got3, *vectors)
        vector_round()
        done_last = whole_rows(mine3, hold(got3))
        done(done_last, *tok_3)
        grad_tokens = place(at, *hold((tok_own, (tok_1[0], tok_2[0], tok_3[0]), (tok_1[1], tok_2[1], tok_3[1]))), F32)
        grad_tokens = grad_tokens.reshape(seq_count, seq_len, width)
        vector_round(len(rounds) + 1)
        vectors = vectors[0]
        slot_sum = pick(vectors[: placed.size].reshape(placed.shape), z)
        common = vectors[placed.size :].reshape(common.shape)
        part = lambda v, n: lax.dynamic_slice_in_dim(v, l_index * (n // n_local), n // n_local, v.ndim - 1)
        binner = part(slot_sum[:hidden_cols].reshape(b_inner.shape), head_size)
        bqv = part(slot_sum[hidden_cols:].reshape(b_qv.shape), head_size)
        common = part(common, width)
        grad_wqkv = done_last[:, : 3 * head_cols].reshape(width // n_local, 3, head_cols).transpose(1, 0, 2)
        return (
            output,
            grad_tokens,
            grad_wqkv,
            bqv,
            done_last[:, 3 * head_cols :].T,
            done_win,
            binner,
            done_wdown.T,
            common[:2],
            common[2:],
        )

    return local


def solution(mesh):
    placed = (
        P(("outer", "local"), None, None),
        P(("outer", "local"), None),
        P(None, None, "tensor"),
        P(None, "tensor", None),
        P("tensor", None),
        P(None, "tensor"),
        P("tensor", None),
        P("tensor", None),
        P(),
        P(),
        P(("outer", "local"), None, None),
    )
    return jax.shard_map(
        make(dict(mesh.shape)),
        mesh=mesh,
        in_specs=placed,
        out_specs=(
            P(("outer", "local"), None, None),
            P(("outer", "local"), None, None),
            P(None, "local", "tensor"),
            P(None, "tensor", "local"),
            P("tensor", "local"),
            P("local", "tensor"),
            P("tensor", "local"),
            P("tensor", "local"),
            P(None, "local"),
            P(None, "local"),
        ),
        check_vma=False,
    )
```

```python
import functools
import math

import jax
import jax.numpy as jnp
from jax import lax
from jax.experimental import pallas as pl
from jax.experimental.pallas import tpu as pltpu
from jax.sharding import PartitionSpec as P

EPSILON = 1e-12
MASKED = -1e30
BF = jnp.bfloat16
F32 = jnp.float32
SHORT = pl.CostEstimate(flops=1000, bytes_accessed=1000, transcendentals=0)
ROOM = {'attend': 36, 'rise': 36, 'fall': 36, 'back': 36, 'attend_back': 48}
ROWS_BY_ROWS = (((1,), (1,)), ((), ()))


def dot(left, right):
    return jnp.dot(left, right, preferred_element_type=F32)


def dot_t(left, right):
    return lax.dot_general(left, right, ROWS_BY_ROWS, preferred_element_type=F32)


def normalize(values):
    centre = values - jnp.mean(values, axis=-1, keepdims=True)
    variance = jnp.mean(centre * centre, axis=-1, keepdims=True)
    recip = lax.rsqrt(variance + EPSILON)
    return (centre * recip, recip)


def norm_back(grad_norm, normed, recip):
    first = jnp.mean(grad_norm, axis=-1, keepdims=True)
    second = jnp.mean(grad_norm * normed, axis=-1, keepdims=True)
    return recip * (grad_norm - first - normed * second)


def col_sum(value):
    return jnp.sum(value, axis=0, keepdims=True)


def softmax_columns(raw, allowed):
    scores = jnp.where(allowed, raw, MASKED)
    grown = jnp.exp(scores - jnp.max(scores, axis=0, keepdims=True))
    return grown, 1.0 / jnp.sum(grown, axis=0, keepdims=True)


def column(row):
    return jnp.broadcast_to(row, (8, row.shape[1])).T[:, :1]


def store_relative(out_ref, value, at_ref):
    flipped = value.T.astype(BF)
    block = flipped.shape[0] // 8
    for i in range(8):
        spot = (((i >> 1) & 1) ^ at_ref[0]) * 4 + ((i >> 2) ^ at_ref[1]) * 2 + ((i & 1) ^ at_ref[2])
        out_ref[pl.ds(pl.multiple_of(spot * block, block), block)] = flipped[i * block : (i + 1) * block]


def call(kernel, name, at, grid, in_specs, out_specs, out_shape, scratch=()):
    return pl.pallas_call(
        kernel,
        grid_spec=pltpu.PrefetchScalarGridSpec(
            num_scalar_prefetch=1, grid=grid, in_specs=in_specs, out_specs=out_specs, scratch_shapes=list(scratch)
        ),
        out_shape=out_shape,
        cost_estimate=SHORT,
        compiler_params=pltpu.CompilerParams(vmem_limit_bytes=ROOM.get(name, 60) * 2**20),
        name=name,
    )


def const(*shape):
    return pl.BlockSpec(shape, lambda i, at: (0,) * len(shape))


def slot(*shape):
    return pl.BlockSpec((1, *shape), lambda i, at: (i,) + (0,) * len(shape))


def attend_kernel(heads, scale, at_ref, x_ref, w_ref, bias_ref, seg_ref, extra_ref, *out_refs):
    x = x_ref[0]
    size = w_ref.shape[1] // heads
    q_t = ((dot_t(w_ref[0], x) + column(bias_ref[0:1])).astype(BF) * scale).astype(BF)
    k = dot_t(x, w_ref[1]).astype(BF)
    v_t = (dot_t(w_ref[2], x) + column(bias_ref[1:2])).astype(BF)
    row = seg_ref[pl.ds(pl.program_id(0), 1)].astype(F32)
    allowed = column(row) == row
    parts = []
    for h in range(heads):
        at = slice(h * size, (h + 1) * size)
        grown, inv = softmax_columns(dot(k[:, at], q_t[at]), allowed)
        parts.append(dot(v_t[at], grown.astype(BF)) * inv)
    context = jnp.concatenate(parts, 0).T.astype(BF)
    count, rows, cols = len(out_refs), context.shape[0] // 2, context.shape[1]
    ahead = lax.rem(pl.program_id(0) + count - at_ref[3], count)
    for s, out_ref in enumerate(out_refs):
        @pl.when(ahead == s)
        def _():
            out_ref[:rows, :cols] = context[:rows]
            out_ref[:rows, cols:] = context[rows:]
            out_ref[rows:] = extra_ref[...]


def attend(at, tokens, w_rows, bias, segments, heads, extra):
    seqs, length, width = tokens.shape
    cols = w_rows.shape[1]
    return call(
        functools.partial(attend_kernel, heads, (cols // heads) ** -0.5), "attend", at, (seqs,),
        [slot(length, width), const(3, cols, width), const(2, cols), const(seqs, length), const(*extra.shape)],
        [const(length // 2 + extra.shape[0], 2 * cols)] * seqs,
        [jax.ShapeDtypeStruct((length // 2 + extra.shape[0], 2 * cols), BF)] * seqs,
    )(at, tokens, w_rows, bias, segments, extra)


def fetch_copies(core, own_ref, mine_ref, theirs_ref, held, sems):
    slots = held.shape[0]
    copies = [[pltpu.make_async_copy(own_ref.at[c], held.at[0, c], sems.at[0, c]) for c in range(2)]]
    for s in range(1, slots):
        copies.append([
            pltpu.make_async_copy(mine_ref.at[:, s - 1], held.at[s, core], sems.at[s, 0]),
            pltpu.make_async_copy(theirs_ref.at[:, s - 1], held.at[s, 1 - core], sems.at[s, 1]),
        ])
    return copies


def fetch_slot(at_ref, refs, held, sems):
    step = pl.program_id(0)
    copies = fetch_copies(at_ref[0], *refs, held, sems)

    @pl.when(step == 0)
    def _():
        for pair in copies:
            for copy in pair:
                copy.start()

    for s, pair in enumerate(copies):
        @pl.when(step == s)
        def _():
            for copy in pair:
                copy.wait()

    return held[step].reshape(8 * held.shape[3], held.shape[4])


def pieces(weight):
    own, mine, theirs = weight
    piece = own.shape[0] // 8
    split = lambda v: v.reshape(4, -1, piece, own.shape[1])
    return own.reshape(2, 4, piece, own.shape[1]), split(mine), split(theirs)


def held_scratch(slots, weight):
    rows, width = weight[0].shape
    return [pltpu.VMEM((slots, 2, 4, rows // 8, width), BF), pltpu.SemaphoreType.DMA((slots, 2))]


def here(*shape):
    return pl.BlockSpec((1, *shape), lambda i, at: (at[3],) + (0,) * len(shape))


FAR = pl.BlockSpec(memory_space=pl.ANY)


def rise_kernel(slots, at_ref, *refs):
    ctx_refs = refs[:slots]
    (w_out_ref, x_ref, gains_ref, shifts_ref, own_ref, mine_ref, theirs_ref, bias_ref,
     hidden_ref, low_ref, norm_ref, recip_ref, act_ref, slope_ref, x_rel_ref, hidden_rel_ref, held, sems) = refs[slots:]
    step = pl.program_id(0)
    weight = fetch_slot(at_ref, (own_ref, mine_ref, theirs_ref), held, sems)

    @pl.when(step == 0)
    def _():
        rows, cols = low_ref.shape[0] // 2, w_out_ref.shape[1]
        sides = []
        for side in (slice(0, cols), slice(cols, None)):
            share = dot(ctx_refs[0][:rows, side], w_out_ref[0])
            for s in range(1, slots):
                share += dot(ctx_refs[s][:rows, side], w_out_ref[s])
            sides.append(share)
        attention = jnp.concatenate(sides)
        own = x_ref[0].astype(F32)
        norm, recip = normalize(own + attention + shifts_ref[0:1])
        hidden = norm * gains_ref[0:1] + shifts_ref[1:2]
        norm_ref[...] = norm
        recip_ref[...] = recip
        hidden_ref[...] = hidden
        low_ref[...] = hidden.astype(BF)
        store_relative(x_rel_ref, own, at_ref)
        store_relative(hidden_rel_ref, hidden, at_ref)

    pre = dot(low_ref[...], weight) + bias_ref[0]
    cumul = 0.5 * (1.0 + lax.erf(pre * (1.0 / math.sqrt(2.0))))
    act_ref[0] = (pre * cumul).astype(BF)
    slope_ref[0] = (cumul + pre * jnp.exp(-0.5 * pre * pre) * (1.0 / math.sqrt(2.0 * math.pi))).astype(BF)


def rise(at, ctx, w_out, x, gains, shifts, w_in, bias):
    slots, cols, rows = len(ctx), w_out.shape[1], x.shape[1]
    width, hidden = w_in[0].shape
    return call(
        functools.partial(rise_kernel, slots), "rise", at, (slots,),
        [const(*ctx[0].shape)] * slots
        + [
            const(slots, cols, width), here(rows, width), const(*gains.shape),
            const(*shifts.shape), FAR, FAR, FAR, slot(1, hidden),
        ],
        [
            const(rows, width), const(rows, width), const(rows, width), const(rows, 1),
            slot(rows, hidden), slot(rows, hidden), const(width, rows), const(width, rows),
        ],
        [
            jax.ShapeDtypeStruct((rows, width), F32),
            jax.ShapeDtypeStruct((rows, width), BF),
            jax.ShapeDtypeStruct((rows, width), F32),
            jax.ShapeDtypeStruct((rows, 1), F32),
            jax.ShapeDtypeStruct((slots, rows, hidden), BF),
            jax.ShapeDtypeStruct((slots, rows, hidden), BF),
            jax.ShapeDtypeStruct((width, rows), BF),
            jax.ShapeDtypeStruct((width, rows), BF),
        ],
        held_scratch(slots, w_in),
    )(at, *ctx, w_out, x, gains, shifts, *pieces(w_in), bias[:, None, :])


def store_parts(keep_ref, send_ref, x_first, first, whole):
    block, last = keep_ref.shape[2], first + whole.shape[1]
    low = whole.astype(BF)
    for i in range(4):
        spot = jnp.where(x_first, i, 3 - i) if i in (1, 2) else i
        keep_ref[spot, 0, :, first:last] = low[i * block : (i + 1) * block]
        send_ref[spot, 0, :, first:last] = low[(4 + i) * block : (5 + i) * block]


def fall_kernel(slots, at_ref, act_ref, own_ref, mine_ref, theirs_ref, hidden_ref, cot_ref, gains_ref, shifts_ref,
                out_ref, grad_ref, low_ref, vec_ref, keep_ref, send_ref, sum_ref, rel_ref, held, sems):
    s = pl.program_id(0)
    copies = fetch_copies(at_ref[0], own_ref, mine_ref, theirs_ref, held, sems)

    @pl.when(s == 0)
    def _():
        for pair in copies:
            for copy in pair:
                copy.start()

    for i, pair in enumerate(copies):
        @pl.when(s == i)
        def _():
            for copy in pair:
                copy.wait()

    @pl.when(s == 0)
    def _():
        sum_ref[...] = jnp.zeros_like(sum_ref)

    @pl.when(s < slots)
    def _():
        sum_ref[...] += dot(act_ref[0], held[s].reshape(8 * held.shape[3], held.shape[4]))

    @pl.when(s == slots - 1)
    def _():
        norm, recip = normalize(hidden_ref[...] + sum_ref[...] + shifts_ref[2:3])
        out_ref[...] = (norm * gains_ref[1:2] + shifts_ref[3:4]).astype(BF)
        cot = cot_ref[0].astype(F32)
        grad = norm_back(cot * gains_ref[1:2], norm, recip)
        grad_ref[...] = grad
        low_ref[...] = grad.astype(BF)
        store_relative(rel_ref, grad, at_ref)
        vec_ref[0:1] = col_sum(cot * norm)
        vec_ref[1:2] = col_sum(grad)
        vec_ref[2:3] = col_sum(cot)

    @pl.when(s >= slots)
    def _():
        store_parts(keep_ref, send_ref, s - slots < slots // 2, 0, dot(rel_ref[...], act_ref[0]))


def part_specs(slots, block, cols, start=0):
    spec = pl.BlockSpec((4, 1, block, cols), lambda i, at: (0, lax.max(i - start, 0), 0, 0))
    return [spec] * 2, [jax.ShapeDtypeStruct((4, slots, block, cols), BF)] * 2


def fall(at, act, w_down, hidden, cot, gains, shifts):
    slots, rows, inner = act.shape
    width = w_down[0].shape[1]
    specs, shapes = part_specs(slots, width // 8, inner, slots)
    return call(
        functools.partial(fall_kernel, slots), "fall", at, (2 * slots,),
        [
            pl.BlockSpec((1, rows, inner), lambda i, at: (lax.rem(i, slots), 0, 0)), FAR, FAR, FAR, const(rows, width),
            here(rows, width), const(*gains.shape), const(*shifts.shape),
        ],
        [const(rows, width), const(rows, width), const(rows, width), const(3, width), *specs],
        [
            jax.ShapeDtypeStruct((rows, width), BF),
            jax.ShapeDtypeStruct((rows, width), F32),
            jax.ShapeDtypeStruct((rows, width), BF),
            jax.ShapeDtypeStruct((3, width), F32),
            *shapes,
        ],
        [pltpu.VMEM((rows, width), F32), pltpu.VMEM((width, rows), BF)] + held_scratch(slots, w_down),
    )(at, act, *pieces(w_down), hidden, cot, gains, shifts)


def back_kernel(slots, at_ref, grad2_ref, low2_ref, own2_ref, mine2_ref, theirs2_ref, slope_ref, own1_ref, mine1_ref,
                theirs1_ref, norm_ref, recip_ref, gains_ref, hidden_rel_ref, bias_ref, grad_ref, low_ref, rel_ref, vec_ref,
                keep_ref, send_ref, sum_ref, held2, sems2, held1, sems1):
    s = pl.program_id(0)
    w_down = fetch_slot(at_ref, (own2_ref, mine2_ref, theirs2_ref), held2, sems2)
    w_in = fetch_slot(at_ref, (own1_ref, mine1_ref, theirs1_ref), held1, sems1)
    pre = dot_t(low2_ref[...], w_down) * slope_ref[0].astype(F32)
    bias_ref[0] = col_sum(pre)
    pre_low = pre.astype(BF)
    store_parts(keep_ref, send_ref, s < slots // 2, 0, dot(hidden_rel_ref[...], pre_low))
    share = dot_t(pre_low, w_in)

    @pl.when(s == 0)
    def _():
        sum_ref[...] = share

    @pl.when(s > 0)
    def _():
        sum_ref[...] += share

    @pl.when(s == slots - 1)
    def _():
        norm = norm_ref[...]
        grad_h = grad2_ref[...] + sum_ref[...]
        grad = norm_back(grad_h * gains_ref[0:1], norm, recip_ref[...])
        grad_ref[...] = grad
        low_ref[...] = grad.astype(BF)
        store_relative(rel_ref, grad, at_ref)
        vec_ref[0:1] = col_sum(grad_h * norm)
        vec_ref[1:2] = col_sum(grad)
        vec_ref[2:3] = col_sum(grad_h)


def back(at, grad2, low2, w_down, slope, w_in, norm, recip, gains, hidden_rel):
    slots, rows, inner = slope.shape
    width = grad2.shape[1]
    specs, shapes = part_specs(slots, width // 8, inner)
    return call(
        functools.partial(back_kernel, slots), "back", at, (slots,),
        [
            const(rows, width), const(rows, width), FAR, FAR, FAR, slot(rows, inner), FAR, FAR, FAR,
            const(rows, width), const(rows, 1), const(*gains.shape), const(width, rows),
        ],
        [slot(1, inner), const(rows, width), const(rows, width), const(width, rows), const(3, width), *specs],
        [
            jax.ShapeDtypeStruct((slots, 1, inner), F32),
            jax.ShapeDtypeStruct((rows, width), F32),
            jax.ShapeDtypeStruct((rows, width), BF),
            jax.ShapeDtypeStruct((width, rows), BF),
            jax.ShapeDtypeStruct((3, width), F32),
            *shapes,
        ],
        [pltpu.VMEM((rows, width), F32)] + held_scratch(slots, w_down) + held_scratch(slots, w_in),
    )(at, grad2, low2, *pieces(w_down), slope, *pieces(w_in), norm, recip, gains, hidden_rel)


def attend_back_kernel(first, slots, heads, scale, at_ref, x_ref, low_ref, grad_ref, *refs):
    ctx_refs = refs[:slots]
    (own_ref, mine_ref, theirs_ref, bias_ref, w_out_ref, seg_ref, x_rel_ref, grad_rel_ref,
     vec_ref, tok_ref, keep_ref, send_ref, sum_ref, q_ref, k_ref, v_ref, ctx_ref, proj_ref, held, sems) = refs[slots:]
    s = pl.program_id(0)
    half = mine_ref.shape[-1]
    mine_at = pl.ds(pl.multiple_of(at_ref[0] * half, half), half)
    theirs_at = pl.ds(pl.multiple_of((1 - at_ref[0]) * half, half), half)
    copies = []
    for i in range(slots):
        if first + i == 0:
            copies.append([
                pltpu.make_async_copy(own_ref.at[:2], held.at[i, :2], sems.at[i, 0]),
                pltpu.make_async_copy(own_ref.at[2:], held.at[i, 2:], sems.at[i, 1]),
            ])
        else:
            copies.append([
                pltpu.make_async_copy(mine_ref.at[:, first + i - 1], held.at[i, :, :, mine_at], sems.at[i, 0]),
                pltpu.make_async_copy(theirs_ref.at[:, first + i - 1], held.at[i, :, :, theirs_at], sems.at[i, 1]),
            ])

    @pl.when(s == 0)
    def _():
        for pair in copies:
            for copy in pair:
                copy.start()

    for i, pair in enumerate(copies):
        @pl.when(s == i)
        def _():
            for copy in pair:
                copy.wait()
            rows, cols = ctx_ref.shape[0] // 2, ctx_ref.shape[1]
            ctx_ref[:rows] = ctx_refs[i][:rows, :cols]
            ctx_ref[rows:] = ctx_refs[i][:rows, cols:]

    store_parts(keep_ref, send_ref, s < slots // 2, proj_ref.shape[1], dot(grad_rel_ref[...], ctx_ref[...]))
    x, low = x_ref[0], low_ref[...]
    cols = w_out_ref.shape[1]
    size = cols // heads
    weight = held[s].reshape(3, cols, x.shape[1])
    q_t = (dot_t(weight[0], x) + column(bias_ref[0, 0:1])).astype(BF)
    q_scaled = (q_t * scale).astype(BF)
    q = q_t.T
    k_t = dot_t(weight[1], x).astype(BF)
    k = k_t.T
    v = (dot_t(x, weight[2]) + bias_ref[0, 1:2]).astype(BF)
    gc_t = dot_t(w_out_ref[0], low).astype(BF)
    gc = gc_t.T
    row = seg_ref[pl.ds(at_ref[3], 1)].astype(F32)
    allowed = column(row) == row
    for h in range(heads):
        at = slice(h * size, (h + 1) * size)
        grown, inv = softmax_columns(dot(k[:, at], q_scaled[at]), allowed)
        probs = grown * inv
        grad_probs = dot(v[:, at], gc_t[at])
        inner = jnp.sum(probs * grad_probs, axis=0, keepdims=True)
        grad_scores = (probs * (grad_probs - inner) * scale).astype(BF)
        q_ref[at] = dot(k_t[at], grad_scores)
        k_ref[:, at] = dot(grad_scores, q[:, at])
        v_ref[:, at] = dot(probs.astype(BF), gc[:, at])
    grad_q = q_ref[...].T
    grad_v = v_ref[...]
    vec_ref[0, 0:1] = col_sum(grad_q)
    vec_ref[0, 1:2] = col_sum(grad_v)
    parts = [grad_q.astype(BF), k_ref[...].astype(BF), grad_v.astype(BF)]
    for c in range(3):
        proj_ref[:, c * cols : (c + 1) * cols] = parts[c]
    proj = proj_ref[...]
    share = dot(proj, weight.reshape(3 * cols, x.shape[1]))
    store_parts(keep_ref, send_ref, s < slots // 2, 0, dot(x_rel_ref[...], proj))

    @pl.when(s == 0)
    def _():
        sum_ref[...] = share + grad_ref[...]

    @pl.when(s > 0)
    def _():
        sum_ref[...] += share

    @pl.when(s == slots - 1)
    def _():
        tok_ref[...] = sum_ref[...].astype(tok_ref.dtype)


def attend_back(at, first, x, low, grad, ctx, w_qkv, bias, heads, w_out, segments, x_rel, grad_rel, kind):
    slots, cols = len(ctx), w_out.shape[1]
    rows, width = x.shape[1:]
    own, mine, theirs = w_qkv
    piece, half = mine.shape[-2:]
    split = lambda v: v.reshape(4, -1, piece, half)
    later = lambda *shape: pl.BlockSpec((1, *shape), lambda i, at: (i + first,) + (0,) * len(shape))
    specs, shapes = part_specs(slots, width // 8, 4 * cols)
    return call(
        functools.partial(attend_back_kernel, first, slots, heads, (cols // heads) ** -0.5), "attend_back", at, (slots,),
        [here(rows, width), const(rows, width), const(rows, width)]
        + [const(*ctx[0].shape)] * slots
        + [
            FAR, FAR, FAR, later(2, cols), later(cols, width), const(*segments.shape), const(width, rows), const(width, rows),
        ],
        [slot(2, cols), const(rows, width), *specs],
        [
            jax.ShapeDtypeStruct((slots, 2, cols), F32),
            jax.ShapeDtypeStruct((rows, width), kind),
            *shapes,
        ],
        [
            pltpu.VMEM((rows, width), F32), pltpu.VMEM((cols, rows), F32), pltpu.VMEM((rows, cols), F32),
            pltpu.VMEM((rows, cols), F32), pltpu.VMEM((rows, cols), BF), pltpu.VMEM((rows, 3 * cols), BF),
            pltpu.VMEM((slots, 4, piece, width), BF), pltpu.SemaphoreType.DMA((slots, 2)),
        ],
    )(at, x, low, grad, *ctx, own.reshape(4, piece, width), split(mine), split(theirs), bias, w_out, segments, x_rel, grad_rel)


def place_kernel(slots, at_ref, *refs):
    sources, (out_ref, held, sems) = refs[:-3], refs[-3:]
    here = at_ref[3]

    def each(step, act):
        for s in range(slots):
            for source, wanted in ((s, here - step == s),) + (((slots - 1 + s, step - here == s),) if s else ()):
                @pl.when(wanted)
                def _():
                    act(pltpu.make_async_copy(sources[source], held.at[step], sems.at[step]))

    step = pl.program_id(0)

    @pl.when(step == 0)
    def _():
        for j in range(slots):
            each(j, lambda copy: copy.start())

    pltpu.make_async_copy(sources[0], held.at[step], sems.at[step]).wait()
    out_ref[0] = held[step].astype(out_ref.dtype)


def place_end_kernel(slots, at_ref, own_ref, behind_ref, ahead_ref, whole_ref, out_ref, held, sem):
    here = at_ref[3]
    for source, wanted in ((ahead_ref, here == 0), (behind_ref, here == slots - 1), (own_ref, lax.rem(here, slots - 1) > 0)):
        @pl.when(wanted)
        def _():
            copy = pltpu.make_async_copy(source, held, sem)
            copy.start()
            copy.wait()

    out_ref[0] = held[...].astype(out_ref.dtype)


def place_end(at, own, behind, ahead, whole):
    slots = whole.shape[0]
    spot = lambda i, at: (jnp.where(at[3] == 0, slots - 1, jnp.where(at[3] == slots - 1, 0, at[3])), 0, 0)
    return pl.pallas_call(
        functools.partial(place_end_kernel, slots),
        grid_spec=pltpu.PrefetchScalarGridSpec(
            num_scalar_prefetch=1, grid=(1,), in_specs=[FAR] * 4, out_specs=pl.BlockSpec((1, *own.shape), spot),
            scratch_shapes=[pltpu.VMEM(own.shape, own.dtype), pltpu.SemaphoreType.DMA],
        ),
        out_shape=jax.ShapeDtypeStruct(whole.shape, whole.dtype),
        input_output_aliases={4: 0},
        cost_estimate=SHORT,
        name="place_end",
    )(at, own, behind, ahead, whole)


def place(at, own, behind, ahead, kind):
    slots = len(behind) + 1
    values = [own, *behind, *ahead]
    return call(
        functools.partial(place_kernel, slots), "place", at, (slots,),
        [FAR] * len(values), slot(*own.shape),
        jax.ShapeDtypeStruct((slots, *own.shape), kind),
        [pltpu.VMEM((slots, *own.shape), own.dtype), pltpu.SemaphoreType.DMA((slots,))],
    )(at, *values)


def swap(value, axis, size, bit):
    return lax.ppermute(value, axis, [(i, i ^ bit) for i in range(size)])


def ordered(own, got, bit, axis):
    first = jnp.where(bit == 0, own, got)
    second = jnp.where(bit == 0, got, own)
    return jnp.stack([first, second], axis)


def in_three(value):
    high = value.astype(BF)
    rest = value - high.astype(F32)
    middle = rest.astype(BF)
    return jnp.stack([high, middle, (rest - middle.astype(F32)).astype(BF)])


class Order:
    def __init__(self):
        self.last = ()

    def hold(self, values, *waits):
        leaves, tree = jax.tree.flatten(values)
        held = lax.optimization_barrier((leaves, self.last, waits))[0]
        return jax.tree.unflatten(tree, held)

    def done(self, *values):
        self.last = tuple(values)

    def run(self, made, *waits):
        self.last = waits
        made = self.hold(made)
        self.last = tuple(jax.tree.leaves(made)[:1])
        return made


def make(sizes):
    n_outer, n_local, n_tensor = sizes["outer"], sizes["local"], sizes["tensor"]

    def local(tokens, segments, w_qkv, b_qv, w_out, w_in, b_inner, w_down, gains, shifts, cotangent):
        seq_count, seq_len, width = tokens.shape
        heads, head_size = b_qv.shape[1], b_qv.shape[2]
        head_cols = heads * head_size
        hidden_cols = w_in.shape[1]
        z = lax.axis_index("tensor")
        l_index = lax.axis_index("local")
        core, x = l_index & 1, l_index >> 1
        y = lax.axis_index("outer") & 1
        z_from = lambda s: jnp.mod(z - s, n_tensor)
        z_to = lambda s: jnp.mod(z + s, n_tensor)
        cyclic = lambda v, s: lax.ppermute(v, "tensor", [(i, (i + s) % n_tensor) for i in range(n_tensor)])
        pick = lambda v, i: lax.dynamic_index_in_dim(v, i, 0, keepdims=False)
        others = range(1, n_tensor)
        by_x = lambda v: swap(v, "local", n_local, 2)
        by_y = lambda v: swap(v, "outer", n_outer, 1)
        by_core = lambda v: swap(v, "local", n_local, 1)
        at = jnp.stack([core, x, y, z]).astype(jnp.int32)
        order = Order()
        hold, done, run = order.hold, order.done, order.run

        place8 = core * 4 + y * 2 + x
        half = width // 2

        def piece_of(weight):
            n = weight.shape[0] // 8
            return lax.dynamic_slice_in_dim(weight, place8 * n, n, 0)

        def halves(parts, rows):
            return jnp.stack([p[rows, :half] for p in parts]), jnp.stack([p[rows, half:] for p in parts])

        def plane_two(a, b, a1, b1):
            return ordered(a, a1, x, 0), ordered(b, b1, y, 0)

        def plane_three(a, b, a1, b1, rows):
            a, a1, b, b1 = (v[:, :, rows] for v in (a, a1, b, b1))
            return jnp.concatenate([ordered(a, a1, y, 0), ordered(b, b1, x, 1)], -1)

        qkv_rows = w_qkv.transpose(0, 2, 1)
        flat_qkv = qkv_rows.reshape(3 * head_cols, width)

        first = jnp.concatenate([piece_of(w_out), piece_of(w_in), piece_of(w_down)])
        first_z = [cyclic(first, s) for s in others]
        done(first)
        piece_qkv = lax.dynamic_slice(
            hold(flat_qkv), ((y * 2 + x) * (flat_qkv.shape[0] // 4), core * half), (flat_qkv.shape[0] // 4, half)
        )
        biases = jnp.concatenate([b_inner.reshape(-1), b_qv.reshape(-1)])
        bias_rows = -(-biases.size // half)
        bias_pack = in_three(jnp.pad(hold(biases), (0, bias_rows * half - biases.size)).reshape(bias_rows, half))
        bias_pack = jnp.pad(bias_pack.reshape(3 * bias_rows, half), ((0, -3 * bias_rows % 16), (0, 0)))
        extra = jnp.concatenate([bias_pack, piece_qkv])

        context = attend(at, hold(tokens), qkv_rows, b_qv.reshape(2, head_cols), segments, heads, extra)
        (ctx_own, *ctx_send), first_z = run((context, first_z))
        ctx_z = [cyclic(v, s) for v, s in zip(ctx_send, others)]
        cut, end = w_out.shape[0] // 8, (w_out.shape[0] + w_in.shape[0]) // 8
        a, b = halves(first_z, slice(0, end))
        a1, b1 = by_x(a), by_y(b)
        c, d = halves(first_z, slice(end, None))
        done(c, d, a1, b1)
        a, b = plane_two(*hold((a, b, a1, b1)))
        a1, b1 = by_y(a), by_x(b)
        done(a, b, *ctx_z)
        ctx_z = hold(ctx_z)
        c1, d1 = by_x(hold(c)), by_y(hold(d))
        top = seq_len // 2
        bias_got = jnp.stack([p[top : top + 3 * bias_rows] for p in ctx_z]).astype(F32)
        bias_got = bias_got.reshape(n_tensor - 1, 3, bias_rows * half)
        bias_got = bias_got[:, 0] + bias_got[:, 1] + bias_got[:, 2]
        bias_all = jnp.concatenate([biases[None], bias_got[:, : biases.size]])
        b_inner_all = bias_all[:, :hidden_cols]
        b_qv_all = bias_all[:, hidden_cols:].reshape(n_tensor, 2, head_cols)
        done(b_inner_all, a1, b1)
        a, b, a1, b1 = hold((a, b, a1, b1))
        in_both = plane_three(a, b, a1, b1, slice(cut, None))
        in_core = by_core(in_both)
        out_both = plane_three(a, b, a1, b1, slice(0, cut))
        out_core = by_core(out_both)
        done(in_both, out_both, c1, d1)
        c, d = plane_two(*hold((c, d, c1, d1)))
        c1, d1 = by_y(c), by_x(d)
        done(c, d, out_core, in_core)
        out_got = ordered(*hold((out_both, out_core)), core, 0).transpose(3, 0, 1, 2, 4, 5)
        out_all = jnp.concatenate([w_out[None], out_got.reshape(n_tensor - 1, *w_out.shape)])
        in_parts = (w_in, in_both, in_core)
        e = jnp.stack([p[-piece_qkv.shape[0] :] for p in ctx_z])
        e1 = by_x(e)
        done(out_all, in_core, e)
        ctx = [ctx_own, *ctx_z]
        made = rise(at, hold(ctx), out_all, tokens, gains, shifts, in_parts, b_inner_all)
        made, c1, d1, e1 = run((made, c1, d1, e1))
        hidden1, hidden_low, norm_one, recip_one, activation, slope, tokens_rel, hidden_rel = made
        down_both = plane_three(c, d, c1, d1, slice(None))
        down_core = by_core(down_both)
        e = ordered(e, e1, x, 0)
        e1 = by_y(e)
        done(down_both, down_core, e)
        down_parts = (w_down, down_both, down_core)
        made = fall(at, hold(activation), down_parts, hidden1, cotangent, gains, shifts)
        made, e1 = run((made, e1))
        output_own, grad_r2, grad_r2_low, vec_two, keep1, send1 = made

        steps = [(i, i + 1) for i in range(n_tensor - 1)]
        back_steps = [(i + 1, i) for i in range(n_tensor - 1)]

        def hop(right, left, step):
            return (
                lax.ppermute(right, "tensor", steps[step:]),
                lax.ppermute(left, "tensor", back_steps[: len(steps) - step]),
            )

        block = width // 8

        class Part:
            def __init__(self, slots, *arrays):
                self.parts = [v[:, slots].reshape(2, 2, -1, *v.shape[2:]) for v in arrays]

            def total(self, *index):
                terms = [p[index].astype(F32) for p in self.parts]
                return functools.reduce(lambda u, v: u + v, terms).astype(BF)

            def take(self, got):
                self.parts = [p[0] for p in self.parts]
                self.parts.append(got.reshape(self.parts[0].shape))

            def totals(self):
                return [self.total(i) for i in range(self.parts[0].shape[0])]

        def pair_of(keep, got):
            count = keep.shape[1]
            return Part(slice(0, count // 2), keep, got), Part(slice(count // 2, count), keep, got)

        def plane(by_first, by_second):
            flying = []
            for move, group in ((by_x, by_first), (by_y, by_second)):
                sends = [p.total(1) for p in group]
                flat = jnp.concatenate([v.reshape(-1, *v.shape[-2:]) for v in sends])
                done(*order.last, flat)
                flying.append(move(flat))
            return flying

        def landed(flying, *groups):
            for flat, group in zip(flying, groups):
                first = 0
                for p in group:
                    size = math.prod(p.parts[0].shape[:-2]) // 2
                    p.take(flat[first : first + size])
                    first += size

        z_near = lambda v: swap(v, "tensor", n_tensor, 1)
        z_far = lambda v: swap(v, "tensor", n_tensor, 2)
        odd = (z & 1) == 1

        def after_near(values, got):
            first, second = jnp.where(odd, got[1], got[0]), jnp.where(odd, got[0], got[1])
            return values[0].astype(F32) + first.astype(F32), values[1].astype(F32) + second.astype(F32)

        def outer_rest(mine):
            bit = 2
            while bit < n_outer:
                mine = mine + swap(mine.astype(BF), "outer", n_outer, bit).astype(F32)
                bit *= 2
            return mine

        def whole_rows(mine, got):
            return ordered(mine, got.astype(F32), y, 0).reshape(2 * block, mine.shape[-1])

        out_1 = hop(output_own, output_own, 0)
        core1 = by_core(send1)
        qkv_both = ordered(e, e1, y, 0)
        qkv_core = by_core(qkv_both)
        qkv_parts = (flat_qkv, qkv_both, qkv_core)
        done(qkv_both, core1)
        h1 = pair_of(*hold((keep1, core1)))
        flight = plane([h1[0]], [h1[1]])
        made = back(
            at, hold(grad_r2), grad_r2_low, down_parts, slope, in_parts, norm_one, recip_one, gains, hidden_rel
        )
        made, qkv_core, out_1, flight = run((made, qkv_core, out_1, flight))
        qkv_parts = (flat_qkv, qkv_both, qkv_core)
        grad_binner, grad_r1, grad_r1_low, grad_r1_rel, vec_one, keep2, send2 = made
        out_2 = hop(*out_1, 1)
        core2 = by_core(send2)
        landed(flight, [h1[0]], [h1[1]])
        done(core2)
        h2 = pair_of(*hold((keep2, core2)))
        groups = [h2[0], h1[1]], [h2[1], h1[0]]
        flight = plane(*groups)
        two = n_tensor // 2
        made = attend_back(
            at, 0, tokens, hold(grad_r1_low), grad_r1, ctx[:two], qkv_parts, b_qv_all, heads, out_all, segments,
            tokens_rel, grad_r1_rel, F32,
        )
        made, out_2, flight = run((made, out_2, flight))
        bqv_a, tok_a, keep_a, send_a = made
        out_3 = hop(*out_2, 2)
        core_a = by_core(send_a)
        landed(flight, *groups)
        total1 = h1[0].totals() + h1[1].totals()
        near1 = z_near(jnp.stack([total1[1], total1[3]]))
        done(core_a)
        ha = pair_of(*hold((keep_a, core_a)))
        groups = [ha[0], h2[1]], [ha[1], h2[0]]
        flight = plane(*groups)
        made = attend_back(
            at, two, tokens, hold(grad_r1_low), tok_a, ctx[two:], qkv_parts, b_qv_all, heads, out_all, segments,
            tokens_rel, grad_r1_rel, BF,
        )
        made, out_3, flight, near1 = run((made, out_3, flight, near1))
        bqv_b, tok_own, keep_b, send_b = made
        tok_1 = hop(tok_own, tok_own, 0)
        core_b = by_core(send_b)
        landed(flight, *groups)

        grad_bqv = jnp.concatenate([bqv_a, bqv_b])
        slot_vec = [
            jnp.concatenate([grad_binner[s].reshape(-1, half), grad_bqv[s].reshape(-1, half)]) for s in range(n_tensor)
        ]
        common = jnp.concatenate([vec_one, vec_two]).reshape(-1, half)
        n_slot = slot_vec[0].shape[0]
        vec_got = z_near(jnp.concatenate([slot_vec[1], slot_vec[3], common]))
        done(core_b)
        hb = pair_of(*hold((keep_b, core_b)))
        groups = [hb[0], ha[1]], [hb[1], ha[0]]
        flight = plane(*groups)
        total2 = h2[0].totals() + h2[1].totals()
        near2 = jnp.stack([total2[1], total2[3]])
        mine1, far1 = after_near((total1[0], total1[2]), near1)
        outs = hold((output_own, out_1, out_2, out_3))
        output = place(at, outs[0], [v[0] for v in outs[1:]], [v[1] for v in outs[1:]], BF)
        output = output.reshape(seq_count, seq_len, width)
        output, tok_1, flight, vec_got = run((output, tok_1, flight, vec_got))
        tok_2 = hop(*tok_1, 1)
        landed(flight, *groups)
        groups = [hb[1]], [hb[0]]
        flight = plane(*groups)
        near2 = z_near(hold(near2))
        vec_got = vec_got[: 2 * n_slot].reshape(2, n_slot, half), vec_got[2 * n_slot :]
        vec_0, vec_2 = after_near((slot_vec[0], slot_vec[2]), vec_got[0])
        common = common + vec_got[1]
        vec_send = jnp.concatenate([vec_2, common])
        done(vec_send, *flight)
        landed(hold(flight), *groups)
        total3 = [t for part in (*ha, *hb) for t in part.totals()]
        near3 = z_near(jnp.stack([total3[1], total3[3]]))
        vec_got = z_far(hold(vec_send))
        done(*total3, near2)
        mine2, far2 = after_near((total2[0], total2[2]), hold(near2))
        far12 = z_far(jnp.stack([far1, far2]).astype(BF))
        done(far2, *tok_2, vec_got, near3)
        tok_3 = hop(*hold(tok_2), 2)
        mine3, far3 = after_near((total3[0], total3[2]), hold(near3))
        far3 = z_far(far3.astype(BF))
        vectors = jnp.concatenate([vec_0, common]) + hold(vec_got)
        vec_got = by_core(vectors)
        done(far3, far12, vec_got)
        mine12 = outer_rest(jnp.stack([mine1, mine2]) + hold(far12).astype(F32))
        got12 = by_y(mine12.astype(BF))
        vectors = vectors + hold(vec_got)
        vec_got = by_x(vectors)
        mine3 = outer_rest(mine3 + hold(far3).astype(F32))
        got3 = by_y(mine3.astype(BF))
        tok_held = hold((tok_own, (tok_1[0], tok_2[0], tok_2[0]), (tok_1[1], tok_2[1], tok_2[1])))
        grad_tokens = place(at, *tok_held, F32)
        done(grad_tokens, got12, got3, vec_got)
        got12, got3, vec_got = hold((got12, got3, vec_got))
        vectors = vectors + vec_got
        vec_got = by_y(vectors)
        done_wdown = whole_rows(mine12[0], got12[0])
        done_win = whole_rows(mine12[1], got12[1])
        done(done_wdown, done_win, vec_got)
        got3 = hold(got3)
        done_last = whole_rows(mine3, got3)
        vectors = vectors + hold(vec_got)
        bit = 2
        while bit < n_outer:
            vectors = vectors + swap(vectors, "outer", n_outer, bit)
            bit *= 2
        slot_sum = vectors[:n_slot].reshape(-1)
        common = vectors[n_slot:].reshape(6, width)
        common = jnp.stack([common[i] for i in (0, 3, 1, 2, 4, 5)])
        part = lambda v, n: lax.dynamic_slice_in_dim(v, l_index * (n // n_local), n // n_local, v.ndim - 1)
        binner = part(slot_sum[:hidden_cols].reshape(b_inner.shape), head_size)
        bqv = part(slot_sum[hidden_cols:].reshape(b_qv.shape), head_size)
        common = part(common, width)
        grad_wqkv = done_last[:, : 3 * head_cols].reshape(width // n_local, 3, head_cols).transpose(1, 0, 2)
        done(grad_wqkv, common, binner, bqv, *tok_3)
        grad_tokens = place_end(at, *hold((tok_own, tok_3[0], tok_3[1], grad_tokens)))
        grad_tokens = grad_tokens.reshape(seq_count, seq_len, width)
        return (
            output,
            grad_tokens,
            grad_wqkv,
            bqv,
            done_last[:, 3 * head_cols :].T,
            done_win,
            binner,
            done_wdown.T,
            common[:2],
            common[2:],
        )

    return local


def solution(mesh):
    placed = (
        P(("outer", "local"), None, None),
        P(("outer", "local"), None),
        P(None, None, "tensor"),
        P(None, "tensor", None),
        P("tensor", None),
        P(None, "tensor"),
        P("tensor", None),
        P("tensor", None),
        P(),
        P(),
        P(("outer", "local"), None, None),
    )
    return jax.shard_map(
        make(dict(mesh.shape)),
        mesh=mesh,
        in_specs=placed,
        out_specs=(
            P(("outer", "local"), None, None),
            P(("outer", "local"), None, None),
            P(None, "local", "tensor"),
            P(None, "tensor", "local"),
            P("tensor", "local"),
            P("local", "tensor"),
            P("tensor", "local"),
            P("tensor", "local"),
            P(None, "local"),
            P(None, "local"),
        ),
        check_vma=False,
    )
```

```python
import functools
import math

import jax
import jax.numpy as jnp
from jax import lax
from jax.experimental import pallas as pl
from jax.experimental.pallas import tpu as pltpu
from jax.sharding import PartitionSpec as P

EPSILON = 1e-12
MASKED = -1e30
BF = jnp.bfloat16
F32 = jnp.float32
SHORT = pl.CostEstimate(flops=1000, bytes_accessed=1000, transcendentals=0)
ROOM = {'attend': 36, 'rise': 36, 'fall': 36, 'back': 36, 'attend_back': 48}
ROWS_BY_ROWS = (((1,), (1,)), ((), ()))


def dot(left, right):
    return jnp.dot(left, right, preferred_element_type=F32)


def dot_t(left, right):
    return lax.dot_general(left, right, ROWS_BY_ROWS, preferred_element_type=F32)


def normalize(values):
    centre = values - jnp.mean(values, axis=-1, keepdims=True)
    variance = jnp.mean(centre * centre, axis=-1, keepdims=True)
    recip = lax.rsqrt(variance + EPSILON)
    return (centre * recip, recip)


def norm_back(grad_norm, normed, recip):
    first = jnp.mean(grad_norm, axis=-1, keepdims=True)
    second = jnp.mean(grad_norm * normed, axis=-1, keepdims=True)
    return recip * (grad_norm - first - normed * second)


def col_sum(value):
    return jnp.sum(value, axis=0, keepdims=True)


def softmax_columns(raw, allowed):
    scores = jnp.where(allowed, raw, MASKED)
    grown = jnp.exp(scores - jnp.max(scores, axis=0, keepdims=True))
    return grown, 1.0 / jnp.sum(grown, axis=0, keepdims=True)


def column(row):
    return jnp.broadcast_to(row, (8, row.shape[1])).T[:, :1]


def store_relative(out_ref, value, at_ref):
    flipped = value.T.astype(BF)
    block = flipped.shape[0] // 8
    for i in range(8):
        spot = (((i >> 1) & 1) ^ at_ref[0]) * 4 + ((i >> 2) ^ at_ref[1]) * 2 + ((i & 1) ^ at_ref[2])
        out_ref[pl.ds(pl.multiple_of(spot * block, block), block)] = flipped[i * block : (i + 1) * block]


def call(kernel, name, at, grid, in_specs, out_specs, out_shape, scratch=()):
    return pl.pallas_call(
        kernel,
        grid_spec=pltpu.PrefetchScalarGridSpec(
            num_scalar_prefetch=1, grid=grid, in_specs=in_specs, out_specs=out_specs, scratch_shapes=list(scratch)
        ),
        out_shape=out_shape,
        cost_estimate=SHORT,
        compiler_params=pltpu.CompilerParams(vmem_limit_bytes=ROOM.get(name, 60) * 2**20),
        name=name,
    )


def const(*shape):
    return pl.BlockSpec(shape, lambda i, at: (0,) * len(shape))


def slot(*shape):
    return pl.BlockSpec((1, *shape), lambda i, at: (i,) + (0,) * len(shape))


def attend_kernel(heads, scale, at_ref, x_ref, w_ref, bias_ref, seg_ref, extra_ref, *out_refs):
    x = x_ref[0]
    size = w_ref.shape[1] // heads
    q_t = ((dot_t(w_ref[0], x) + column(bias_ref[0:1])).astype(BF) * scale).astype(BF)
    k = dot_t(x, w_ref[1]).astype(BF)
    v_t = (dot_t(w_ref[2], x) + column(bias_ref[1:2])).astype(BF)
    row = seg_ref[pl.ds(pl.program_id(0), 1)].astype(F32)
    allowed = column(row) == row
    parts = []
    for h in range(heads):
        at = slice(h * size, (h + 1) * size)
        grown, inv = softmax_columns(dot(k[:, at], q_t[at]), allowed)
        parts.append(dot(v_t[at], grown.astype(BF)) * inv)
    context = jnp.concatenate(parts, 0).T.astype(BF)
    count, rows, cols = len(out_refs), context.shape[0] // 2, context.shape[1]
    ahead = lax.rem(pl.program_id(0) + count - at_ref[3], count)
    for s, out_ref in enumerate(out_refs):
        @pl.when(ahead == s)
        def _():
            out_ref[:rows, :cols] = context[:rows]
            out_ref[:rows, cols:] = context[rows:]
            out_ref[rows:] = extra_ref[...]


def attend(at, tokens, w_rows, bias, segments, heads, extra):
    seqs, length, width = tokens.shape
    cols = w_rows.shape[1]
    return call(
        functools.partial(attend_kernel, heads, (cols // heads) ** -0.5), "attend", at, (seqs,),
        [slot(length, width), const(3, cols, width), const(2, cols), const(seqs, length), const(*extra.shape)],
        [const(length // 2 + extra.shape[0], 2 * cols)] * seqs,
        [jax.ShapeDtypeStruct((length // 2 + extra.shape[0], 2 * cols), BF)] * seqs,
    )(at, tokens, w_rows, bias, segments, extra)


def fetch_copies(core, own_ref, mine_ref, theirs_ref, held, sems):
    slots = held.shape[0]
    copies = [[pltpu.make_async_copy(own_ref.at[c], held.at[0, c], sems.at[0, c]) for c in range(2)]]
    for s in range(1, slots):
        copies.append([
            pltpu.make_async_copy(mine_ref.at[:, s - 1], held.at[s, core], sems.at[s, 0]),
            pltpu.make_async_copy(theirs_ref.at[:, s - 1], held.at[s, 1 - core], sems.at[s, 1]),
        ])
    return copies


def fetch_slot(at_ref, refs, held, sems):
    step = pl.program_id(0)
    copies = fetch_copies(at_ref[0], *refs, held, sems)

    @pl.when(step == 0)
    def _():
        for pair in copies:
            for copy in pair:
                copy.start()

    for s, pair in enumerate(copies):
        @pl.when(step == s)
        def _():
            for copy in pair:
                copy.wait()

    return held[step].reshape(8 * held.shape[3], held.shape[4])


def pieces(weight):
    own, mine, theirs = weight
    piece = own.shape[0] // 8
    split = lambda v: v.reshape(4, -1, piece, own.shape[1])
    return own.reshape(2, 4, piece, own.shape[1]), split(mine), split(theirs)


def held_scratch(slots, weight):
    rows, width = weight[0].shape
    return [pltpu.VMEM((slots, 2, 4, rows // 8, width), BF), pltpu.SemaphoreType.DMA((slots, 2))]


def here(*shape):
    return pl.BlockSpec((1, *shape), lambda i, at: (at[3],) + (0,) * len(shape))


FAR = pl.BlockSpec(memory_space=pl.ANY)


def rise_kernel(slots, at_ref, *refs):
    ctx_refs = refs[:slots]
    (w_out_ref, x_ref, gains_ref, shifts_ref, own_ref, mine_ref, theirs_ref, bias_ref,
     hidden_ref, low_ref, norm_ref, recip_ref, act_ref, slope_ref, x_rel_ref, hidden_rel_ref, held, sems) = refs[slots:]
    step = pl.program_id(0)
    weight = fetch_slot(at_ref, (own_ref, mine_ref, theirs_ref), held, sems)

    @pl.when(step == 0)
    def _():
        rows, cols = low_ref.shape[0] // 2, w_out_ref.shape[1]
        sides = []
        for side in (slice(0, cols), slice(cols, None)):
            share = dot(ctx_refs[0][:rows, side], w_out_ref[0])
            for s in range(1, slots):
                share += dot(ctx_refs[s][:rows, side], w_out_ref[s])
            sides.append(share)
        attention = jnp.concatenate(sides)
        own = x_ref[0].astype(F32)
        norm, recip = normalize(own + attention + shifts_ref[0:1])
        hidden = norm * gains_ref[0:1] + shifts_ref[1:2]
        norm_ref[...] = norm
        recip_ref[...] = recip
        hidden_ref[...] = hidden
        low_ref[...] = hidden.astype(BF)
        store_relative(x_rel_ref, own, at_ref)
        store_relative(hidden_rel_ref, hidden, at_ref)

    pre = dot(low_ref[...], weight) + bias_ref[0]
    cumul = 0.5 * (1.0 + lax.erf(pre * (1.0 / math.sqrt(2.0))))
    act_ref[0] = (pre * cumul).astype(BF)
    slope_ref[0] = (cumul + pre * jnp.exp(-0.5 * pre * pre) * (1.0 / math.sqrt(2.0 * math.pi))).astype(BF)


def rise(at, ctx, w_out, x, gains, shifts, w_in, bias):
    slots, cols, rows = len(ctx), w_out.shape[1], x.shape[1]
    width, hidden = w_in[0].shape
    return call(
        functools.partial(rise_kernel, slots), "rise", at, (slots,),
        [const(*ctx[0].shape)] * slots
        + [
            const(slots, cols, width), here(rows, width), const(*gains.shape),
            const(*shifts.shape), FAR, FAR, FAR, slot(1, hidden),
        ],
        [
            const(rows, width), const(rows, width), const(rows, width), const(rows, 1),
            slot(rows, hidden), slot(rows, hidden), const(width, rows), const(width, rows),
        ],
        [
            jax.ShapeDtypeStruct((rows, width), F32),
            jax.ShapeDtypeStruct((rows, width), BF),
            jax.ShapeDtypeStruct((rows, width), F32),
            jax.ShapeDtypeStruct((rows, 1), F32),
            jax.ShapeDtypeStruct((slots, rows, hidden), BF),
            jax.ShapeDtypeStruct((slots, rows, hidden), BF),
            jax.ShapeDtypeStruct((width, rows), BF),
            jax.ShapeDtypeStruct((width, rows), BF),
        ],
        held_scratch(slots, w_in),
    )(at, *ctx, w_out, x, gains, shifts, *pieces(w_in), bias[:, None, :])


def store_parts(keep_ref, send_ref, x_first, first, whole):
    block, last = keep_ref.shape[2], first + whole.shape[1]
    low = whole.astype(BF)
    for i in range(4):
        spot = jnp.where(x_first, i, 3 - i) if i in (1, 2) else i
        keep_ref[spot, 0, :, first:last] = low[i * block : (i + 1) * block]
        send_ref[spot, 0, :, first:last] = low[(4 + i) * block : (5 + i) * block]


def fall_kernel(slots, at_ref, act_ref, own_ref, mine_ref, theirs_ref, hidden_ref, cot_ref, gains_ref, shifts_ref,
                out_ref, grad_ref, low_ref, vec_ref, keep_ref, send_ref, sum_ref, rel_ref, held, sems):
    s = pl.program_id(0)
    copies = fetch_copies(at_ref[0], own_ref, mine_ref, theirs_ref, held, sems)

    @pl.when(s == 0)
    def _():
        for pair in copies:
            for copy in pair:
                copy.start()

    for i, pair in enumerate(copies):
        @pl.when(s == i)
        def _():
            for copy in pair:
                copy.wait()

    @pl.when(s == 0)
    def _():
        sum_ref[...] = jnp.zeros_like(sum_ref)

    @pl.when(s < slots)
    def _():
        sum_ref[...] += dot(act_ref[0], held[s].reshape(8 * held.shape[3], held.shape[4]))

    @pl.when(s == slots - 1)
    def _():
        norm, recip = normalize(hidden_ref[...] + sum_ref[...] + shifts_ref[2:3])
        out_ref[...] = (norm * gains_ref[1:2] + shifts_ref[3:4]).astype(BF)
        cot = cot_ref[0].astype(F32)
        grad = norm_back(cot * gains_ref[1:2], norm, recip)
        grad_ref[...] = grad
        low_ref[...] = grad.astype(BF)
        store_relative(rel_ref, grad, at_ref)
        vec_ref[0:1] = col_sum(cot * norm)
        vec_ref[1:2] = col_sum(grad)
        vec_ref[2:3] = col_sum(cot)

    @pl.when(s >= slots)
    def _():
        store_parts(keep_ref, send_ref, s - slots < slots // 2, 0, dot(rel_ref[...], act_ref[0]))


def part_specs(slots, block, cols, start=0):
    spec = pl.BlockSpec((4, 1, block, cols), lambda i, at: (0, lax.max(i - start, 0), 0, 0))
    return [spec] * 2, [jax.ShapeDtypeStruct((4, slots, block, cols), BF)] * 2


def fall(at, act, w_down, hidden, cot, gains, shifts):
    slots, rows, inner = act.shape
    width = w_down[0].shape[1]
    specs, shapes = part_specs(slots, width // 8, inner, slots)
    return call(
        functools.partial(fall_kernel, slots), "fall", at, (2 * slots,),
        [
            pl.BlockSpec((1, rows, inner), lambda i, at: (lax.rem(i, slots), 0, 0)), FAR, FAR, FAR, const(rows, width),
            here(rows, width), const(*gains.shape), const(*shifts.shape),
        ],
        [const(rows, width), const(rows, width), const(rows, width), const(3, width), *specs],
        [
            jax.ShapeDtypeStruct((rows, width), BF),
            jax.ShapeDtypeStruct((rows, width), F32),
            jax.ShapeDtypeStruct((rows, width), BF),
            jax.ShapeDtypeStruct((3, width), F32),
            *shapes,
        ],
        [pltpu.VMEM((rows, width), F32), pltpu.VMEM((width, rows), BF)] + held_scratch(slots, w_down),
    )(at, act, *pieces(w_down), hidden, cot, gains, shifts)


def back_kernel(slots, at_ref, grad2_ref, low2_ref, own2_ref, mine2_ref, theirs2_ref, slope_ref, own1_ref, mine1_ref,
                theirs1_ref, norm_ref, recip_ref, gains_ref, hidden_rel_ref, bias_ref, grad_ref, low_ref, rel_ref, vec_ref,
                keep_ref, send_ref, sum_ref, held2, sems2, held1, sems1):
    s = pl.program_id(0)
    w_down = fetch_slot(at_ref, (own2_ref, mine2_ref, theirs2_ref), held2, sems2)
    w_in = fetch_slot(at_ref, (own1_ref, mine1_ref, theirs1_ref), held1, sems1)
    pre = dot_t(low2_ref[...], w_down) * slope_ref[0].astype(F32)
    bias_ref[0] = col_sum(pre)
    pre_low = pre.astype(BF)
    store_parts(keep_ref, send_ref, s < slots // 2, 0, dot(hidden_rel_ref[...], pre_low))
    share = dot_t(pre_low, w_in)

    @pl.when(s == 0)
    def _():
        sum_ref[...] = share

    @pl.when(s > 0)
    def _():
        sum_ref[...] += share

    @pl.when(s == slots - 1)
    def _():
        norm = norm_ref[...]
        grad_h = grad2_ref[...] + sum_ref[...]
        grad = norm_back(grad_h * gains_ref[0:1], norm, recip_ref[...])
        grad_ref[...] = grad
        low_ref[...] = grad.astype(BF)
        store_relative(rel_ref, grad, at_ref)
        vec_ref[0:1] = col_sum(grad_h * norm)
        vec_ref[1:2] = col_sum(grad)
        vec_ref[2:3] = col_sum(grad_h)


def back(at, grad2, low2, w_down, slope, w_in, norm, recip, gains, hidden_rel):
    slots, rows, inner = slope.shape
    width = grad2.shape[1]
    specs, shapes = part_specs(slots, width // 8, inner)
    return call(
        functools.partial(back_kernel, slots), "back", at, (slots,),
        [
            const(rows, width), const(rows, width), FAR, FAR, FAR, slot(rows, inner), FAR, FAR, FAR,
            const(rows, width), const(rows, 1), const(*gains.shape), const(width, rows),
        ],
        [slot(1, inner), const(rows, width), const(rows, width), const(width, rows), const(3, width), *specs],
        [
            jax.ShapeDtypeStruct((slots, 1, inner), F32),
            jax.ShapeDtypeStruct((rows, width), F32),
            jax.ShapeDtypeStruct((rows, width), BF),
            jax.ShapeDtypeStruct((width, rows), BF),
            jax.ShapeDtypeStruct((3, width), F32),
            *shapes,
        ],
        [pltpu.VMEM((rows, width), F32)] + held_scratch(slots, w_down) + held_scratch(slots, w_in),
    )(at, grad2, low2, *pieces(w_down), slope, *pieces(w_in), norm, recip, gains, hidden_rel)


def attend_back_kernel(first, slots, heads, scale, at_ref, x_ref, low_ref, grad_ref, *refs):
    ctx_refs = refs[:slots]
    (own_ref, mine_ref, theirs_ref, bias_ref, w_out_ref, seg_ref, x_rel_ref, grad_rel_ref,
     vec_ref, tok_ref, keep_ref, send_ref, sum_ref, q_ref, k_ref, v_ref, ctx_ref, proj_ref, held, sems) = refs[slots:]
    s = pl.program_id(0)
    half = mine_ref.shape[-1]
    mine_at = pl.ds(pl.multiple_of(at_ref[0] * half, half), half)
    theirs_at = pl.ds(pl.multiple_of((1 - at_ref[0]) * half, half), half)
    copies = []
    for i in range(slots):
        if first + i == 0:
            copies.append([
                pltpu.make_async_copy(own_ref.at[:2], held.at[i, :2], sems.at[i, 0]),
                pltpu.make_async_copy(own_ref.at[2:], held.at[i, 2:], sems.at[i, 1]),
            ])
        else:
            copies.append([
                pltpu.make_async_copy(mine_ref.at[:, first + i - 1], held.at[i, :, :, mine_at], sems.at[i, 0]),
                pltpu.make_async_copy(theirs_ref.at[:, first + i - 1], held.at[i, :, :, theirs_at], sems.at[i, 1]),
            ])

    @pl.when(s == 0)
    def _():
        for pair in copies:
            for copy in pair:
                copy.start()

    for i, pair in enumerate(copies):
        @pl.when(s == i)
        def _():
            for copy in pair:
                copy.wait()
            rows, cols = ctx_ref.shape[0] // 2, ctx_ref.shape[1]
            ctx_ref[:rows] = ctx_refs[i][:rows, :cols]
            ctx_ref[rows:] = ctx_refs[i][:rows, cols:]

    store_parts(keep_ref, send_ref, s < slots // 2, proj_ref.shape[1], dot(grad_rel_ref[...], ctx_ref[...]))
    x, low = x_ref[0], low_ref[...]
    cols = w_out_ref.shape[1]
    size = cols // heads
    weight = held[s].reshape(3, cols, x.shape[1])
    q_t = (dot_t(weight[0], x) + column(bias_ref[0, 0:1])).astype(BF)
    q_scaled = (q_t * scale).astype(BF)
    q = q_t.T
    k_t = dot_t(weight[1], x).astype(BF)
    k = k_t.T
    v = (dot_t(x, weight[2]) + bias_ref[0, 1:2]).astype(BF)
    gc_t = dot_t(w_out_ref[0], low).astype(BF)
    gc = gc_t.T
    row = seg_ref[pl.ds(at_ref[3], 1)].astype(F32)
    allowed = column(row) == row
    for h in range(heads):
        at = slice(h * size, (h + 1) * size)
        grown, inv = softmax_columns(dot(k[:, at], q_scaled[at]), allowed)
        probs = grown * inv
        grad_probs = dot(v[:, at], gc_t[at])
        inner = jnp.sum(probs * grad_probs, axis=0, keepdims=True)
        grad_scores = (probs * (grad_probs - inner) * scale).astype(BF)
        q_ref[at] = dot(k_t[at], grad_scores)
        k_ref[:, at] = dot(grad_scores, q[:, at])
        v_ref[:, at] = dot(probs.astype(BF), gc[:, at])
    grad_q = q_ref[...].T
    grad_v = v_ref[...]
    vec_ref[0, 0:1] = col_sum(grad_q)
    vec_ref[0, 1:2] = col_sum(grad_v)
    parts = [grad_q.astype(BF), k_ref[...].astype(BF), grad_v.astype(BF)]
    for c in range(3):
        proj_ref[:, c * cols : (c + 1) * cols] = parts[c]
    proj = proj_ref[...]
    share = dot(proj, weight.reshape(3 * cols, x.shape[1]))
    store_parts(keep_ref, send_ref, s < slots // 2, 0, dot(x_rel_ref[...], proj))

    @pl.when(s == 0)
    def _():
        sum_ref[...] = share + grad_ref[...]

    @pl.when(s > 0)
    def _():
        sum_ref[...] += share

    @pl.when(s == slots - 1)
    def _():
        tok_ref[...] = sum_ref[...].astype(tok_ref.dtype)


def attend_back(at, first, x, low, grad, ctx, w_qkv, bias, heads, w_out, segments, x_rel, grad_rel, kind):
    slots, cols = len(ctx), w_out.shape[1]
    rows, width = x.shape[1:]
    own, mine, theirs = w_qkv
    piece, half = mine.shape[-2:]
    split = lambda v: v.reshape(4, -1, piece, half)
    later = lambda *shape: pl.BlockSpec((1, *shape), lambda i, at: (i + first,) + (0,) * len(shape))
    specs, shapes = part_specs(slots, width // 8, 4 * cols)
    return call(
        functools.partial(attend_back_kernel, first, slots, heads, (cols // heads) ** -0.5), "attend_back", at, (slots,),
        [here(rows, width), const(rows, width), const(rows, width)]
        + [const(*ctx[0].shape)] * slots
        + [
            FAR, FAR, FAR, later(2, cols), later(cols, width), const(*segments.shape), const(width, rows), const(width, rows),
        ],
        [slot(2, cols), const(rows, width), *specs],
        [
            jax.ShapeDtypeStruct((slots, 2, cols), F32),
            jax.ShapeDtypeStruct((rows, width), kind),
            *shapes,
        ],
        [
            pltpu.VMEM((rows, width), F32), pltpu.VMEM((cols, rows), F32), pltpu.VMEM((rows, cols), F32),
            pltpu.VMEM((rows, cols), F32), pltpu.VMEM((rows, cols), BF), pltpu.VMEM((rows, 3 * cols), BF),
            pltpu.VMEM((slots, 4, piece, width), BF), pltpu.SemaphoreType.DMA((slots, 2)),
        ],
    )(at, x, low, grad, *ctx, own.reshape(4, piece, width), split(mine), split(theirs), bias, w_out, segments, x_rel, grad_rel)


def place_kernel(slots, at_ref, *refs):
    sources, (out_ref, held, sems) = refs[:-3], refs[-3:]
    here = at_ref[3]

    def each(step, act):
        for s in range(slots):
            for source, wanted in ((s, here - step == s),) + (((slots - 1 + s, step - here == s),) if s else ()):
                @pl.when(wanted)
                def _():
                    act(pltpu.make_async_copy(sources[source], held.at[step], sems.at[step]))

    step = pl.program_id(0)

    @pl.when(step == 0)
    def _():
        for j in range(slots):
            each(j, lambda copy: copy.start())

    pltpu.make_async_copy(sources[0], held.at[step], sems.at[step]).wait()
    out_ref[0] = held[step].astype(out_ref.dtype)


def place_end_kernel(slots, at_ref, own_ref, behind_ref, ahead_ref, whole_ref, out_ref, held, sem):
    here = at_ref[3]
    for source, wanted in ((ahead_ref, here == 0), (behind_ref, here == slots - 1), (own_ref, lax.rem(here, slots - 1) > 0)):
        @pl.when(wanted)
        def _():
            copy = pltpu.make_async_copy(source, held, sem)
            copy.start()
            copy.wait()

    out_ref[0] = held[...].astype(out_ref.dtype)


def place_end(at, own, behind, ahead, whole):
    slots = whole.shape[0]
    spot = lambda i, at: (jnp.where(at[3] == 0, slots - 1, jnp.where(at[3] == slots - 1, 0, at[3])), 0, 0)
    return pl.pallas_call(
        functools.partial(place_end_kernel, slots),
        grid_spec=pltpu.PrefetchScalarGridSpec(
            num_scalar_prefetch=1, grid=(1,), in_specs=[FAR] * 4, out_specs=pl.BlockSpec((1, *own.shape), spot),
            scratch_shapes=[pltpu.VMEM(own.shape, own.dtype), pltpu.SemaphoreType.DMA],
        ),
        out_shape=jax.ShapeDtypeStruct(whole.shape, whole.dtype),
        input_output_aliases={4: 0},
        cost_estimate=SHORT,
        name="place_end",
    )(at, own, behind, ahead, whole)


def place(at, own, behind, ahead, kind):
    slots = len(behind) + 1
    values = [own, *behind, *ahead]
    return call(
        functools.partial(place_kernel, slots), "place", at, (slots,),
        [FAR] * len(values), slot(*own.shape),
        jax.ShapeDtypeStruct((slots, *own.shape), kind),
        [pltpu.VMEM((slots, *own.shape), own.dtype), pltpu.SemaphoreType.DMA((slots,))],
    )(at, *values)


def swap(value, axis, size, bit):
    return lax.ppermute(value, axis, [(i, i ^ bit) for i in range(size)])


def ordered(own, got, bit, axis):
    first = jnp.where(bit == 0, own, got)
    second = jnp.where(bit == 0, got, own)
    return jnp.stack([first, second], axis)


def in_three(value):
    high = value.astype(BF)
    rest = value - high.astype(F32)
    middle = rest.astype(BF)
    return jnp.stack([high, middle, (rest - middle.astype(F32)).astype(BF)])


class Order:
    def __init__(self):
        self.last = ()

    def hold(self, values, *waits):
        leaves, tree = jax.tree.flatten(values)
        held = lax.optimization_barrier((leaves, self.last, waits))[0]
        return jax.tree.unflatten(tree, held)

    def done(self, *values):
        self.last = tuple(values)

    def run(self, made, *waits):
        self.last = waits
        made = self.hold(made)
        self.last = tuple(jax.tree.leaves(made)[:1])
        return made


def make(sizes):
    n_outer, n_local, n_tensor = sizes["outer"], sizes["local"], sizes["tensor"]

    def local(tokens, segments, w_qkv, b_qv, w_out, w_in, b_inner, w_down, gains, shifts, cotangent):
        seq_count, seq_len, width = tokens.shape
        heads, head_size = b_qv.shape[1], b_qv.shape[2]
        head_cols = heads * head_size
        hidden_cols = w_in.shape[1]
        z = lax.axis_index("tensor")
        l_index = lax.axis_index("local")
        core, x = l_index & 1, l_index >> 1
        y = lax.axis_index("outer") & 1
        z_from = lambda s: jnp.mod(z - s, n_tensor)
        z_to = lambda s: jnp.mod(z + s, n_tensor)
        cyclic = lambda v, s: lax.ppermute(v, "tensor", [(i, (i + s) % n_tensor) for i in range(n_tensor)])
        pick = lambda v, i: lax.dynamic_index_in_dim(v, i, 0, keepdims=False)
        others = range(1, n_tensor)
        by_x = lambda v: swap(v, "local", n_local, 2)
        by_y = lambda v: swap(v, "outer", n_outer, 1)
        by_core = lambda v: swap(v, "local", n_local, 1)
        at = jnp.stack([core, x, y, z]).astype(jnp.int32)
        order = Order()
        hold, done, run = order.hold, order.done, order.run

        place8 = core * 4 + y * 2 + x
        half = width // 2

        def piece_of(weight):
            n = weight.shape[0] // 8
            return lax.dynamic_slice_in_dim(weight, place8 * n, n, 0)

        def halves(parts, rows):
            return jnp.stack([p[rows, :half] for p in parts]), jnp.stack([p[rows, half:] for p in parts])

        def plane_two(a, b, a1, b1):
            return ordered(a, a1, x, 0), ordered(b, b1, y, 0)

        def plane_three(a, b, a1, b1, rows):
            a, a1, b, b1 = (v[:, :, rows] for v in (a, a1, b, b1))
            return jnp.concatenate([ordered(a, a1, y, 0), ordered(b, b1, x, 1)], -1)

        qkv_rows = w_qkv.transpose(0, 2, 1)
        flat_qkv = qkv_rows.reshape(3 * head_cols, width)

        first = jnp.concatenate([piece_of(w_out), piece_of(w_in), piece_of(w_down)])
        first_z = [cyclic(first, s) for s in others]
        done(first)
        piece_qkv = lax.dynamic_slice(
            hold(flat_qkv), ((y * 2 + x) * (flat_qkv.shape[0] // 4), core * half), (flat_qkv.shape[0] // 4, half)
        )
        biases = jnp.concatenate([b_inner.reshape(-1), b_qv.reshape(-1)])
        bias_rows = -(-biases.size // half)
        bias_pack = in_three(jnp.pad(hold(biases), (0, bias_rows * half - biases.size)).reshape(bias_rows, half))
        bias_pack = jnp.pad(bias_pack.reshape(3 * bias_rows, half), ((0, -3 * bias_rows % 16), (0, 0)))
        extra = jnp.concatenate([bias_pack, piece_qkv])

        context = attend(at, hold(tokens), qkv_rows, b_qv.reshape(2, head_cols), segments, heads, extra)
        (ctx_own, *ctx_send), first_z = run((context, first_z))
        ctx_z = [cyclic(v, s) for v, s in zip(ctx_send, others)]
        cut, end = w_out.shape[0] // 8, (w_out.shape[0] + w_in.shape[0]) // 8
        a, b = halves(first_z, slice(0, end))
        a1, b1 = by_x(a), by_y(b)
        c, d = halves(first_z, slice(end, None))
        done(c, d, a1, b1)
        a, b = plane_two(*hold((a, b, a1, b1)))
        a1, b1 = by_y(a), by_x(b)
        done(a, b, *ctx_z)
        ctx_z = hold(ctx_z)
        c1, d1 = by_x(hold(c)), by_y(hold(d))
        top = seq_len // 2
        bias_got = jnp.stack([p[top : top + 3 * bias_rows] for p in ctx_z]).astype(F32)
        bias_got = bias_got.reshape(n_tensor - 1, 3, bias_rows * half)
        bias_got = bias_got[:, 0] + bias_got[:, 1] + bias_got[:, 2]
        bias_all = jnp.concatenate([biases[None], bias_got[:, : biases.size]])
        b_inner_all = bias_all[:, :hidden_cols]
        b_qv_all = bias_all[:, hidden_cols:].reshape(n_tensor, 2, head_cols)
        done(b_inner_all, a1, b1)
        a, b, a1, b1 = hold((a, b, a1, b1))
        in_both = plane_three(a, b, a1, b1, slice(cut, None))
        in_core = by_core(in_both)
        out_both = plane_three(a, b, a1, b1, slice(0, cut))
        out_core = by_core(out_both)
        done(in_both, out_both, c1, d1)
        c, d = plane_two(*hold((c, d, c1, d1)))
        c1, d1 = by_y(c), by_x(d)
        done(c, d, out_core, in_core)
        out_got = ordered(*hold((out_both, out_core)), core, 0).transpose(3, 0, 1, 2, 4, 5)
        out_all = jnp.concatenate([w_out[None], out_got.reshape(n_tensor - 1, *w_out.shape)])
        in_parts = (w_in, in_both, in_core)
        e = jnp.stack([p[-piece_qkv.shape[0] :] for p in ctx_z])
        e1 = by_x(e)
        done(out_all, in_core, e)
        ctx = [ctx_own, *ctx_z]
        made = rise(at, hold(ctx), out_all, tokens, gains, shifts, in_parts, b_inner_all)
        made, c1, d1, e1 = run((made, c1, d1, e1))
        hidden1, hidden_low, norm_one, recip_one, activation, slope, tokens_rel, hidden_rel = made
        down_both = plane_three(c, d, c1, d1, slice(None))
        down_core = by_core(down_both)
        e = ordered(e, e1, x, 0)
        e1 = by_y(e)
        done(down_both, down_core, e)
        down_parts = (w_down, down_both, down_core)
        made = fall(at, hold(activation), down_parts, hidden1, cotangent, gains, shifts)
        made, e1 = run((made, e1))
        output_own, grad_r2, grad_r2_low, vec_two, keep1, send1 = made

        steps = [(i, i + 1) for i in range(n_tensor - 1)]
        back_steps = [(i + 1, i) for i in range(n_tensor - 1)]

        def hop(right, left, step):
            return (
                lax.ppermute(right, "tensor", steps[step:]),
                lax.ppermute(left, "tensor", back_steps[: len(steps) - step]),
            )

        block = width // 8

        class Part:
            def __init__(self, slots, *arrays):
                self.parts = [v[:, slots].reshape(2, 2, -1, *v.shape[2:]) for v in arrays]

            def total(self, *index):
                terms = [p[index].astype(F32) for p in self.parts]
                return functools.reduce(lambda u, v: u + v, terms).astype(BF)

            def take(self, got):
                self.parts = [p[0] for p in self.parts]
                self.parts.append(got.reshape(self.parts[0].shape))

            def totals(self):
                return [self.total(i) for i in range(self.parts[0].shape[0])]

        def pair_of(keep, got):
            count = keep.shape[1]
            return Part(slice(0, count // 2), keep, got), Part(slice(count // 2, count), keep, got)

        def plane(by_first, by_second):
            flying = []
            for move, group in ((by_x, by_first), (by_y, by_second)):
                sends = [p.total(1) for p in group]
                flat = jnp.concatenate([v.reshape(-1, *v.shape[-2:]) for v in sends])
                done(*order.last, flat)
                flying.append(move(flat))
            return flying

        def landed(flying, *groups):
            for flat, group in zip(flying, groups):
                first = 0
                for p in group:
                    size = math.prod(p.parts[0].shape[:-2]) // 2
                    p.take(flat[first : first + size])
                    first += size

        z_near = lambda v: swap(v, "tensor", n_tensor, 1)
        z_far = lambda v: swap(v, "tensor", n_tensor, 2)
        odd = (z & 1) == 1

        def after_near(values, got):
            first, second = jnp.where(odd, got[1], got[0]), jnp.where(odd, got[0], got[1])
            return values[0].astype(F32) + first.astype(F32), values[1].astype(F32) + second.astype(F32)

        def outer_rest(mine):
            bit = 2
            while bit < n_outer:
                mine = mine + swap(mine.astype(BF), "outer", n_outer, bit).astype(F32)
                bit *= 2
            return mine

        def whole_rows(mine, got):
            return ordered(mine, got.astype(F32), y, 0).reshape(2 * block, mine.shape[-1])

        out_1 = hop(output_own, output_own, 0)
        core1 = by_core(send1)
        qkv_both = ordered(e, e1, y, 0)
        qkv_core = by_core(qkv_both)
        qkv_parts = (flat_qkv, qkv_both, qkv_core)
        done(qkv_both, core1)
        h1 = pair_of(*hold((keep1, core1)))
        flight = plane([h1[0]], [h1[1]])
        made = back(
            at, hold(grad_r2), grad_r2_low, down_parts, slope, in_parts, norm_one, recip_one, gains, hidden_rel
        )
        made, qkv_core, out_1, flight = run((made, qkv_core, out_1, flight))
        qkv_parts = (flat_qkv, qkv_both, qkv_core)
        grad_binner, grad_r1, grad_r1_low, grad_r1_rel, vec_one, keep2, send2 = made
        out_2 = hop(*out_1, 1)
        core2 = by_core(send2)
        landed(flight, [h1[0]], [h1[1]])
        done(core2)
        h2 = pair_of(*hold((keep2, core2)))
        groups = [h2[0], h1[1]], [h2[1], h1[0]]
        flight = plane(*groups)
        two = n_tensor // 2
        made = attend_back(
            at, 0, tokens, hold(grad_r1_low), grad_r1, ctx[:two], qkv_parts, b_qv_all, heads, out_all, segments,
            tokens_rel, grad_r1_rel, F32,
        )
        made, out_2, flight = run((made, out_2, flight))
        bqv_a, tok_a, keep_a, send_a = made
        out_3 = hop(*out_2, 2)
        core_a = by_core(send_a)
        landed(flight, *groups)
        total1 = h1[0].totals() + h1[1].totals()
        near1 = z_near(jnp.stack([total1[1], total1[3]]))
        done(core_a)
        ha = pair_of(*hold((keep_a, core_a)))
        groups = [ha[0], h2[1]], [ha[1], h2[0]]
        flight = plane(*groups)
        made = attend_back(
            at, two, tokens, hold(grad_r1_low), tok_a, ctx[two:], qkv_parts, b_qv_all, heads, out_all, segments,
            tokens_rel, grad_r1_rel, BF,
        )
        made, out_3, flight, near1 = run((made, out_3, flight, near1))
        bqv_b, tok_own, keep_b, send_b = made
        tok_1 = hop(tok_own, tok_own, 0)
        core_b = by_core(send_b)
        landed(flight, *groups)

        grad_bqv = jnp.concatenate([bqv_a, bqv_b])
        slot_vec = [
            jnp.concatenate([grad_binner[s].reshape(-1, half), grad_bqv[s].reshape(-1, half)]) for s in range(n_tensor)
        ]
        common = jnp.concatenate([vec_one, vec_two]).reshape(-1, half)
        n_slot = slot_vec[0].shape[0]
        vec_got = z_near(jnp.concatenate([slot_vec[1], slot_vec[3], common]))
        done(core_b)
        hb = pair_of(*hold((keep_b, core_b)))
        groups = [hb[0], ha[1]], [hb[1], ha[0]]
        flight = plane(*groups)
        total2 = h2[0].totals() + h2[1].totals()
        near2 = jnp.stack([total2[1], total2[3]])
        mine1, far1 = after_near((total1[0], total1[2]), near1)
        far1 = far1.astype(BF)
        done(*order.last, near2, far1, *tok_1, *flight, vec_got)
        tok_1, flight, vec_got, near2, far1 = hold((tok_1, flight, vec_got, near2, far1))
        tok_2 = hop(*tok_1, 1)
        near2 = z_near(near2)
        landed(flight, *groups)
        groups = [hb[1]], [hb[0]]
        flight = plane(*groups)
        vec_got = vec_got[: 2 * n_slot].reshape(2, n_slot, half), vec_got[2 * n_slot :]
        vec_0, vec_2 = after_near((slot_vec[0], slot_vec[2]), vec_got[0])
        common = common + vec_got[1]
        vec_send = jnp.concatenate([vec_2, common])
        done(vec_send, *flight)
        landed(hold(flight), *groups)
        total3 = [t for part in (*ha, *hb) for t in part.totals()]
        near3 = z_near(jnp.stack([total3[1], total3[3]]))
        vec_got = z_far(hold(vec_send))
        done(*total3, near2)
        mine2, far2 = after_near((total2[0], total2[2]), hold(near2))
        far12 = jnp.stack([far1, far2.astype(BF)])
        done(far12, *tok_2)
        tok_2, far12 = hold((tok_2, far12))
        tok_3 = hop(*tok_2, 2)
        far12 = z_far(far12)
        grad_tokens = place(at, tok_own, (tok_1[0], tok_2[0], tok_2[0]), (tok_1[1], tok_2[1], tok_2[1]), F32)
        grad_tokens, near3 = run((grad_tokens, near3))
        mine3, far3 = after_near((total3[0], total3[2]), near3)
        far3 = z_far(far3.astype(BF))
        done(far12, far3)
        done(hold(far12))
        mine12 = outer_rest(jnp.stack([mine1, mine2]) + hold(far12).astype(F32))
        got12 = by_y(mine12.astype(BF))
        done(mine12)
        output = place(at, output_own, (out_1[0], out_2[0], out_3[0]), (out_1[1], out_2[1], hold(out_3[1])), BF)
        output = output.reshape(seq_count, seq_len, width)
        done(output, vec_got)
        vectors = jnp.concatenate([vec_0, common]) + hold(vec_got)
        vec_got = by_core(vectors)
        mine3 = outer_rest(mine3 + hold(far3).astype(F32))
        got3 = by_y(mine3.astype(BF))
        done(mine3, vec_got)
        vectors = vectors + hold(vec_got)
        vec_got = by_x(vectors)
        done(got12)
        got12 = hold(got12)
        done_wdown = whole_rows(mine12[0], got12[0])
        done_win = whole_rows(mine12[1], got12[1])
        done(done_wdown, done_win, got3, vec_got)
        got3, vec_got = hold((got3, vec_got))
        vectors = vectors + vec_got
        vec_got = by_y(vectors)
        done_last = whole_rows(mine3, got3)
        vectors = vectors + hold(vec_got)
        bit = 2
        while bit < n_outer:
            vectors = vectors + swap(vectors, "outer", n_outer, bit)
            bit *= 2
        slot_sum = vectors[:n_slot].reshape(-1)
        common = vectors[n_slot:].reshape(6, width)
        common = jnp.stack([common[i] for i in (0, 3, 1, 2, 4, 5)])
        part = lambda v, n: lax.dynamic_slice_in_dim(v, l_index * (n // n_local), n // n_local, v.ndim - 1)
        binner = part(slot_sum[:hidden_cols].reshape(b_inner.shape), head_size)
        bqv = part(slot_sum[hidden_cols:].reshape(b_qv.shape), head_size)
        common = part(common, width)
        grad_wqkv = done_last[:, : 3 * head_cols].reshape(width // n_local, 3, head_cols).transpose(1, 0, 2)
        done(grad_wqkv, common, binner, bqv, *tok_3)
        grad_tokens = place_end(at, *hold((tok_own, tok_3[0], tok_3[1], grad_tokens)))
        grad_tokens = grad_tokens.reshape(seq_count, seq_len, width)
        return (
            output,
            grad_tokens,
            grad_wqkv,
            bqv,
            done_last[:, 3 * head_cols :].T,
            done_win,
            binner,
            done_wdown.T,
            common[:2],
            common[2:],
        )

    return local


def solution(mesh):
    placed = (
        P(("outer", "local"), None, None),
        P(("outer", "local"), None),
        P(None, None, "tensor"),
        P(None, "tensor", None),
        P("tensor", None),
        P(None, "tensor"),
        P("tensor", None),
        P("tensor", None),
        P(),
        P(),
        P(("outer", "local"), None, None),
    )
    return jax.shard_map(
        make(dict(mesh.shape)),
        mesh=mesh,
        in_specs=placed,
        out_specs=(
            P(("outer", "local"), None, None),
            P(("outer", "local"), None, None),
            P(None, "local", "tensor"),
            P(None, "tensor", "local"),
            P("tensor", "local"),
            P("local", "tensor"),
            P("tensor", "local"),
            P("tensor", "local"),
            P(None, "local"),
            P(None, "local"),
        ),
        check_vma=False,
    )
```

```python
import functools
import math

import jax
import jax.numpy as jnp
from jax import lax
from jax.experimental import pallas as pl
from jax.experimental.pallas import tpu as pltpu
from jax.sharding import PartitionSpec as P

EPSILON = 1e-12
MASKED = -1e30
BF = jnp.bfloat16
F32 = jnp.float32
SHORT = pl.CostEstimate(flops=1000, bytes_accessed=1000, transcendentals=0)
ROOM = {'attend': 36, 'rise': 36, 'fall': 36, 'back': 36, 'attend_back': 48}
ROWS_BY_ROWS = (((1,), (1,)), ((), ()))


def dot(left, right):
    return jnp.dot(left, right, preferred_element_type=F32)


def dot_t(left, right):
    return lax.dot_general(left, right, ROWS_BY_ROWS, preferred_element_type=F32)


def normalize(values):
    centre = values - jnp.mean(values, axis=-1, keepdims=True)
    variance = jnp.mean(centre * centre, axis=-1, keepdims=True)
    recip = lax.rsqrt(variance + EPSILON)
    return (centre * recip, recip)


def norm_back(grad_norm, normed, recip):
    first = jnp.mean(grad_norm, axis=-1, keepdims=True)
    second = jnp.mean(grad_norm * normed, axis=-1, keepdims=True)
    return recip * (grad_norm - first - normed * second)


def col_sum(value):
    return jnp.sum(value, axis=0, keepdims=True)


def softmax_columns(raw, allowed):
    scores = jnp.where(allowed, raw, MASKED)
    grown = jnp.exp(scores - jnp.max(scores, axis=0, keepdims=True))
    return grown, 1.0 / jnp.sum(grown, axis=0, keepdims=True)


def column(row):
    return jnp.broadcast_to(row, (8, row.shape[1])).T[:, :1]


def store_relative(out_ref, value, at_ref):
    flipped = value.T.astype(BF)
    block = flipped.shape[0] // 8
    for i in range(8):
        spot = (((i >> 1) & 1) ^ at_ref[0]) * 4 + ((i >> 2) ^ at_ref[1]) * 2 + ((i & 1) ^ at_ref[2])
        out_ref[pl.ds(pl.multiple_of(spot * block, block), block)] = flipped[i * block : (i + 1) * block]


def call(kernel, name, at, grid, in_specs, out_specs, out_shape, scratch=()):
    return pl.pallas_call(
        kernel,
        grid_spec=pltpu.PrefetchScalarGridSpec(
            num_scalar_prefetch=1, grid=grid, in_specs=in_specs, out_specs=out_specs, scratch_shapes=list(scratch)
        ),
        out_shape=out_shape,
        cost_estimate=SHORT,
        compiler_params=pltpu.CompilerParams(vmem_limit_bytes=ROOM.get(name, 60) * 2**20),
        name=name,
    )


def const(*shape):
    return pl.BlockSpec(shape, lambda i, at: (0,) * len(shape))


def slot(*shape):
    return pl.BlockSpec((1, *shape), lambda i, at: (i,) + (0,) * len(shape))


def attend_kernel(heads, scale, at_ref, x_ref, w_ref, bias_ref, seg_ref, extra_ref, *refs):
    *out_refs, q_low, k_side, v_low, sum_ref = refs
    x = x_ref[0]
    size = w_ref.shape[1] // heads
    q_t = ((dot_t(w_ref[0], x) + column(bias_ref[0:1])).astype(BF) * scale).astype(BF)
    k = dot_t(x, w_ref[1]).astype(BF)
    v_t = (dot_t(w_ref[2], x) + column(bias_ref[1:2])).astype(BF)
    row = seg_ref[pl.ds(pl.program_id(0), 1)].astype(F32)
    allowed = column(row) == row
    q_low[...] = q_t.reshape(q_low.shape)
    v_low[...] = v_t.reshape(v_low.shape)
    for h in range(heads):
        k_side[h] = k[:, h * size : (h + 1) * size]

    def one_head(h, carry):
        grown, inv = softmax_columns(dot(k_side[h], q_low[h]), allowed)
        sum_ref[pl.ds(pl.multiple_of(h * size, size), size)] = dot(v_low[h], grown.astype(BF)) * inv
        return carry

    lax.fori_loop(0, heads, one_head, 0)
    context = sum_ref[...].T.astype(BF)
    count, rows, cols = len(out_refs), context.shape[0] // 2, context.shape[1]
    ahead = lax.rem(pl.program_id(0) + count - at_ref[3], count)
    for s, out_ref in enumerate(out_refs):
        @pl.when(ahead == s)
        def _():
            out_ref[:rows, :cols] = context[:rows]
            out_ref[:rows, cols:] = context[rows:]
            out_ref[rows:] = extra_ref[...]


def attend(at, tokens, w_rows, bias, segments, heads, extra):
    seqs, length, width = tokens.shape
    cols = w_rows.shape[1]
    return call(
        functools.partial(attend_kernel, heads, (cols // heads) ** -0.5), "attend", at, (seqs,),
        [slot(length, width), const(3, cols, width), const(2, cols), const(seqs, length), const(*extra.shape)],
        [const(length // 2 + extra.shape[0], 2 * cols)] * seqs,
        [jax.ShapeDtypeStruct((length // 2 + extra.shape[0], 2 * cols), BF)] * seqs,
        [
            pltpu.VMEM((heads, cols // heads, length), BF), pltpu.VMEM((heads, length, cols // heads), BF),
            pltpu.VMEM((heads, cols // heads, length), BF), pltpu.VMEM((cols, length), F32),
        ],
    )(at, tokens, w_rows, bias, segments, extra)


def fetch_copies(core, own_ref, mine_ref, theirs_ref, held, sems):
    slots = held.shape[0]
    copies = [[pltpu.make_async_copy(own_ref.at[c], held.at[0, c], sems.at[0, c]) for c in range(2)]]
    for s in range(1, slots):
        copies.append([
            pltpu.make_async_copy(mine_ref.at[:, s - 1], held.at[s, core], sems.at[s, 0]),
            pltpu.make_async_copy(theirs_ref.at[:, s - 1], held.at[s, 1 - core], sems.at[s, 1]),
        ])
    return copies


def fetch_slot(at_ref, refs, held, sems):
    step = pl.program_id(0)
    copies = fetch_copies(at_ref[0], *refs, held, sems)

    @pl.when(step == 0)
    def _():
        for pair in copies:
            for copy in pair:
                copy.start()

    for s, pair in enumerate(copies):
        @pl.when(step == s)
        def _():
            for copy in pair:
                copy.wait()

    return held[step].reshape(8 * held.shape[3], held.shape[4])


def pieces(weight):
    own, mine, theirs = weight
    piece = own.shape[0] // 8
    split = lambda v: v.reshape(4, -1, piece, own.shape[1])
    return own.reshape(2, 4, piece, own.shape[1]), split(mine), split(theirs)


def held_scratch(slots, weight):
    rows, width = weight[0].shape
    return [pltpu.VMEM((slots, 2, 4, rows // 8, width), BF), pltpu.SemaphoreType.DMA((slots, 2))]


def here(*shape):
    return pl.BlockSpec((1, *shape), lambda i, at: (at[3],) + (0,) * len(shape))


FAR = pl.BlockSpec(memory_space=pl.ANY)


def rise_kernel(slots, at_ref, *refs):
    ctx_refs = refs[:slots]
    (w_out_ref, x_ref, gains_ref, shifts_ref, own_ref, mine_ref, theirs_ref, bias_ref,
     hidden_ref, low_ref, norm_ref, recip_ref, act_ref, slope_ref, x_rel_ref, hidden_rel_ref, held, sems, ctx_ref) = refs[slots:]
    step = pl.program_id(0)
    weight = fetch_slot(at_ref, (own_ref, mine_ref, theirs_ref), held, sems)

    @pl.when(step == 0)
    def _():
        rows, cols = low_ref.shape[0] // 2, w_out_ref.shape[1]
        for s in range(slots):
            ctx_ref[:rows, s * cols : (s + 1) * cols] = ctx_refs[s][:rows, :cols]
            ctx_ref[rows:, s * cols : (s + 1) * cols] = ctx_refs[s][:rows, cols:]
        attention = dot(ctx_ref[...], w_out_ref[...].reshape(slots * cols, -1))
        own = x_ref[0].astype(F32)
        norm, recip = normalize(own + attention + shifts_ref[0:1])
        hidden = norm * gains_ref[0:1] + shifts_ref[1:2]
        norm_ref[...] = norm
        recip_ref[...] = recip
        hidden_ref[...] = hidden
        low_ref[...] = hidden.astype(BF)
        store_relative(x_rel_ref, own, at_ref)
        store_relative(hidden_rel_ref, hidden, at_ref)

    part = 256 if weight.shape[1] % 256 == 0 else weight.shape[1]
    spots = [slice(i, i + part) for i in range(0, weight.shape[1], part)]
    ready = dot(low_ref[...], weight[:, spots[0]])
    for i, cols in enumerate(spots):
        pre = ready + bias_ref[0, :, cols]
        if i + 1 < len(spots):
            ready = dot(low_ref[...], weight[:, spots[i + 1]])
        cumul = 0.5 * (1.0 + lax.erf(pre * (1.0 / math.sqrt(2.0))))
        slope = cumul + pre * jnp.exp(-0.5 * pre * pre) * (1.0 / math.sqrt(2.0 * math.pi))
        act_ref[0, :, cols] = (pre * cumul).astype(BF)
        slope_ref[0, :, cols] = slope.astype(BF)


def rise(at, ctx, w_out, x, gains, shifts, w_in, bias):
    slots, cols, rows = len(ctx), w_out.shape[1], x.shape[1]
    width, hidden = w_in[0].shape
    return call(
        functools.partial(rise_kernel, slots), "rise", at, (slots,),
        [const(*ctx[0].shape)] * slots
        + [
            const(slots, cols, width), here(rows, width), const(*gains.shape),
            const(*shifts.shape), FAR, FAR, FAR, slot(1, hidden),
        ],
        [
            const(rows, width), const(rows, width), const(rows, width), const(rows, 1),
            slot(rows, hidden), slot(rows, hidden), const(width, rows), const(width, rows),
        ],
        [
            jax.ShapeDtypeStruct((rows, width), F32),
            jax.ShapeDtypeStruct((rows, width), BF),
            jax.ShapeDtypeStruct((rows, width), F32),
            jax.ShapeDtypeStruct((rows, 1), F32),
            jax.ShapeDtypeStruct((slots, rows, hidden), BF),
            jax.ShapeDtypeStruct((slots, rows, hidden), BF),
            jax.ShapeDtypeStruct((width, rows), BF),
            jax.ShapeDtypeStruct((width, rows), BF),
        ],
        held_scratch(slots, w_in) + [pltpu.VMEM((rows, slots * cols), BF)],
    )(at, *ctx, w_out, x, gains, shifts, *pieces(w_in), bias[:, None, :])


def store_parts(keep_ref, send_ref, x_first, first, whole):
    block, last = keep_ref.shape[2], first + whole.shape[1]
    low = whole.astype(BF)
    for i in range(4):
        spot = jnp.where(x_first, i, 3 - i) if i in (1, 2) else i
        keep_ref[spot, 0, :, first:last] = low[i * block : (i + 1) * block]
        send_ref[spot, 0, :, first:last] = low[(4 + i) * block : (5 + i) * block]


def fall_kernel(slots, at_ref, act_ref, own_ref, mine_ref, theirs_ref, hidden_ref, cot_ref, gains_ref, shifts_ref,
                out_ref, grad_ref, low_ref, vec_ref, keep_ref, send_ref, sum_ref, rel_ref, held, sems):
    s = pl.program_id(0)
    copies = fetch_copies(at_ref[0], own_ref, mine_ref, theirs_ref, held, sems)

    @pl.when(s == 0)
    def _():
        for pair in copies:
            for copy in pair:
                copy.start()

    for i, pair in enumerate(copies):
        @pl.when(s == i)
        def _():
            for copy in pair:
                copy.wait()

    @pl.when(s == 0)
    def _():
        sum_ref[...] = jnp.zeros_like(sum_ref)

    @pl.when(s < slots)
    def _():
        sum_ref[...] += dot(act_ref[0], held[s].reshape(8 * held.shape[3], held.shape[4]))

    @pl.when(s == slots - 1)
    def _():
        norm, recip = normalize(hidden_ref[...] + sum_ref[...] + shifts_ref[2:3])
        out_ref[...] = (norm * gains_ref[1:2] + shifts_ref[3:4]).astype(BF)
        cot = cot_ref[0].astype(F32)
        grad = norm_back(cot * gains_ref[1:2], norm, recip)
        grad_ref[...] = grad
        low_ref[...] = grad.astype(BF)
        store_relative(rel_ref, grad, at_ref)
        vec_ref[0:1] = col_sum(cot * norm)
        vec_ref[1:2] = col_sum(grad)
        vec_ref[2:3] = col_sum(cot)

    @pl.when(s >= slots)
    def _():
        store_parts(keep_ref, send_ref, s - slots < slots // 2, 0, dot(rel_ref[...], act_ref[0]))


def part_specs(slots, block, cols, start=0):
    spec = pl.BlockSpec((4, 1, block, cols), lambda i, at: (0, lax.max(i - start, 0), 0, 0))
    return [spec] * 2, [jax.ShapeDtypeStruct((4, slots, block, cols), BF)] * 2


def fall(at, act, w_down, hidden, cot, gains, shifts):
    slots, rows, inner = act.shape
    width = w_down[0].shape[1]
    specs, shapes = part_specs(slots, width // 8, inner, slots)
    return call(
        functools.partial(fall_kernel, slots), "fall", at, (2 * slots,),
        [
            pl.BlockSpec((1, rows, inner), lambda i, at: (lax.rem(i, slots), 0, 0)), FAR, FAR, FAR, const(rows, width),
            here(rows, width), const(*gains.shape), const(*shifts.shape),
        ],
        [const(rows, width), const(rows, width), const(rows, width), const(3, width), *specs],
        [
            jax.ShapeDtypeStruct((rows, width), BF),
            jax.ShapeDtypeStruct((rows, width), F32),
            jax.ShapeDtypeStruct((rows, width), BF),
            jax.ShapeDtypeStruct((3, width), F32),
            *shapes,
        ],
        [pltpu.VMEM((rows, width), F32), pltpu.VMEM((width, rows), BF)] + held_scratch(slots, w_down),
    )(at, act, *pieces(w_down), hidden, cot, gains, shifts)


def back_kernel(slots, at_ref, grad2_ref, low2_ref, own2_ref, mine2_ref, theirs2_ref, slope_ref, own1_ref, mine1_ref,
                theirs1_ref, norm_ref, recip_ref, gains_ref, hidden_rel_ref, bias_ref, grad_ref, low_ref, rel_ref, vec_ref,
                keep_ref, send_ref, sum_ref, held2, sems2, held1, sems1):
    s = pl.program_id(0)
    w_down = fetch_slot(at_ref, (own2_ref, mine2_ref, theirs2_ref), held2, sems2)
    w_in = fetch_slot(at_ref, (own1_ref, mine1_ref, theirs1_ref), held1, sems1)
    pre = dot_t(low2_ref[...], w_down) * slope_ref[0].astype(F32)
    bias_ref[0] = col_sum(pre)
    pre_low = pre.astype(BF)
    store_parts(keep_ref, send_ref, s < slots // 2, 0, dot(hidden_rel_ref[...], pre_low))
    share = dot_t(pre_low, w_in)

    @pl.when(s == 0)
    def _():
        sum_ref[...] = share

    @pl.when(s > 0)
    def _():
        sum_ref[...] += share

    @pl.when(s == slots - 1)
    def _():
        norm = norm_ref[...]
        grad_h = grad2_ref[...] + sum_ref[...]
        grad = norm_back(grad_h * gains_ref[0:1], norm, recip_ref[...])
        grad_ref[...] = grad
        low_ref[...] = grad.astype(BF)
        store_relative(rel_ref, grad, at_ref)
        vec_ref[0:1] = col_sum(grad_h * norm)
        vec_ref[1:2] = col_sum(grad)
        vec_ref[2:3] = col_sum(grad_h)


def back(at, grad2, low2, w_down, slope, w_in, norm, recip, gains, hidden_rel):
    slots, rows, inner = slope.shape
    width = grad2.shape[1]
    specs, shapes = part_specs(slots, width // 8, inner)
    return call(
        functools.partial(back_kernel, slots), "back", at, (slots,),
        [
            const(rows, width), const(rows, width), FAR, FAR, FAR, slot(rows, inner), FAR, FAR, FAR,
            const(rows, width), const(rows, 1), const(*gains.shape), const(width, rows),
        ],
        [slot(1, inner), const(rows, width), const(rows, width), const(width, rows), const(3, width), *specs],
        [
            jax.ShapeDtypeStruct((slots, 1, inner), F32),
            jax.ShapeDtypeStruct((rows, width), F32),
            jax.ShapeDtypeStruct((rows, width), BF),
            jax.ShapeDtypeStruct((width, rows), BF),
            jax.ShapeDtypeStruct((3, width), F32),
            *shapes,
        ],
        [pltpu.VMEM((rows, width), F32)] + held_scratch(slots, w_down) + held_scratch(slots, w_in),
    )(at, grad2, low2, *pieces(w_down), slope, *pieces(w_in), norm, recip, gains, hidden_rel)


def attend_back_kernel(first, slots, heads, scale, at_ref, x_ref, low_ref, grad_ref, *refs):
    ctx_refs = refs[:slots]
    (own_ref, mine_ref, theirs_ref, bias_ref, w_out_ref, seg_ref, x_rel_ref, grad_rel_ref,
     vec_ref, tok_ref, keep_ref, send_ref, sum_ref, q_ref, k_ref, v_ref, ctx_ref, proj_ref, held, sems) = refs[slots:]
    s = pl.program_id(0)
    half = mine_ref.shape[-1]
    mine_at = pl.ds(pl.multiple_of(at_ref[0] * half, half), half)
    theirs_at = pl.ds(pl.multiple_of((1 - at_ref[0]) * half, half), half)
    copies = []
    for i in range(slots):
        if first + i == 0:
            copies.append([
                pltpu.make_async_copy(own_ref.at[:2], held.at[i, :2], sems.at[i, 0]),
                pltpu.make_async_copy(own_ref.at[2:], held.at[i, 2:], sems.at[i, 1]),
            ])
        else:
            copies.append([
                pltpu.make_async_copy(mine_ref.at[:, first + i - 1], held.at[i, :, :, mine_at], sems.at[i, 0]),
                pltpu.make_async_copy(theirs_ref.at[:, first + i - 1], held.at[i, :, :, theirs_at], sems.at[i, 1]),
            ])

    @pl.when(s == 0)
    def _():
        for pair in copies:
            for copy in pair:
                copy.start()

    for i, pair in enumerate(copies):
        @pl.when(s == i)
        def _():
            for copy in pair:
                copy.wait()
            rows, cols = ctx_ref.shape[0] // 2, ctx_ref.shape[1]
            ctx_ref[:rows] = ctx_refs[i][:rows, :cols]
            ctx_ref[rows:] = ctx_refs[i][:rows, cols:]

    x, low = x_ref[0], low_ref[...]
    cols = w_out_ref.shape[1]
    size = cols // heads
    weight = held[s].reshape(3, cols, x.shape[1])
    q_t = (dot_t(weight[0], x) + column(bias_ref[0, 0:1])).astype(BF)
    q_scaled = (q_t * scale).astype(BF)
    q = q_t.T
    k_t = dot_t(weight[1], x).astype(BF)
    k = k_t.T
    v = (dot_t(x, weight[2]) + bias_ref[0, 1:2]).astype(BF)
    gc_t = dot_t(w_out_ref[0], low).astype(BF)
    gc = gc_t.T
    row = seg_ref[pl.ds(at_ref[3], 1)].astype(F32)
    allowed = column(row) == row
    spot = lambda h: slice(h * size, (h + 1) * size)
    first_of = lambda h: (dot(k[:, spot(h)], q_scaled[spot(h)]), dot(v[:, spot(h)], gc_t[spot(h)]))
    ready = first_of(0)
    for h in range(heads):
        at = spot(h)
        raw, grad_probs = ready
        if h + 1 < heads:
            ready = first_of(h + 1)
        if h == 0:
            whole = dot(grad_rel_ref[...], ctx_ref[...])
            store_parts(keep_ref, send_ref, s < slots // 2, proj_ref.shape[1], whole)
        grown, inv = softmax_columns(raw, allowed)
        probs = grown * inv
        inner = jnp.sum(probs * grad_probs, axis=0, keepdims=True)
        grad_scores = (probs * (grad_probs - inner) * scale).astype(BF)
        v_ref[:, at] = dot(probs.astype(BF), gc[:, at])
        q_ref[at] = dot(k_t[at], grad_scores)
        k_ref[:, at] = dot(grad_scores, q[:, at])
    grad_q = q_ref[...].T
    grad_v = v_ref[...]
    vec_ref[0, 0:1] = col_sum(grad_q)
    vec_ref[0, 1:2] = col_sum(grad_v)
    parts = [grad_q.astype(BF), k_ref[...].astype(BF), grad_v.astype(BF)]
    for c in range(3):
        proj_ref[:, c * cols : (c + 1) * cols] = parts[c]
    proj = proj_ref[...]
    share = dot(proj, weight.reshape(3 * cols, x.shape[1]))
    store_parts(keep_ref, send_ref, s < slots // 2, 0, dot(x_rel_ref[...], proj))

    @pl.when(s == 0)
    def _():
        sum_ref[...] = share + grad_ref[...]

    @pl.when(s > 0)
    def _():
        sum_ref[...] += share

    @pl.when(s == slots - 1)
    def _():
        tok_ref[...] = sum_ref[...].astype(tok_ref.dtype)


def attend_back(at, first, x, low, grad, ctx, w_qkv, bias, heads, w_out, segments, x_rel, grad_rel, kind):
    slots, cols = len(ctx), w_out.shape[1]
    rows, width = x.shape[1:]
    own, mine, theirs = w_qkv
    piece, half = mine.shape[-2:]
    split = lambda v: v.reshape(4, -1, piece, half)
    later = lambda *shape: pl.BlockSpec((1, *shape), lambda i, at: (i + first,) + (0,) * len(shape))
    specs, shapes = part_specs(slots, width // 8, 4 * cols)
    return call(
        functools.partial(attend_back_kernel, first, slots, heads, (cols // heads) ** -0.5), "attend_back", at, (slots,),
        [here(rows, width), const(rows, width), const(rows, width)]
        + [const(*ctx[0].shape)] * slots
        + [
            FAR, FAR, FAR, later(2, cols), later(cols, width), const(*segments.shape), const(width, rows), const(width, rows),
        ],
        [slot(2, cols), const(rows, width), *specs],
        [
            jax.ShapeDtypeStruct((slots, 2, cols), F32),
            jax.ShapeDtypeStruct((rows, width), kind),
            *shapes,
        ],
        [
            pltpu.VMEM((rows, width), F32), pltpu.VMEM((cols, rows), F32), pltpu.VMEM((rows, cols), F32),
            pltpu.VMEM((rows, cols), F32), pltpu.VMEM((rows, cols), BF), pltpu.VMEM((rows, 3 * cols), BF),
            pltpu.VMEM((slots, 4, piece, width), BF), pltpu.SemaphoreType.DMA((slots, 2)),
        ],
    )(at, x, low, grad, *ctx, own.reshape(4, piece, width), split(mine), split(theirs), bias, w_out, segments, x_rel, grad_rel)


def place_kernel(slots, at_ref, *refs):
    sources, (out_ref, held, sems) = refs[:-3], refs[-3:]
    here = at_ref[3]

    def each(step, act):
        for s in range(slots):
            for source, wanted in ((s, here - step == s),) + (((slots - 1 + s, step - here == s),) if s else ()):
                @pl.when(wanted)
                def _():
                    act(pltpu.make_async_copy(sources[source], held.at[step], sems.at[step]))

    step = pl.program_id(0)

    @pl.when(step == 0)
    def _():
        for j in range(slots):
            each(j, lambda copy: copy.start())

    pltpu.make_async_copy(sources[0], held.at[step], sems.at[step]).wait()
    out_ref[0] = held[step].astype(out_ref.dtype)


def place_end_kernel(slots, at_ref, own_ref, behind_ref, ahead_ref, whole_ref, out_ref, held, sem):
    here = at_ref[3]
    for source, wanted in ((ahead_ref, here == 0), (behind_ref, here == slots - 1), (own_ref, lax.rem(here, slots - 1) > 0)):
        @pl.when(wanted)
        def _():
            copy = pltpu.make_async_copy(source, held, sem)
            copy.start()
            copy.wait()

    out_ref[0] = held[...].astype(out_ref.dtype)


def place_end(at, own, behind, ahead, whole):
    slots = whole.shape[0]
    spot = lambda i, at: (jnp.where(at[3] == 0, slots - 1, jnp.where(at[3] == slots - 1, 0, at[3])), 0, 0)
    return pl.pallas_call(
        functools.partial(place_end_kernel, slots),
        grid_spec=pltpu.PrefetchScalarGridSpec(
            num_scalar_prefetch=1, grid=(1,), in_specs=[FAR] * 4, out_specs=pl.BlockSpec((1, *own.shape), spot),
            scratch_shapes=[pltpu.VMEM(own.shape, own.dtype), pltpu.SemaphoreType.DMA],
        ),
        out_shape=jax.ShapeDtypeStruct(whole.shape, whole.dtype),
        input_output_aliases={4: 0},
        cost_estimate=SHORT,
        name="place_end",
    )(at, own, behind, ahead, whole)


def place(at, own, behind, ahead, kind):
    slots = len(behind) + 1
    values = [own, *behind, *ahead]
    return call(
        functools.partial(place_kernel, slots), "place", at, (slots,),
        [FAR] * len(values), slot(*own.shape),
        jax.ShapeDtypeStruct((slots, *own.shape), kind),
        [pltpu.VMEM((slots, *own.shape), own.dtype), pltpu.SemaphoreType.DMA((slots,))],
    )(at, *values)


def swap(value, axis, size, bit):
    return lax.ppermute(value, axis, [(i, i ^ bit) for i in range(size)])


def ordered(own, got, bit, axis):
    first = jnp.where(bit == 0, own, got)
    second = jnp.where(bit == 0, got, own)
    return jnp.stack([first, second], axis)


def in_three(value):
    high = value.astype(BF)
    rest = value - high.astype(F32)
    middle = rest.astype(BF)
    return jnp.stack([high, middle, (rest - middle.astype(F32)).astype(BF)])


class Order:
    def __init__(self):
        self.last = ()

    def hold(self, values, *waits):
        leaves, tree = jax.tree.flatten(values)
        held = lax.optimization_barrier((leaves, self.last, waits))[0]
        return jax.tree.unflatten(tree, held)

    def done(self, *values):
        self.last = tuple(values)

    def run(self, made, *waits):
        self.last = waits
        made = self.hold(made)
        self.last = tuple(jax.tree.leaves(made)[:1])
        return made


def make(sizes):
    n_outer, n_local, n_tensor = sizes["outer"], sizes["local"], sizes["tensor"]

    def local(tokens, segments, w_qkv, b_qv, w_out, w_in, b_inner, w_down, gains, shifts, cotangent):
        seq_count, seq_len, width = tokens.shape
        heads, head_size = b_qv.shape[1], b_qv.shape[2]
        head_cols = heads * head_size
        hidden_cols = w_in.shape[1]
        z = lax.axis_index("tensor")
        l_index = lax.axis_index("local")
        core, x = l_index & 1, l_index >> 1
        y = lax.axis_index("outer") & 1
        z_from = lambda s: jnp.mod(z - s, n_tensor)
        z_to = lambda s: jnp.mod(z + s, n_tensor)
        cyclic = lambda v, s: lax.ppermute(v, "tensor", [(i, (i + s) % n_tensor) for i in range(n_tensor)])
        pick = lambda v, i: lax.dynamic_index_in_dim(v, i, 0, keepdims=False)
        others = range(1, n_tensor)
        by_x = lambda v: swap(v, "local", n_local, 2)
        by_y = lambda v: swap(v, "outer", n_outer, 1)
        by_core = lambda v: swap(v, "local", n_local, 1)
        at = jnp.stack([core, x, y, z]).astype(jnp.int32)
        order = Order()
        hold, done, run = order.hold, order.done, order.run

        place8 = core * 4 + y * 2 + x
        half = width // 2

        def piece_of(weight):
            n = weight.shape[0] // 8
            return lax.dynamic_slice_in_dim(weight, place8 * n, n, 0)

        def halves(parts, rows):
            return jnp.stack([p[rows, :half] for p in parts]), jnp.stack([p[rows, half:] for p in parts])

        def plane_two(a, b, a1, b1):
            return ordered(a, a1, x, 0), ordered(b, b1, y, 0)

        def plane_three(a, b, a1, b1, rows):
            a, a1, b, b1 = (v[:, :, rows] for v in (a, a1, b, b1))
            return jnp.concatenate([ordered(a, a1, y, 0), ordered(b, b1, x, 1)], -1)

        qkv_rows = w_qkv.transpose(0, 2, 1)
        flat_qkv = qkv_rows.reshape(3 * head_cols, width)

        first = jnp.concatenate([piece_of(w_out), piece_of(w_in), piece_of(w_down)])
        first_z = [cyclic(first, s) for s in others]
        done(first)
        biases = jnp.concatenate([b_inner.reshape(-1), b_qv.reshape(-1)])
        bias_rows = -(-biases.size // half)
        bias_pack = in_three(jnp.pad(hold(biases), (0, bias_rows * half - biases.size)).reshape(bias_rows, half))
        bias_pack = jnp.pad(bias_pack.reshape(3 * bias_rows, half), ((0, -3 * bias_rows % 16), (0, 0)))

        context = attend(at, hold(tokens), qkv_rows, b_qv.reshape(2, head_cols), segments, heads, bias_pack)
        (ctx_own, *ctx_send), first_z = run((context, first_z))
        ctx_z = [cyclic(v, s) for v, s in zip(ctx_send, others)]
        cut, end = w_out.shape[0] // 8, (w_out.shape[0] + w_in.shape[0]) // 8
        a, b = halves(first_z, slice(0, end))
        a1, b1 = by_x(a), by_y(b)
        c, d = halves(first_z, slice(end, None))
        piece_qkv = lax.dynamic_slice(
            hold(flat_qkv), ((y * 2 + x) * (flat_qkv.shape[0] // 4), core * half), (flat_qkv.shape[0] // 4, half)
        )
        done(c, d, piece_qkv, a1, b1)
        a, b = plane_two(*hold((a, b, a1, b1)))
        a1, b1 = by_y(a), by_x(b)
        done(a, b, *ctx_z)
        ctx_z = hold(ctx_z)
        c1, d1 = by_x(hold(c)), by_y(hold(d))
        top = seq_len // 2
        bias_got = jnp.stack([p[top : top + 3 * bias_rows] for p in ctx_z]).astype(F32)
        bias_got = bias_got.reshape(n_tensor - 1, 3, bias_rows * half)
        bias_got = bias_got[:, 0] + bias_got[:, 1] + bias_got[:, 2]
        bias_all = jnp.concatenate([biases[None], bias_got[:, : biases.size]])
        b_inner_all = bias_all[:, :hidden_cols]
        b_qv_all = bias_all[:, hidden_cols:].reshape(n_tensor, 2, head_cols)
        done(b_inner_all, a1, b1)
        a, b, a1, b1, piece_qkv = hold((a, b, a1, b1, piece_qkv))
        third_z = [cyclic(piece_qkv, s) for s in others]
        in_both = plane_three(a, b, a1, b1, slice(cut, None))
        out_both = plane_three(a, b, a1, b1, slice(0, cut))
        done(in_both, out_both, b_inner_all, c1, d1)
        in_both, out_both, c, d, c1, d1 = hold((in_both, out_both, c, d, c1, d1))
        in_core, out_core = by_core(in_both), by_core(out_both)
        c, d = plane_two(c, d, c1, d1)
        done(c, d, in_core, out_core)
        c1, d1 = by_y(hold(c)), by_x(hold(d))
        out_got = ordered(*hold((out_both, out_core)), core, 0).transpose(3, 0, 1, 2, 4, 5)
        out_all = jnp.concatenate([w_out[None], out_got.reshape(n_tensor - 1, *w_out.shape)])
        in_parts = (w_in, in_both, in_core)
        done(out_all, *third_z)
        e = jnp.stack(hold(third_z))
        e1 = by_x(e)
        done(e)
        ctx = [ctx_own, *ctx_z]
        made = rise(at, hold(ctx), out_all, tokens, gains, shifts, in_parts, b_inner_all)
        made, c1, d1, e1 = run((made, c1, d1, e1))
        hidden1, hidden_low, norm_one, recip_one, activation, slope, tokens_rel, hidden_rel = made
        down_both = plane_three(c, d, c1, d1, slice(None))
        down_core = by_core(down_both)
        e = ordered(e, e1, x, 0)
        e1 = by_y(e)
        done(down_both, down_core, e)
        down_parts = (w_down, down_both, down_core)
        made = fall(at, hold(activation), down_parts, hidden1, cotangent, gains, shifts)
        made, e1 = run((made, e1))
        output_own, grad_r2, grad_r2_low, vec_two, keep1, send1 = made

        steps = [(i, i + 1) for i in range(n_tensor - 1)]
        back_steps = [(i + 1, i) for i in range(n_tensor - 1)]

        def hop(right, left, step):
            return (
                lax.ppermute(right, "tensor", steps[step:]),
                lax.ppermute(left, "tensor", back_steps[: len(steps) - step]),
            )

        block = width // 8

        class Part:
            def __init__(self, slots, *arrays):
                self.parts = [v[:, slots].reshape(2, 2, -1, *v.shape[2:]) for v in arrays]

            def total(self, *index):
                terms = [p[index].astype(F32) for p in self.parts]
                return functools.reduce(lambda u, v: u + v, terms).astype(BF)

            def take(self, got):
                self.parts = [p[0] for p in self.parts]
                self.parts.append(got.reshape(self.parts[0].shape))

            def totals(self):
                return [self.total(i) for i in range(self.parts[0].shape[0])]

        def pair_of(keep, got):
            count = keep.shape[1]
            return Part(slice(0, count // 2), keep, got), Part(slice(count // 2, count), keep, got)

        def plane(by_first, by_second):
            flying = []
            for move, group in ((by_x, by_first), (by_y, by_second)):
                sends = [p.total(1) for p in group]
                flat = jnp.concatenate([v.reshape(-1, *v.shape[-2:]) for v in sends])
                done(*order.last, flat)
                flying.append(move(flat))
            return flying

        def landed(flying, *groups):
            for flat, group in zip(flying, groups):
                first = 0
                for p in group:
                    size = math.prod(p.parts[0].shape[:-2]) // 2
                    p.take(flat[first : first + size])
                    first += size

        z_near = lambda v: swap(v, "tensor", n_tensor, 1)
        z_far = lambda v: swap(v, "tensor", n_tensor, 2)
        odd = (z & 1) == 1

        def after_near(values, got):
            first, second = jnp.where(odd, got[1], got[0]), jnp.where(odd, got[0], got[1])
            return values[0].astype(F32) + first.astype(F32), values[1].astype(F32) + second.astype(F32)

        def outer_rest(mine):
            bit = 2
            while bit < n_outer:
                mine = mine + swap(mine.astype(BF), "outer", n_outer, bit).astype(F32)
                bit *= 2
            return mine

        def whole_rows(mine, got):
            return ordered(mine, got.astype(F32), y, 0).reshape(2 * block, mine.shape[-1])

        out_1 = hop(output_own, output_own, 0)
        core1 = by_core(send1)
        qkv_both = ordered(e, e1, y, 0)
        qkv_core = by_core(qkv_both)
        qkv_parts = (flat_qkv, qkv_both, qkv_core)
        done(qkv_both, core1)
        h1 = pair_of(*hold((keep1, core1)))
        flight = plane([h1[0]], [h1[1]])
        made = back(
            at, hold(grad_r2), grad_r2_low, down_parts, slope, in_parts, norm_one, recip_one, gains, hidden_rel
        )
        made, qkv_core, out_1, flight = run((made, qkv_core, out_1, flight))
        qkv_parts = (flat_qkv, qkv_both, qkv_core)
        grad_binner, grad_r1, grad_r1_low, grad_r1_rel, vec_one, keep2, send2 = made
        out_2 = hop(*out_1, 1)
        core2 = by_core(send2)
        landed(flight, [h1[0]], [h1[1]])
        done(core2)
        h2 = pair_of(*hold((keep2, core2)))
        groups = [h2[0], h1[1]], [h2[1], h1[0]]
        flight = plane(*groups)
        two = n_tensor // 2
        made = attend_back(
            at, 0, tokens, hold(grad_r1_low), grad_r1, ctx[:two], qkv_parts, b_qv_all, heads, out_all, segments,
            tokens_rel, grad_r1_rel, F32,
        )
        made, out_2, flight = run((made, out_2, flight))
        bqv_a, tok_a, keep_a, send_a = made
        out_3 = hop(*out_2, 2)
        core_a = by_core(send_a)
        landed(flight, *groups)
        total1 = h1[0].totals() + h1[1].totals()
        near1 = z_near(jnp.stack([total1[1], total1[3]]))
        done(core_a)
        ha = pair_of(*hold((keep_a, core_a)))
        groups = [ha[0], h2[1]], [ha[1], h2[0]]
        flight = plane(*groups)
        made = attend_back(
            at, two, tokens, hold(grad_r1_low), tok_a, ctx[two:], qkv_parts, b_qv_all, heads, out_all, segments,
            tokens_rel, grad_r1_rel, BF,
        )
        made, out_3, flight, near1 = run((made, out_3, flight, near1))
        bqv_b, tok_own, keep_b, send_b = made
        tok_1 = hop(tok_own, tok_own, 0)
        core_b = by_core(send_b)
        landed(flight, *groups)

        grad_bqv = jnp.concatenate([bqv_a, bqv_b])
        slot_vec = [
            jnp.concatenate([grad_binner[s].reshape(-1, half), grad_bqv[s].reshape(-1, half)]) for s in range(n_tensor)
        ]
        common = jnp.concatenate([vec_one, vec_two]).reshape(-1, half)
        n_slot = slot_vec[0].shape[0]
        vec_got = z_near(jnp.concatenate([slot_vec[1], slot_vec[3], common]))
        done(core_b)
        hb = pair_of(*hold((keep_b, core_b)))
        groups = [hb[0], ha[1]], [hb[1], ha[0]]
        flight = plane(*groups)
        total2 = h2[0].totals() + h2[1].totals()
        near2 = jnp.stack([total2[1], total2[3]])
        mine1, far1 = after_near((total1[0], total1[2]), near1)
        far1 = far1.astype(BF)
        done(*order.last, near2, far1, *tok_1, *flight, vec_got)
        tok_1, flight, vec_got, near2, far1 = hold((tok_1, flight, vec_got, near2, far1))
        tok_2 = hop(*tok_1, 1)
        near2 = z_near(near2)
        landed(flight, *groups)
        groups = [hb[1]], [hb[0]]
        flight = plane(*groups)
        vec_got = vec_got[: 2 * n_slot].reshape(2, n_slot, half), vec_got[2 * n_slot :]
        vec_0, vec_2 = after_near((slot_vec[0], slot_vec[2]), vec_got[0])
        common = common + vec_got[1]
        vec_send = jnp.concatenate([vec_2, common])
        done(vec_send, *flight)
        landed(hold(flight), *groups)
        total3 = [t for part in (*ha, *hb) for t in part.totals()]
        near3 = z_near(jnp.stack([total3[1], total3[3]]))
        vec_got = z_far(hold(vec_send))
        done(*total3, near2)
        mine2, far2 = after_near((total2[0], total2[2]), hold(near2))
        far12 = jnp.stack([far1, far2.astype(BF)])
        done(far12, *tok_2)
        tok_2, far12 = hold((tok_2, far12))
        tok_3 = hop(*tok_2, 2)
        far12 = z_far(far12)
        grad_tokens = place(at, tok_own, (tok_1[0], tok_2[0], tok_2[0]), (tok_1[1], tok_2[1], tok_2[1]), F32)
        grad_tokens, near3 = run((grad_tokens, near3))
        mine3, far3 = after_near((total3[0], total3[2]), near3)
        far3 = z_far(far3.astype(BF))
        done(far12, far3)
        done(hold(far12))
        mine12 = outer_rest(jnp.stack([mine1, mine2]) + hold(far12).astype(F32))
        got12 = by_y(mine12.astype(BF))
        done(mine12)
        output = place(at, output_own, (out_1[0], out_2[0], out_3[0]), (out_1[1], out_2[1], hold(out_3[1])), BF)
        output = output.reshape(seq_count, seq_len, width)
        done(output, vec_got)
        vectors = jnp.concatenate([vec_0, common]) + hold(vec_got)
        vec_got = by_core(vectors)
        mine3 = outer_rest(mine3 + hold(far3).astype(F32))
        got3 = by_y(mine3.astype(BF))
        done(mine3, vec_got)
        vectors = vectors + hold(vec_got)
        vec_got = by_x(vectors)
        done(got12)
        got12 = hold(got12)
        done_wdown = whole_rows(mine12[0], got12[0])
        done_win = whole_rows(mine12[1], got12[1])
        done(done_wdown, done_win, got3, vec_got)
        got3, vec_got = hold((got3, vec_got))
        vectors = vectors + vec_got
        vec_got = by_y(vectors)
        done_last = whole_rows(mine3, got3)
        vectors = vectors + hold(vec_got)
        bit = 2
        while bit < n_outer:
            vectors = vectors + swap(vectors, "outer", n_outer, bit)
            bit *= 2
        slot_sum = vectors[:n_slot].reshape(-1)
        common = vectors[n_slot:].reshape(6, width)
        common = jnp.stack([common[i] for i in (0, 3, 1, 2, 4, 5)])
        part = lambda v, n: lax.dynamic_slice_in_dim(v, l_index * (n // n_local), n // n_local, v.ndim - 1)
        binner = part(slot_sum[:hidden_cols].reshape(b_inner.shape), head_size)
        bqv = part(slot_sum[hidden_cols:].reshape(b_qv.shape), head_size)
        common = part(common, width)
        grad_wqkv = done_last[:, : 3 * head_cols].reshape(width // n_local, 3, head_cols).transpose(1, 0, 2)
        done(grad_wqkv, common, binner, bqv, *tok_3)
        grad_tokens = place_end(at, *hold((tok_own, tok_3[0], tok_3[1], grad_tokens)))
        grad_tokens = grad_tokens.reshape(seq_count, seq_len, width)
        return (
            output,
            grad_tokens,
            grad_wqkv,
            bqv,
            done_last[:, 3 * head_cols :].T,
            done_win,
            binner,
            done_wdown.T,
            common[:2],
            common[2:],
        )

    return local


def solution(mesh):
    placed = (
        P(("outer", "local"), None, None),
        P(("outer", "local"), None),
        P(None, None, "tensor"),
        P(None, "tensor", None),
        P("tensor", None),
        P(None, "tensor"),
        P("tensor", None),
        P("tensor", None),
        P(),
        P(),
        P(("outer", "local"), None, None),
    )
    return jax.shard_map(
        make(dict(mesh.shape)),
        mesh=mesh,
        in_specs=placed,
        out_specs=(
            P(("outer", "local"), None, None),
            P(("outer", "local"), None, None),
            P(None, "local", "tensor"),
            P(None, "tensor", "local"),
            P("tensor", "local"),
            P("local", "tensor"),
            P("tensor", "local"),
            P("tensor", "local"),
            P(None, "local"),
            P(None, "local"),
        ),
        check_vma=False,
    )
```

```python
import functools
import math

import jax
import jax.numpy as jnp
from jax import lax
from jax.experimental import pallas as pl
from jax.experimental.pallas import tpu as pltpu
from jax.sharding import PartitionSpec as P

EPSILON = 1e-12
MASKED = -1e30
BF = jnp.bfloat16
F32 = jnp.float32
SHORT = pl.CostEstimate(flops=1000, bytes_accessed=1000, transcendentals=0)
ROOM = {'attend': 36, 'rise': 36, 'fall': 36, 'back': 36, 'attend_back': 48}
ROWS_BY_ROWS = (((1,), (1,)), ((), ()))


def dot(left, right):
    return jnp.dot(left, right, preferred_element_type=F32)


def dot_t(left, right):
    return lax.dot_general(left, right, ROWS_BY_ROWS, preferred_element_type=F32)


def normalize(values):
    centre = values - jnp.mean(values, axis=-1, keepdims=True)
    variance = jnp.mean(centre * centre, axis=-1, keepdims=True)
    recip = lax.rsqrt(variance + EPSILON)
    return (centre * recip, recip)


def norm_back(grad_norm, normed, recip):
    first = jnp.mean(grad_norm, axis=-1, keepdims=True)
    second = jnp.mean(grad_norm * normed, axis=-1, keepdims=True)
    return recip * (grad_norm - first - normed * second)


def col_sum(value):
    return jnp.sum(value, axis=0, keepdims=True)


def softmax_columns(raw, allowed):
    scores = jnp.where(allowed, raw, MASKED)
    grown = jnp.exp(scores - jnp.max(scores, axis=0, keepdims=True))
    return grown, 1.0 / jnp.sum(grown, axis=0, keepdims=True)


def column(row):
    return jnp.broadcast_to(row, (8, row.shape[1])).T[:, :1]


def store_relative(out_ref, value, at_ref):
    flipped = value.T.astype(BF)
    block = flipped.shape[0] // 8
    for i in range(8):
        spot = (((i >> 1) & 1) ^ at_ref[0]) * 4 + ((i >> 2) ^ at_ref[1]) * 2 + ((i & 1) ^ at_ref[2])
        out_ref[pl.ds(pl.multiple_of(spot * block, block), block)] = flipped[i * block : (i + 1) * block]


def call(kernel, name, at, grid, in_specs, out_specs, out_shape, scratch=()):
    return pl.pallas_call(
        kernel,
        grid_spec=pltpu.PrefetchScalarGridSpec(
            num_scalar_prefetch=1, grid=grid, in_specs=in_specs, out_specs=out_specs, scratch_shapes=list(scratch)
        ),
        out_shape=out_shape,
        cost_estimate=SHORT,
        compiler_params=pltpu.CompilerParams(vmem_limit_bytes=ROOM.get(name, 60) * 2**20),
        name=name,
    )


def const(*shape):
    return pl.BlockSpec(shape, lambda i, at: (0,) * len(shape))


def slot(*shape):
    return pl.BlockSpec((1, *shape), lambda i, at: (i,) + (0,) * len(shape))


def attend_kernel(heads, scale, at_ref, x_ref, w_ref, bias_ref, seg_ref, extra_ref, *refs):
    *out_refs, q_low, k_side, v_low, sum_ref = refs
    x = x_ref[0]
    size = w_ref.shape[1] // heads
    q_t = ((dot_t(w_ref[0], x) + column(bias_ref[0:1])).astype(BF) * scale).astype(BF)
    k = dot_t(x, w_ref[1]).astype(BF)
    v_t = (dot_t(w_ref[2], x) + column(bias_ref[1:2])).astype(BF)
    row = seg_ref[pl.ds(pl.program_id(0), 1)].astype(F32)
    allowed = column(row) == row
    q_low[...] = q_t.reshape(q_low.shape)
    v_low[...] = v_t.reshape(v_low.shape)
    for h in range(heads):
        k_side[h] = k[:, h * size : (h + 1) * size]

    def one_head(h, carry):
        grown, inv = softmax_columns(dot(k_side[h], q_low[h]), allowed)
        sum_ref[pl.ds(pl.multiple_of(h * size, size), size)] = dot(v_low[h], grown.astype(BF)) * inv
        return carry

    lax.fori_loop(0, heads, one_head, 0)
    context = sum_ref[...].T.astype(BF)
    count, rows, cols = len(out_refs), context.shape[0] // 2, context.shape[1]
    ahead = lax.rem(pl.program_id(0) + count - at_ref[3], count)
    for s, out_ref in enumerate(out_refs):
        @pl.when(ahead == s)
        def _():
            out_ref[:rows, :cols] = context[:rows]
            out_ref[:rows, cols:] = context[rows:]
            out_ref[rows:] = extra_ref[...]


def attend(at, tokens, w_rows, bias, segments, heads, extra):
    seqs, length, width = tokens.shape
    cols = w_rows.shape[1]
    return call(
        functools.partial(attend_kernel, heads, (cols // heads) ** -0.5), "attend", at, (seqs,),
        [slot(length, width), const(3, cols, width), const(2, cols), const(seqs, length), const(*extra.shape)],
        [const(length // 2 + extra.shape[0], 2 * cols)] * seqs,
        [jax.ShapeDtypeStruct((length // 2 + extra.shape[0], 2 * cols), BF)] * seqs,
        [
            pltpu.VMEM((heads, cols // heads, length), BF), pltpu.VMEM((heads, length, cols // heads), BF),
            pltpu.VMEM((heads, cols // heads, length), BF), pltpu.VMEM((cols, length), F32),
        ],
    )(at, tokens, w_rows, bias, segments, extra)


def fetch_copies(core, own_ref, mine_ref, theirs_ref, held, sems):
    slots = held.shape[0]
    copies = [[pltpu.make_async_copy(own_ref.at[c], held.at[0, c], sems.at[0, c]) for c in range(2)]]
    for s in range(1, slots):
        copies.append([
            pltpu.make_async_copy(mine_ref.at[:, s - 1], held.at[s, core], sems.at[s, 0]),
            pltpu.make_async_copy(theirs_ref.at[:, s - 1], held.at[s, 1 - core], sems.at[s, 1]),
        ])
    return copies


def fetch_slot(at_ref, refs, held, sems):
    step = pl.program_id(0)
    copies = fetch_copies(at_ref[0], *refs, held, sems)

    @pl.when(step == 0)
    def _():
        for pair in copies:
            for copy in pair:
                copy.start()

    for s, pair in enumerate(copies):
        @pl.when(step == s)
        def _():
            for copy in pair:
                copy.wait()

    return held[step].reshape(8 * held.shape[3], held.shape[4])


def pieces(weight):
    own, mine, theirs = weight
    piece = own.shape[0] // 8
    split = lambda v: v.reshape(4, -1, piece, own.shape[1])
    return own.reshape(2, 4, piece, own.shape[1]), split(mine), split(theirs)


def held_scratch(slots, weight):
    rows, width = weight[0].shape
    return [pltpu.VMEM((slots, 2, 4, rows // 8, width), BF), pltpu.SemaphoreType.DMA((slots, 2))]


def here(*shape):
    return pl.BlockSpec((1, *shape), lambda i, at: (at[3],) + (0,) * len(shape))


FAR = pl.BlockSpec(memory_space=pl.ANY)


def rise_kernel(slots, at_ref, *refs):
    ctx_refs = refs[:slots]
    (w_out_ref, x_ref, gains_ref, shifts_ref, own_ref, mine_ref, theirs_ref, bias_ref,
     hidden_ref, low_ref, norm_ref, recip_ref, act_ref, slope_ref, x_rel_ref, hidden_rel_ref, held, sems, ctx_ref) = refs[slots:]
    step = pl.program_id(0)
    weight = fetch_slot(at_ref, (own_ref, mine_ref, theirs_ref), held, sems)

    @pl.when(step == 0)
    def _():
        rows, cols = low_ref.shape[0] // 2, w_out_ref.shape[1]
        for s in range(slots):
            ctx_ref[:rows, s * cols : (s + 1) * cols] = ctx_refs[s][:rows, :cols]
            ctx_ref[rows:, s * cols : (s + 1) * cols] = ctx_refs[s][:rows, cols:]
        attention = dot(ctx_ref[...], w_out_ref[...].reshape(slots * cols, -1))
        own = x_ref[0].astype(F32)
        norm, recip = normalize(own + attention + shifts_ref[0:1])
        hidden = norm * gains_ref[0:1] + shifts_ref[1:2]
        norm_ref[...] = norm
        recip_ref[...] = recip
        hidden_ref[...] = hidden
        low_ref[...] = hidden.astype(BF)
        store_relative(x_rel_ref, own, at_ref)
        store_relative(hidden_rel_ref, hidden, at_ref)

    part = 256 if weight.shape[1] % 256 == 0 else weight.shape[1]
    spots = [slice(i, i + part) for i in range(0, weight.shape[1], part)]
    ready = dot(low_ref[...], weight[:, spots[0]])
    for i, cols in enumerate(spots):
        pre = ready + bias_ref[0, :, cols]
        if i + 1 < len(spots):
            ready = dot(low_ref[...], weight[:, spots[i + 1]])
        cumul = 0.5 * (1.0 + lax.erf(pre * (1.0 / math.sqrt(2.0))))
        slope = cumul + pre * jnp.exp(-0.5 * pre * pre) * (1.0 / math.sqrt(2.0 * math.pi))
        act_ref[0, :, cols] = (pre * cumul).astype(BF)
        slope_ref[0, :, cols] = slope.astype(BF)


def rise(at, ctx, w_out, x, gains, shifts, w_in, bias):
    slots, cols, rows = len(ctx), w_out.shape[1], x.shape[1]
    width, hidden = w_in[0].shape
    return call(
        functools.partial(rise_kernel, slots), "rise", at, (slots,),
        [const(*ctx[0].shape)] * slots
        + [
            const(slots, cols, width), here(rows, width), const(*gains.shape),
            const(*shifts.shape), FAR, FAR, FAR, slot(1, hidden),
        ],
        [
            const(rows, width), const(rows, width), const(rows, width), const(rows, 1),
            slot(rows, hidden), slot(rows, hidden), const(width, rows), const(width, rows),
        ],
        [
            jax.ShapeDtypeStruct((rows, width), F32),
            jax.ShapeDtypeStruct((rows, width), BF),
            jax.ShapeDtypeStruct((rows, width), F32),
            jax.ShapeDtypeStruct((rows, 1), F32),
            jax.ShapeDtypeStruct((slots, rows, hidden), BF),
            jax.ShapeDtypeStruct((slots, rows, hidden), BF),
            jax.ShapeDtypeStruct((width, rows), BF),
            jax.ShapeDtypeStruct((width, rows), BF),
        ],
        held_scratch(slots, w_in) + [pltpu.VMEM((rows, slots * cols), BF)],
    )(at, *ctx, w_out, x, gains, shifts, *pieces(w_in), bias[:, None, :])


def store_parts(keep_ref, send_ref, x_first, first, whole):
    block, last = keep_ref.shape[2], first + whole.shape[1]
    low = whole.astype(BF)
    for i in range(4):
        spot = jnp.where(x_first, i, 3 - i) if i in (1, 2) else i
        keep_ref[spot, 0, :, first:last] = low[i * block : (i + 1) * block]
        send_ref[spot, 0, :, first:last] = low[(4 + i) * block : (5 + i) * block]


def fall_kernel(slots, at_ref, act_ref, own_ref, mine_ref, theirs_ref, hidden_ref, cot_ref, gains_ref, shifts_ref,
                out_ref, grad_ref, low_ref, vec_ref, keep_ref, send_ref, sum_ref, rel_ref, held, sems):
    s = pl.program_id(0)
    copies = fetch_copies(at_ref[0], own_ref, mine_ref, theirs_ref, held, sems)

    @pl.when(s == 0)
    def _():
        for pair in copies:
            for copy in pair:
                copy.start()

    for i, pair in enumerate(copies):
        @pl.when(s == i)
        def _():
            for copy in pair:
                copy.wait()

    @pl.when(s == 0)
    def _():
        sum_ref[...] = jnp.zeros_like(sum_ref)

    @pl.when(s < slots)
    def _():
        sum_ref[...] += dot(act_ref[0], held[s].reshape(8 * held.shape[3], held.shape[4]))

    @pl.when(s == slots - 1)
    def _():
        norm, recip = normalize(hidden_ref[...] + sum_ref[...] + shifts_ref[2:3])
        out_ref[...] = (norm * gains_ref[1:2] + shifts_ref[3:4]).astype(BF)
        cot = cot_ref[0].astype(F32)
        grad = norm_back(cot * gains_ref[1:2], norm, recip)
        grad_ref[...] = grad
        low_ref[...] = grad.astype(BF)
        store_relative(rel_ref, grad, at_ref)
        vec_ref[0:1] = col_sum(cot * norm)
        vec_ref[1:2] = col_sum(grad)
        vec_ref[2:3] = col_sum(cot)

    @pl.when(s >= slots)
    def _():
        store_parts(keep_ref, send_ref, s - slots < slots // 2, 0, dot(rel_ref[...], act_ref[0]))


def part_specs(slots, block, cols, start=0):
    spec = pl.BlockSpec((4, 1, block, cols), lambda i, at: (0, lax.max(i - start, 0), 0, 0))
    return [spec] * 2, [jax.ShapeDtypeStruct((4, slots, block, cols), BF)] * 2


def fall(at, act, w_down, hidden, cot, gains, shifts):
    slots, rows, inner = act.shape
    width = w_down[0].shape[1]
    specs, shapes = part_specs(slots, width // 8, inner, slots)
    return call(
        functools.partial(fall_kernel, slots), "fall", at, (2 * slots,),
        [
            pl.BlockSpec((1, rows, inner), lambda i, at: (lax.rem(i, slots), 0, 0)), FAR, FAR, FAR, const(rows, width),
            here(rows, width), const(*gains.shape), const(*shifts.shape),
        ],
        [const(rows, width), const(rows, width), const(rows, width), const(3, width), *specs],
        [
            jax.ShapeDtypeStruct((rows, width), BF),
            jax.ShapeDtypeStruct((rows, width), F32),
            jax.ShapeDtypeStruct((rows, width), BF),
            jax.ShapeDtypeStruct((3, width), F32),
            *shapes,
        ],
        [pltpu.VMEM((rows, width), F32), pltpu.VMEM((width, rows), BF)] + held_scratch(slots, w_down),
    )(at, act, *pieces(w_down), hidden, cot, gains, shifts)


def back_kernel(slots, at_ref, grad2_ref, low2_ref, own2_ref, mine2_ref, theirs2_ref, slope_ref, own1_ref, mine1_ref,
                theirs1_ref, norm_ref, recip_ref, gains_ref, hidden_rel_ref, bias_ref, grad_ref, low_ref, rel_ref, vec_ref,
                keep_ref, send_ref, sum_ref, held2, sems2, held1, sems1):
    s = pl.program_id(0)
    w_down = fetch_slot(at_ref, (own2_ref, mine2_ref, theirs2_ref), held2, sems2)
    w_in = fetch_slot(at_ref, (own1_ref, mine1_ref, theirs1_ref), held1, sems1)
    pre = dot_t(low2_ref[...], w_down) * slope_ref[0].astype(F32)
    bias_ref[0] = col_sum(pre)
    pre_low = pre.astype(BF)
    store_parts(keep_ref, send_ref, s < slots // 2, 0, dot(hidden_rel_ref[...], pre_low))
    share = dot_t(pre_low, w_in)

    @pl.when(s == 0)
    def _():
        sum_ref[...] = share

    @pl.when(s > 0)
    def _():
        sum_ref[...] += share

    @pl.when(s == slots - 1)
    def _():
        norm = norm_ref[...]
        grad_h = grad2_ref[...] + sum_ref[...]
        grad = norm_back(grad_h * gains_ref[0:1], norm, recip_ref[...])
        grad_ref[...] = grad
        low_ref[...] = grad.astype(BF)
        store_relative(rel_ref, grad, at_ref)
        vec_ref[0:1] = col_sum(grad_h * norm)
        vec_ref[1:2] = col_sum(grad)
        vec_ref[2:3] = col_sum(grad_h)


def back(at, grad2, low2, w_down, slope, w_in, norm, recip, gains, hidden_rel):
    slots, rows, inner = slope.shape
    width = grad2.shape[1]
    specs, shapes = part_specs(slots, width // 8, inner)
    return call(
        functools.partial(back_kernel, slots), "back", at, (slots,),
        [
            const(rows, width), const(rows, width), FAR, FAR, FAR, slot(rows, inner), FAR, FAR, FAR,
            const(rows, width), const(rows, 1), const(*gains.shape), const(width, rows),
        ],
        [slot(1, inner), const(rows, width), const(rows, width), const(width, rows), const(3, width), *specs],
        [
            jax.ShapeDtypeStruct((slots, 1, inner), F32),
            jax.ShapeDtypeStruct((rows, width), F32),
            jax.ShapeDtypeStruct((rows, width), BF),
            jax.ShapeDtypeStruct((width, rows), BF),
            jax.ShapeDtypeStruct((3, width), F32),
            *shapes,
        ],
        [pltpu.VMEM((rows, width), F32)] + held_scratch(slots, w_down) + held_scratch(slots, w_in),
    )(at, grad2, low2, *pieces(w_down), slope, *pieces(w_in), norm, recip, gains, hidden_rel)


def attend_back_kernel(first, slots, heads, scale, at_ref, x_ref, low_ref, grad_ref, *refs):
    ctx_refs = refs[:slots]
    (own_ref, mine_ref, theirs_ref, bias_ref, w_out_ref, seg_ref, x_rel_ref, grad_rel_ref,
     vec_ref, tok_ref, keep_ref, send_ref, sum_ref, q_ref, k_ref, v_ref, ctx_ref, proj_ref, held, sems) = refs[slots:]
    s = pl.program_id(0)
    half = mine_ref.shape[-1]
    mine_at = pl.ds(pl.multiple_of(at_ref[0] * half, half), half)
    theirs_at = pl.ds(pl.multiple_of((1 - at_ref[0]) * half, half), half)
    copies = []
    for i in range(slots):
        if first + i == 0:
            copies.append([
                pltpu.make_async_copy(own_ref.at[:2], held.at[i, :2], sems.at[i, 0]),
                pltpu.make_async_copy(own_ref.at[2:], held.at[i, 2:], sems.at[i, 1]),
            ])
        else:
            copies.append([
                pltpu.make_async_copy(mine_ref.at[:, first + i - 1], held.at[i, :, :, mine_at], sems.at[i, 0]),
                pltpu.make_async_copy(theirs_ref.at[:, first + i - 1], held.at[i, :, :, theirs_at], sems.at[i, 1]),
            ])

    @pl.when(s == 0)
    def _():
        for pair in copies:
            for copy in pair:
                copy.start()

    for i, pair in enumerate(copies):
        @pl.when(s == i)
        def _():
            for copy in pair:
                copy.wait()
            rows, cols = ctx_ref.shape[0] // 2, ctx_ref.shape[1]
            ctx_ref[:rows] = ctx_refs[i][:rows, :cols]
            ctx_ref[rows:] = ctx_refs[i][:rows, cols:]

    x, low = x_ref[0], low_ref[...]
    cols = w_out_ref.shape[1]
    size = cols // heads
    weight = held[s].reshape(3, cols, x.shape[1])
    q_t = (dot_t(weight[0], x) + column(bias_ref[0, 0:1])).astype(BF)
    q_scaled = (q_t * scale).astype(BF)
    q = q_t.T
    k_t = dot_t(weight[1], x).astype(BF)
    k = k_t.T
    v = (dot_t(x, weight[2]) + bias_ref[0, 1:2]).astype(BF)
    gc_t = dot_t(w_out_ref[0], low).astype(BF)
    gc = gc_t.T
    row = seg_ref[pl.ds(at_ref[3], 1)].astype(F32)
    allowed = column(row) == row
    spot = lambda h: slice(h * size, (h + 1) * size)
    first_of = lambda h: (dot(k[:, spot(h)], q_scaled[spot(h)]), dot(v[:, spot(h)], gc_t[spot(h)]))
    ready = first_of(0)
    for h in range(heads):
        at = spot(h)
        raw, grad_probs = ready
        if h + 1 < heads:
            ready = first_of(h + 1)
        if h == 0:
            whole = dot(grad_rel_ref[...], ctx_ref[...])
            store_parts(keep_ref, send_ref, s < slots // 2, proj_ref.shape[1], whole)
        grown, inv = softmax_columns(raw, allowed)
        probs = grown * inv
        inner = jnp.sum(probs * grad_probs, axis=0, keepdims=True)
        grad_scores = (probs * (grad_probs - inner) * scale).astype(BF)
        v_ref[:, at] = dot(probs.astype(BF), gc[:, at])
        q_ref[at] = dot(k_t[at], grad_scores)
        k_ref[:, at] = dot(grad_scores, q[:, at])
    grad_q = q_ref[...].T
    grad_v = v_ref[...]
    vec_ref[0, 0:1] = col_sum(grad_q)
    vec_ref[0, 1:2] = col_sum(grad_v)
    parts = [grad_q.astype(BF), k_ref[...].astype(BF), grad_v.astype(BF)]
    for c in range(3):
        proj_ref[:, c * cols : (c + 1) * cols] = parts[c]
    proj = proj_ref[...]
    share = dot(proj, weight.reshape(3 * cols, x.shape[1]))
    store_parts(keep_ref, send_ref, s < slots // 2, 0, dot(x_rel_ref[...], proj))

    @pl.when(s == 0)
    def _():
        sum_ref[...] = share + grad_ref[...]

    @pl.when(s > 0)
    def _():
        sum_ref[...] += share

    @pl.when(s == slots - 1)
    def _():
        tok_ref[...] = sum_ref[...].astype(tok_ref.dtype)


def attend_back(at, first, x, low, grad, ctx, w_qkv, bias, heads, w_out, segments, x_rel, grad_rel, kind):
    slots, cols = len(ctx), w_out.shape[1]
    rows, width = x.shape[1:]
    own, mine, theirs = w_qkv
    piece, half = mine.shape[-2:]
    split = lambda v: v.reshape(4, -1, piece, half)
    later = lambda *shape: pl.BlockSpec((1, *shape), lambda i, at: (i + first,) + (0,) * len(shape))
    specs, shapes = part_specs(slots, width // 8, 4 * cols)
    return call(
        functools.partial(attend_back_kernel, first, slots, heads, (cols // heads) ** -0.5), "attend_back", at, (slots,),
        [here(rows, width), const(rows, width), const(rows, width)]
        + [const(*ctx[0].shape)] * slots
        + [
            FAR, FAR, FAR, later(2, cols), later(cols, width), const(*segments.shape), const(width, rows), const(width, rows),
        ],
        [slot(2, cols), const(rows, width), *specs],
        [
            jax.ShapeDtypeStruct((slots, 2, cols), F32),
            jax.ShapeDtypeStruct((rows, width), kind),
            *shapes,
        ],
        [
            pltpu.VMEM((rows, width), F32), pltpu.VMEM((cols, rows), F32), pltpu.VMEM((rows, cols), F32),
            pltpu.VMEM((rows, cols), F32), pltpu.VMEM((rows, cols), BF), pltpu.VMEM((rows, 3 * cols), BF),
            pltpu.VMEM((slots, 4, piece, width), BF), pltpu.SemaphoreType.DMA((slots, 2)),
        ],
    )(at, x, low, grad, *ctx, own.reshape(4, piece, width), split(mine), split(theirs), bias, w_out, segments, x_rel, grad_rel)


def place_kernel(slots, at_ref, *refs):
    sources, (out_ref, held, sems) = refs[:-3], refs[-3:]
    here = at_ref[3]
    end = (here == 0) | (here == slots - 1)
    far = jnp.where(here < 2, slots - 1, 0)

    def each(step, act):
        wanted = (
            step == here,
            step == here + 1 - 2 * lax.rem(here, 2),
            (step == slots - 1 - here) & (here > 0) & (here < slots - 1),
            (step == far) & (here > 0) & (here < slots - 1),
            (step == jnp.where(here == 0, 2, 1)) & end,
            (step == slots - 1 - here) & end,
        )
        for source, now in zip(sources, wanted):
            @pl.when(now)
            def _():
                act(pltpu.make_async_copy(source, held.at[step], sems.at[step]))

    step = pl.program_id(0)

    @pl.when(step == 0)
    def _():
        for j in range(slots):
            each(j, lambda copy: copy.start())

    pltpu.make_async_copy(sources[0], held.at[step], sems.at[step]).wait()
    out_ref[0] = held[step].astype(out_ref.dtype)


def place_end_kernel(slots, at_ref, own_ref, last_ref, whole_ref, out_ref, held, sem):
    here = at_ref[3]
    end = (here == 0) | (here == slots - 1)
    for source, wanted in ((last_ref, end), (own_ref, jnp.logical_not(end))):
        @pl.when(wanted)
        def _():
            copy = pltpu.make_async_copy(source, held, sem)
            copy.start()
            copy.wait()

    out_ref[0] = held[...].astype(out_ref.dtype)


def place_end(at, own, last, whole):
    slots = whole.shape[0]
    spot = lambda i, at: (jnp.where(at[3] == 0, slots - 1, jnp.where(at[3] == slots - 1, 0, at[3])), 0, 0)
    return pl.pallas_call(
        functools.partial(place_end_kernel, slots),
        grid_spec=pltpu.PrefetchScalarGridSpec(
            num_scalar_prefetch=1, grid=(1,), in_specs=[FAR] * 3, out_specs=pl.BlockSpec((1, *own.shape), spot),
            scratch_shapes=[pltpu.VMEM(own.shape, own.dtype), pltpu.SemaphoreType.DMA],
        ),
        out_shape=jax.ShapeDtypeStruct(whole.shape, whole.dtype),
        input_output_aliases={3: 0},
        cost_estimate=SHORT,
        name="place_end",
    )(at, own, last, whole)


def place(at, slots, values, kind):
    own = values[0]
    return call(
        functools.partial(place_kernel, slots), "place", at, (slots,),
        [FAR] * len(values), slot(*own.shape),
        jax.ShapeDtypeStruct((slots, *own.shape), kind),
        [pltpu.VMEM((slots, *own.shape), own.dtype), pltpu.SemaphoreType.DMA((slots,))],
    )(at, *values)


def swap(value, axis, size, bit):
    return lax.ppermute(value, axis, [(i, i ^ bit) for i in range(size)])


def ordered(own, got, bit, axis):
    first = jnp.where(bit == 0, own, got)
    second = jnp.where(bit == 0, got, own)
    return jnp.stack([first, second], axis)


def in_three(value):
    high = value.astype(BF)
    rest = value - high.astype(F32)
    middle = rest.astype(BF)
    return jnp.stack([high, middle, (rest - middle.astype(F32)).astype(BF)])


class Order:
    def __init__(self):
        self.last = ()

    def hold(self, values, *waits):
        leaves, tree = jax.tree.flatten(values)
        held = lax.optimization_barrier((leaves, self.last, waits))[0]
        return jax.tree.unflatten(tree, held)

    def done(self, *values):
        self.last = tuple(values)

    def run(self, made, *waits):
        self.last = waits
        made = self.hold(made)
        self.last = tuple(jax.tree.leaves(made)[:1])
        return made


def make(sizes):
    n_outer, n_local, n_tensor = sizes["outer"], sizes["local"], sizes["tensor"]

    def local(tokens, segments, w_qkv, b_qv, w_out, w_in, b_inner, w_down, gains, shifts, cotangent):
        seq_count, seq_len, width = tokens.shape
        heads, head_size = b_qv.shape[1], b_qv.shape[2]
        head_cols = heads * head_size
        hidden_cols = w_in.shape[1]
        z = lax.axis_index("tensor")
        l_index = lax.axis_index("local")
        core, x = l_index & 1, l_index >> 1
        y = lax.axis_index("outer") & 1
        z_from = lambda s: jnp.mod(z - s, n_tensor)
        z_to = lambda s: jnp.mod(z + s, n_tensor)
        cyclic = lambda v, s: lax.ppermute(v, "tensor", [(i, (i + s) % n_tensor) for i in range(n_tensor)])
        pick = lambda v, i: lax.dynamic_index_in_dim(v, i, 0, keepdims=False)
        others = range(1, n_tensor)
        by_x = lambda v: swap(v, "local", n_local, 2)
        by_y = lambda v: swap(v, "outer", n_outer, 1)
        by_core = lambda v: swap(v, "local", n_local, 1)
        at = jnp.stack([core, x, y, z]).astype(jnp.int32)
        order = Order()
        hold, done, run = order.hold, order.done, order.run

        place8 = core * 4 + y * 2 + x
        half = width // 2

        def piece_of(weight):
            n = weight.shape[0] // 8
            return lax.dynamic_slice_in_dim(weight, place8 * n, n, 0)

        def halves(parts, rows):
            return jnp.stack([p[rows, :half] for p in parts]), jnp.stack([p[rows, half:] for p in parts])

        def plane_two(a, b, a1, b1):
            return ordered(a, a1, x, 0), ordered(b, b1, y, 0)

        def plane_three(a, b, a1, b1, rows):
            a, a1, b, b1 = (v[:, :, rows] for v in (a, a1, b, b1))
            return jnp.concatenate([ordered(a, a1, y, 0), ordered(b, b1, x, 1)], -1)

        qkv_rows = w_qkv.transpose(0, 2, 1)
        flat_qkv = qkv_rows.reshape(3 * head_cols, width)

        first = jnp.concatenate([piece_of(w_out), piece_of(w_in), piece_of(w_down)])
        first_z = [cyclic(first, s) for s in others]
        done(first)
        biases = jnp.concatenate([b_inner.reshape(-1), b_qv.reshape(-1)])
        bias_rows = -(-biases.size // half)
        bias_pack = in_three(jnp.pad(hold(biases), (0, bias_rows * half - biases.size)).reshape(bias_rows, half))
        bias_pack = jnp.pad(bias_pack.reshape(3 * bias_rows, half), ((0, -3 * bias_rows % 16), (0, 0)))

        context = attend(at, hold(tokens), qkv_rows, b_qv.reshape(2, head_cols), segments, heads, bias_pack)
        (ctx_own, *ctx_send), first_z = run((context, first_z))
        ctx_z = [cyclic(v, s) for v, s in zip(ctx_send, others)]
        cut, end = w_out.shape[0] // 8, (w_out.shape[0] + w_in.shape[0]) // 8
        a, b = halves(first_z, slice(0, end))
        a1, b1 = by_x(a), by_y(b)
        c, d = halves(first_z, slice(end, None))
        piece_qkv = lax.dynamic_slice(
            hold(flat_qkv), ((y * 2 + x) * (flat_qkv.shape[0] // 4), core * half), (flat_qkv.shape[0] // 4, half)
        )
        done(c, d, piece_qkv, a1, b1)
        a, b = plane_two(*hold((a, b, a1, b1)))
        a1, b1 = by_y(a), by_x(b)
        done(a, b, *ctx_z)
        ctx_z = hold(ctx_z)
        c1, d1 = by_x(hold(c)), by_y(hold(d))
        top = seq_len // 2
        bias_got = jnp.stack([p[top : top + 3 * bias_rows] for p in ctx_z]).astype(F32)
        bias_got = bias_got.reshape(n_tensor - 1, 3, bias_rows * half)
        bias_got = bias_got[:, 0] + bias_got[:, 1] + bias_got[:, 2]
        bias_all = jnp.concatenate([biases[None], bias_got[:, : biases.size]])
        b_inner_all = bias_all[:, :hidden_cols]
        b_qv_all = bias_all[:, hidden_cols:].reshape(n_tensor, 2, head_cols)
        done(b_inner_all, a1, b1)
        a, b, a1, b1, piece_qkv = hold((a, b, a1, b1, piece_qkv))
        third_z = [cyclic(piece_qkv, s) for s in others]
        in_both = plane_three(a, b, a1, b1, slice(cut, None))
        out_both = plane_three(a, b, a1, b1, slice(0, cut))
        done(in_both, out_both, b_inner_all, c1, d1)
        in_both, out_both, c, d, c1, d1 = hold((in_both, out_both, c, d, c1, d1))
        in_core, out_core = by_core(in_both), by_core(out_both)
        c, d = plane_two(c, d, c1, d1)
        done(c, d, in_core, out_core)
        c1, d1 = by_y(hold(c)), by_x(hold(d))
        out_got = ordered(*hold((out_both, out_core)), core, 0).transpose(3, 0, 1, 2, 4, 5)
        out_all = jnp.concatenate([w_out[None], out_got.reshape(n_tensor - 1, *w_out.shape)])
        in_parts = (w_in, in_both, in_core)
        done(out_all, *third_z)
        e = jnp.stack(hold(third_z))
        e1 = by_x(e)
        done(e)
        ctx = [ctx_own, *ctx_z]
        made = rise(at, hold(ctx), out_all, tokens, gains, shifts, in_parts, b_inner_all)
        made, c1, d1, e1 = run((made, c1, d1, e1))
        hidden1, hidden_low, norm_one, recip_one, activation, slope, tokens_rel, hidden_rel = made
        down_both = plane_three(c, d, c1, d1, slice(None))
        down_core = by_core(down_both)
        e = ordered(e, e1, x, 0)
        e1 = by_y(e)
        done(down_both, down_core, e)
        down_parts = (w_down, down_both, down_core)
        made = fall(at, hold(activation), down_parts, hidden1, cotangent, gains, shifts)
        made, e1 = run((made, e1))
        output_own, grad_r2, grad_r2_low, vec_two, keep1, send1 = made

        across = lambda v: swap(v, "tensor", n_tensor, 1)
        middle = lambda v: lax.ppermute(v, "tensor", [(1, 2), (2, 1)])
        outward = lambda v: lax.ppermute(v, "tensor", [(1, 0), (2, 3)])

        def hop_one(own):
            return across(own), middle(own)

        def hop_two(partner, other):
            return middle(partner), outward(other)

        def hop_three(passed, _):
            return (outward(passed),)

        block = width // 8

        class Part:
            def __init__(self, slots, *arrays):
                self.parts = [v[:, slots].reshape(2, 2, -1, *v.shape[2:]) for v in arrays]

            def total(self, *index):
                terms = [p[index].astype(F32) for p in self.parts]
                return functools.reduce(lambda u, v: u + v, terms).astype(BF)

            def take(self, got):
                self.parts = [p[0] for p in self.parts]
                self.parts.append(got.reshape(self.parts[0].shape))

            def totals(self):
                return [self.total(i) for i in range(self.parts[0].shape[0])]

        def pair_of(keep, got):
            count = keep.shape[1]
            return Part(slice(0, count // 2), keep, got), Part(slice(count // 2, count), keep, got)

        def plane(by_first, by_second):
            flying = []
            for move, group in ((by_x, by_first), (by_y, by_second)):
                sends = [p.total(1) for p in group]
                flat = jnp.concatenate([v.reshape(-1, *v.shape[-2:]) for v in sends])
                done(*order.last, flat)
                flying.append(move(flat))
            return flying

        def landed(flying, *groups):
            for flat, group in zip(flying, groups):
                first = 0
                for p in group:
                    size = math.prod(p.parts[0].shape[:-2]) // 2
                    p.take(flat[first : first + size])
                    first += size

        z_near = lambda v: swap(v, "tensor", n_tensor, 1)
        z_far = lambda v: swap(v, "tensor", n_tensor, 2)
        odd = (z & 1) == 1

        def after_near(values, got):
            first, second = jnp.where(odd, got[1], got[0]), jnp.where(odd, got[0], got[1])
            return values[0].astype(F32) + first.astype(F32), values[1].astype(F32) + second.astype(F32)

        def outer_rest(mine):
            bit = 2
            while bit < n_outer:
                mine = mine + swap(mine.astype(BF), "outer", n_outer, bit).astype(F32)
                bit *= 2
            return mine

        def whole_rows(mine, got):
            return ordered(mine, got.astype(F32), y, 0).reshape(2 * block, mine.shape[-1])

        out_1 = hop_one(output_own)
        core1 = by_core(send1)
        qkv_both = ordered(e, e1, y, 0)
        qkv_core = by_core(qkv_both)
        qkv_parts = (flat_qkv, qkv_both, qkv_core)
        done(qkv_both, core1)
        h1 = pair_of(*hold((keep1, core1)))
        flight = plane([h1[0]], [h1[1]])
        made = back(
            at, hold(grad_r2), grad_r2_low, down_parts, slope, in_parts, norm_one, recip_one, gains, hidden_rel
        )
        made, qkv_core, out_1, flight = run((made, qkv_core, out_1, flight))
        qkv_parts = (flat_qkv, qkv_both, qkv_core)
        grad_binner, grad_r1, grad_r1_low, grad_r1_rel, vec_one, keep2, send2 = made
        out_2 = hop_two(*out_1)
        core2 = by_core(send2)
        landed(flight, [h1[0]], [h1[1]])
        done(core2)
        h2 = pair_of(*hold((keep2, core2)))
        groups = [h2[0], h1[1]], [h2[1], h1[0]]
        flight = plane(*groups)
        two = n_tensor // 2
        made = attend_back(
            at, 0, tokens, hold(grad_r1_low), grad_r1, ctx[:two], qkv_parts, b_qv_all, heads, out_all, segments,
            tokens_rel, grad_r1_rel, F32,
        )
        made, out_2, flight = run((made, out_2, flight))
        bqv_a, tok_a, keep_a, send_a = made
        out_3 = hop_three(*out_2)
        core_a = by_core(send_a)
        landed(flight, *groups)
        total1 = h1[0].totals() + h1[1].totals()
        near1 = z_near(jnp.stack([total1[1], total1[3]]))
        done(core_a)
        ha = pair_of(*hold((keep_a, core_a)))
        groups = [ha[0], h2[1]], [ha[1], h2[0]]
        flight = plane(*groups)
        made = attend_back(
            at, two, tokens, hold(grad_r1_low), tok_a, ctx[two:], qkv_parts, b_qv_all, heads, out_all, segments,
            tokens_rel, grad_r1_rel, BF,
        )
        made, out_3, flight, near1 = run((made, out_3, flight, near1))
        bqv_b, tok_own, keep_b, send_b = made
        tok_1 = hop_one(tok_own)
        core_b = by_core(send_b)
        landed(flight, *groups)

        grad_bqv = jnp.concatenate([bqv_a, bqv_b])
        slot_vec = [
            jnp.concatenate([grad_binner[s].reshape(-1, half), grad_bqv[s].reshape(-1, half)]) for s in range(n_tensor)
        ]
        common = jnp.concatenate([vec_one, vec_two]).reshape(-1, half)
        n_slot = slot_vec[0].shape[0]
        vec_got = z_near(jnp.concatenate([slot_vec[1], slot_vec[3], common]))
        done(core_b)
        hb = pair_of(*hold((keep_b, core_b)))
        groups = [hb[0], ha[1]], [hb[1], ha[0]]
        flight = plane(*groups)
        total2 = h2[0].totals() + h2[1].totals()
        near2 = jnp.stack([total2[1], total2[3]])
        mine1, far1 = after_near((total1[0], total1[2]), near1)
        far1 = far1.astype(BF)
        done(*order.last, near2, far1, *tok_1, *flight, vec_got)
        tok_1, flight, vec_got, near2, far1 = hold((tok_1, flight, vec_got, near2, far1))
        tok_2 = hop_two(*tok_1)
        near2 = z_near(near2)
        landed(flight, *groups)
        groups = [hb[1]], [hb[0]]
        flight = plane(*groups)
        vec_got = vec_got[: 2 * n_slot].reshape(2, n_slot, half), vec_got[2 * n_slot :]
        vec_0, vec_2 = after_near((slot_vec[0], slot_vec[2]), vec_got[0])
        common = common + vec_got[1]
        vec_send = jnp.concatenate([vec_2, common])
        done(vec_send, *flight)
        landed(hold(flight), *groups)
        total3 = [t for part in (*ha, *hb) for t in part.totals()]
        near3 = z_near(jnp.stack([total3[1], total3[3]]))
        vec_got = z_far(hold(vec_send))
        done(*total3, near2)
        mine2, far2 = after_near((total2[0], total2[2]), hold(near2))
        far12 = jnp.stack([far1, far2.astype(BF)])
        done(far12, *tok_2)
        tok_2, far12 = hold((tok_2, far12))
        tok_3 = hop_three(*tok_2)
        far12 = z_far(far12)
        grad_tokens = place(at, n_tensor, (tok_own, *tok_1, *tok_2, tok_2[0]), F32)
        grad_tokens, near3 = run((grad_tokens, near3))
        mine3, far3 = after_near((total3[0], total3[2]), near3)
        far3 = z_far(far3.astype(BF))
        done(far12, far3)
        done(hold(far12))
        mine12 = outer_rest(jnp.stack([mine1, mine2]) + hold(far12).astype(F32))
        got12 = by_y(mine12.astype(BF))
        done(mine12)
        output = place(at, n_tensor, (output_own, *out_1, *out_2, hold(out_3[0])), BF)
        output = output.reshape(seq_count, seq_len, width)
        done(output, vec_got)
        vectors = jnp.concatenate([vec_0, common]) + hold(vec_got)
        vec_got = by_core(vectors)
        mine3 = outer_rest(mine3 + hold(far3).astype(F32))
        got3 = by_y(mine3.astype(BF))
        done(mine3, vec_got)
        vectors = vectors + hold(vec_got)
        vec_got = by_x(vectors)
        done(got12)
        got12 = hold(got12)
        done_wdown = whole_rows(mine12[0], got12[0])
        done_win = whole_rows(mine12[1], got12[1])
        done(done_wdown, done_win, got3, vec_got)
        got3, vec_got = hold((got3, vec_got))
        vectors = vectors + vec_got
        vec_got = by_y(vectors)
        done_last = whole_rows(mine3, got3)
        vectors = vectors + hold(vec_got)
        bit = 2
        while bit < n_outer:
            vectors = vectors + swap(vectors, "outer", n_outer, bit)
            bit *= 2
        slot_sum = vectors[:n_slot].reshape(-1)
        common = vectors[n_slot:].reshape(6, width)
        common = jnp.stack([common[i] for i in (0, 3, 1, 2, 4, 5)])
        part = lambda v, n: lax.dynamic_slice_in_dim(v, l_index * (n // n_local), n // n_local, v.ndim - 1)
        binner = part(slot_sum[:hidden_cols].reshape(b_inner.shape), head_size)
        bqv = part(slot_sum[hidden_cols:].reshape(b_qv.shape), head_size)
        common = part(common, width)
        grad_wqkv = done_last[:, : 3 * head_cols].reshape(width // n_local, 3, head_cols).transpose(1, 0, 2)
        done(grad_wqkv, common, binner, bqv, *tok_3)
        grad_tokens = place_end(at, *hold((tok_own, tok_3[0], grad_tokens)))
        grad_tokens = grad_tokens.reshape(seq_count, seq_len, width)
        return (
            output,
            grad_tokens,
            grad_wqkv,
            bqv,
            done_last[:, 3 * head_cols :].T,
            done_win,
            binner,
            done_wdown.T,
            common[:2],
            common[2:],
        )

    return local


def solution(mesh):
    placed = (
        P(("outer", "local"), None, None),
        P(("outer", "local"), None),
        P(None, None, "tensor"),
        P(None, "tensor", None),
        P("tensor", None),
        P(None, "tensor"),
        P("tensor", None),
        P("tensor", None),
        P(),
        P(),
        P(("outer", "local"), None, None),
    )
    return jax.shard_map(
        make(dict(mesh.shape)),
        mesh=mesh,
        in_specs=placed,
        out_specs=(
            P(("outer", "local"), None, None),
            P(("outer", "local"), None, None),
            P(None, "local", "tensor"),
            P(None, "tensor", "local"),
            P("tensor", "local"),
            P("local", "tensor"),
            P("tensor", "local"),
            P("tensor", "local"),
            P(None, "local"),
            P(None, "local"),
        ),
        check_vma=False,
    )
```

```python
import functools
import math

import jax
import jax.numpy as jnp
from jax import lax
from jax.experimental import pallas as pl
from jax.experimental.pallas import tpu as pltpu
from jax.sharding import PartitionSpec as P

EPSILON = 1e-12
MASKED = -1e30
BF = jnp.bfloat16
F32 = jnp.float32
SHORT = pl.CostEstimate(flops=1000, bytes_accessed=1000, transcendentals=0)
ROOM = {'attend': 36, 'rise': 36, 'fall': 36, 'back': 36, 'attend_back': 48}
ROWS_BY_ROWS = (((1,), (1,)), ((), ()))


def dot(left, right):
    return jnp.dot(left, right, preferred_element_type=F32)


def dot_t(left, right):
    return lax.dot_general(left, right, ROWS_BY_ROWS, preferred_element_type=F32)


def normalize(values):
    centre = values - jnp.mean(values, axis=-1, keepdims=True)
    variance = jnp.mean(centre * centre, axis=-1, keepdims=True)
    recip = lax.rsqrt(variance + EPSILON)
    return (centre * recip, recip)


def norm_back(grad_norm, normed, recip):
    first = jnp.mean(grad_norm, axis=-1, keepdims=True)
    second = jnp.mean(grad_norm * normed, axis=-1, keepdims=True)
    return recip * (grad_norm - first - normed * second)


def col_sum(value):
    return jnp.sum(value, axis=0, keepdims=True)


def softmax_columns(raw, allowed):
    scores = jnp.where(allowed, raw, MASKED)
    grown = jnp.exp(scores - jnp.max(scores, axis=0, keepdims=True))
    return grown, 1.0 / jnp.sum(grown, axis=0, keepdims=True)


def column(row):
    return jnp.broadcast_to(row, (8, row.shape[1])).T[:, :1]


def store_relative(out_ref, value, at_ref):
    flipped = value.T.astype(BF)
    block = flipped.shape[0] // 8
    for i in range(8):
        spot = (((i >> 1) & 1) ^ at_ref[0]) * 4 + ((i >> 2) ^ at_ref[1]) * 2 + ((i & 1) ^ at_ref[2])
        out_ref[pl.ds(pl.multiple_of(spot * block, block), block)] = flipped[i * block : (i + 1) * block]


def call(kernel, name, at, grid, in_specs, out_specs, out_shape, scratch=()):
    return pl.pallas_call(
        kernel,
        grid_spec=pltpu.PrefetchScalarGridSpec(
            num_scalar_prefetch=1, grid=grid, in_specs=in_specs, out_specs=out_specs, scratch_shapes=list(scratch)
        ),
        out_shape=out_shape,
        cost_estimate=SHORT,
        compiler_params=pltpu.CompilerParams(vmem_limit_bytes=ROOM.get(name, 60) * 2**20),
        name=name,
    )


def const(*shape):
    return pl.BlockSpec(shape, lambda i, at: (0,) * len(shape))


def slot(*shape):
    return pl.BlockSpec((1, *shape), lambda i, at: (i,) + (0,) * len(shape))


def attend_kernel(heads, scale, at_ref, x_ref, w_ref, bias_ref, seg_ref, extra_ref, *refs):
    *out_refs, q_low, k_side, v_low, sum_ref = refs
    x = x_ref[0]
    size = w_ref.shape[1] // heads
    q_t = ((dot_t(w_ref[0], x) + column(bias_ref[0:1])).astype(BF) * scale).astype(BF)
    k = dot_t(x, w_ref[1]).astype(BF)
    v_t = (dot_t(w_ref[2], x) + column(bias_ref[1:2])).astype(BF)
    row = seg_ref[pl.ds(pl.program_id(0), 1)].astype(F32)
    allowed = column(row) == row
    q_low[...] = q_t.reshape(q_low.shape)
    v_low[...] = v_t.reshape(v_low.shape)
    for h in range(heads):
        k_side[h] = k[:, h * size : (h + 1) * size]

    def one_head(h, carry):
        grown, inv = softmax_columns(dot(k_side[h], q_low[h]), allowed)
        sum_ref[pl.ds(pl.multiple_of(h * size, size), size)] = dot(v_low[h], grown.astype(BF)) * inv
        return carry

    lax.fori_loop(0, heads, one_head, 0)
    context = sum_ref[...].T.astype(BF)
    count, rows, cols = len(out_refs), context.shape[0] // 2, context.shape[1]
    ahead = pl.program_id(0) ^ at_ref[3]
    for s, out_ref in enumerate(out_refs):
        @pl.when(ahead == s)
        def _():
            out_ref[:rows, :cols] = context[:rows]
            out_ref[:rows, cols:] = context[rows:]
            out_ref[rows:] = extra_ref[...]


def attend(at, tokens, w_rows, bias, segments, heads, extra):
    seqs, length, width = tokens.shape
    cols = w_rows.shape[1]
    return call(
        functools.partial(attend_kernel, heads, (cols // heads) ** -0.5), "attend", at, (seqs,),
        [slot(length, width), const(3, cols, width), const(2, cols), const(seqs, length), const(*extra.shape)],
        [const(length // 2 + extra.shape[0], 2 * cols)] * seqs,
        [jax.ShapeDtypeStruct((length // 2 + extra.shape[0], 2 * cols), BF)] * seqs,
        [
            pltpu.VMEM((heads, cols // heads, length), BF), pltpu.VMEM((heads, length, cols // heads), BF),
            pltpu.VMEM((heads, cols // heads, length), BF), pltpu.VMEM((cols, length), F32),
        ],
    )(at, tokens, w_rows, bias, segments, extra)


def fetch_copies(core, own_ref, mine_ref, theirs_ref, held, sems):
    slots = held.shape[0]
    copies = [[pltpu.make_async_copy(own_ref.at[c], held.at[0, c], sems.at[0, c]) for c in range(2)]]
    for s in range(1, slots):
        copies.append([
            pltpu.make_async_copy(mine_ref.at[:, s - 1], held.at[s, core], sems.at[s, 0]),
            pltpu.make_async_copy(theirs_ref.at[:, s - 1], held.at[s, 1 - core], sems.at[s, 1]),
        ])
    return copies


def fetch_slot(at_ref, refs, held, sems):
    step = pl.program_id(0)
    copies = fetch_copies(at_ref[0], *refs, held, sems)

    @pl.when(step == 0)
    def _():
        for pair in copies:
            for copy in pair:
                copy.start()

    for s, pair in enumerate(copies):
        @pl.when(step == s)
        def _():
            for copy in pair:
                copy.wait()

    return held[step].reshape(8 * held.shape[3], held.shape[4])


def pieces(weight):
    own, mine, theirs = weight
    piece = own.shape[0] // 8
    split = lambda v: v.reshape(4, -1, piece, own.shape[1])
    return own.reshape(2, 4, piece, own.shape[1]), split(mine), split(theirs)


def held_scratch(slots, weight):
    rows, width = weight[0].shape
    return [pltpu.VMEM((slots, 2, 4, rows // 8, width), BF), pltpu.SemaphoreType.DMA((slots, 2))]


def here(*shape):
    return pl.BlockSpec((1, *shape), lambda i, at: (at[3],) + (0,) * len(shape))


FAR = pl.BlockSpec(memory_space=pl.ANY)


def rise_kernel(slots, at_ref, *refs):
    ctx_refs = refs[:slots]
    (w_out_ref, x_ref, gains_ref, shifts_ref, own_ref, mine_ref, theirs_ref, bias_ref,
     hidden_ref, low_ref, norm_ref, recip_ref, act_ref, slope_ref, x_rel_ref, hidden_rel_ref, held, sems, ctx_ref) = refs[slots:]
    step = pl.program_id(0)
    weight = fetch_slot(at_ref, (own_ref, mine_ref, theirs_ref), held, sems)

    @pl.when(step == 0)
    def _():
        rows, cols = low_ref.shape[0] // 2, w_out_ref.shape[1]
        for s in range(slots):
            ctx_ref[:rows, s * cols : (s + 1) * cols] = ctx_refs[s][:rows, :cols]
            ctx_ref[rows:, s * cols : (s + 1) * cols] = ctx_refs[s][:rows, cols:]
        attention = dot(ctx_ref[...], w_out_ref[...].reshape(slots * cols, -1))
        own = x_ref[0].astype(F32)
        norm, recip = normalize(own + attention + shifts_ref[0:1])
        hidden = norm * gains_ref[0:1] + shifts_ref[1:2]
        norm_ref[...] = norm
        recip_ref[...] = recip
        hidden_ref[...] = hidden
        low_ref[...] = hidden.astype(BF)
        store_relative(x_rel_ref, own, at_ref)
        store_relative(hidden_rel_ref, hidden, at_ref)

    part = 256 if weight.shape[1] % 256 == 0 else weight.shape[1]
    spots = [slice(i, i + part) for i in range(0, weight.shape[1], part)]
    ready = dot(low_ref[...], weight[:, spots[0]])
    for i, cols in enumerate(spots):
        pre = ready + bias_ref[0, :, cols]
        if i + 1 < len(spots):
            ready = dot(low_ref[...], weight[:, spots[i + 1]])
        cumul = 0.5 * (1.0 + lax.erf(pre * (1.0 / math.sqrt(2.0))))
        slope = cumul + pre * jnp.exp(-0.5 * pre * pre) * (1.0 / math.sqrt(2.0 * math.pi))
        act_ref[0, :, cols] = (pre * cumul).astype(BF)
        slope_ref[0, :, cols] = slope.astype(BF)


def rise(at, ctx, w_out, x, gains, shifts, w_in, bias):
    slots, cols, rows = len(ctx), w_out.shape[1], x.shape[1]
    width, hidden = w_in[0].shape
    return call(
        functools.partial(rise_kernel, slots), "rise", at, (slots,),
        [const(*ctx[0].shape)] * slots
        + [
            const(slots, cols, width), here(rows, width), const(*gains.shape),
            const(*shifts.shape), FAR, FAR, FAR, slot(1, hidden),
        ],
        [
            const(rows, width), const(rows, width), const(rows, width), const(rows, 1),
            slot(rows, hidden), slot(rows, hidden), const(width, rows), const(width, rows),
        ],
        [
            jax.ShapeDtypeStruct((rows, width), F32),
            jax.ShapeDtypeStruct((rows, width), BF),
            jax.ShapeDtypeStruct((rows, width), F32),
            jax.ShapeDtypeStruct((rows, 1), F32),
            jax.ShapeDtypeStruct((slots, rows, hidden), BF),
            jax.ShapeDtypeStruct((slots, rows, hidden), BF),
            jax.ShapeDtypeStruct((width, rows), BF),
            jax.ShapeDtypeStruct((width, rows), BF),
        ],
        held_scratch(slots, w_in) + [pltpu.VMEM((rows, slots * cols), BF)],
    )(at, *ctx, w_out, x, gains, shifts, *pieces(w_in), bias[:, None, :])


def store_parts(keep_ref, send_ref, x_first, first, whole):
    block, last = keep_ref.shape[2], first + whole.shape[1]
    low = whole.astype(BF)
    for i in range(4):
        spot = jnp.where(x_first, i, 3 - i) if i in (1, 2) else i
        keep_ref[spot, 0, :, first:last] = low[i * block : (i + 1) * block]
        send_ref[spot, 0, :, first:last] = low[(4 + i) * block : (5 + i) * block]


def fall_kernel(slots, at_ref, act_ref, own_ref, mine_ref, theirs_ref, hidden_ref, cot_ref, gains_ref, shifts_ref,
                out_ref, grad_ref, low_ref, vec_ref, keep_ref, send_ref, sum_ref, rel_ref, held, sems):
    s = pl.program_id(0)
    copies = fetch_copies(at_ref[0], own_ref, mine_ref, theirs_ref, held, sems)

    @pl.when(s == 0)
    def _():
        for pair in copies:
            for copy in pair:
                copy.start()

    for i, pair in enumerate(copies):
        @pl.when(s == i)
        def _():
            for copy in pair:
                copy.wait()

    @pl.when(s == 0)
    def _():
        sum_ref[...] = jnp.zeros_like(sum_ref)

    @pl.when(s < slots)
    def _():
        sum_ref[...] += dot(act_ref[0], held[s].reshape(8 * held.shape[3], held.shape[4]))

    @pl.when(s == slots - 1)
    def _():
        norm, recip = normalize(hidden_ref[...] + sum_ref[...] + shifts_ref[2:3])
        out_ref[...] = (norm * gains_ref[1:2] + shifts_ref[3:4]).astype(BF)
        cot = cot_ref[0].astype(F32)
        grad = norm_back(cot * gains_ref[1:2], norm, recip)
        grad_ref[...] = grad
        low_ref[...] = grad.astype(BF)
        store_relative(rel_ref, grad, at_ref)
        vec_ref[0:1] = col_sum(cot * norm)
        vec_ref[1:2] = col_sum(grad)
        vec_ref[2:3] = col_sum(cot)

    @pl.when(s >= slots)
    def _():
        store_parts(keep_ref, send_ref, s - slots < slots // 2, 0, dot(rel_ref[...], act_ref[0]))


def part_specs(slots, block, cols, start=0):
    spec = pl.BlockSpec((4, 1, block, cols), lambda i, at: (0, lax.max(i - start, 0), 0, 0))
    return [spec] * 2, [jax.ShapeDtypeStruct((4, slots, block, cols), BF)] * 2


def fall(at, act, w_down, hidden, cot, gains, shifts):
    slots, rows, inner = act.shape
    width = w_down[0].shape[1]
    specs, shapes = part_specs(slots, width // 8, inner, slots)
    return call(
        functools.partial(fall_kernel, slots), "fall", at, (2 * slots,),
        [
            pl.BlockSpec((1, rows, inner), lambda i, at: (lax.rem(i, slots), 0, 0)), FAR, FAR, FAR, const(rows, width),
            here(rows, width), const(*gains.shape), const(*shifts.shape),
        ],
        [const(rows, width), const(rows, width), const(rows, width), const(3, width), *specs],
        [
            jax.ShapeDtypeStruct((rows, width), BF),
            jax.ShapeDtypeStruct((rows, width), F32),
            jax.ShapeDtypeStruct((rows, width), BF),
            jax.ShapeDtypeStruct((3, width), F32),
            *shapes,
        ],
        [pltpu.VMEM((rows, width), F32), pltpu.VMEM((width, rows), BF)] + held_scratch(slots, w_down),
    )(at, act, *pieces(w_down), hidden, cot, gains, shifts)


def back_kernel(slots, at_ref, grad2_ref, low2_ref, own2_ref, mine2_ref, theirs2_ref, slope_ref, own1_ref, mine1_ref,
                theirs1_ref, norm_ref, recip_ref, gains_ref, hidden_rel_ref, bias_ref, grad_ref, low_ref, rel_ref, vec_ref,
                keep_ref, send_ref, sum_ref, held2, sems2, held1, sems1):
    s = pl.program_id(0)
    w_down = fetch_slot(at_ref, (own2_ref, mine2_ref, theirs2_ref), held2, sems2)
    w_in = fetch_slot(at_ref, (own1_ref, mine1_ref, theirs1_ref), held1, sems1)
    pre = dot_t(low2_ref[...], w_down) * slope_ref[0].astype(F32)
    bias_ref[0] = col_sum(pre)
    pre_low = pre.astype(BF)
    store_parts(keep_ref, send_ref, s < slots // 2, 0, dot(hidden_rel_ref[...], pre_low))
    share = dot_t(pre_low, w_in)

    @pl.when(s == 0)
    def _():
        sum_ref[...] = share

    @pl.when(s > 0)
    def _():
        sum_ref[...] += share

    @pl.when(s == slots - 1)
    def _():
        norm = norm_ref[...]
        grad_h = grad2_ref[...] + sum_ref[...]
        grad = norm_back(grad_h * gains_ref[0:1], norm, recip_ref[...])
        grad_ref[...] = grad
        low_ref[...] = grad.astype(BF)
        store_relative(rel_ref, grad, at_ref)
        vec_ref[0:1] = col_sum(grad_h * norm)
        vec_ref[1:2] = col_sum(grad)
        vec_ref[2:3] = col_sum(grad_h)


def back(at, grad2, low2, w_down, slope, w_in, norm, recip, gains, hidden_rel):
    slots, rows, inner = slope.shape
    width = grad2.shape[1]
    specs, shapes = part_specs(slots, width // 8, inner)
    return call(
        functools.partial(back_kernel, slots), "back", at, (slots,),
        [
            const(rows, width), const(rows, width), FAR, FAR, FAR, slot(rows, inner), FAR, FAR, FAR,
            const(rows, width), const(rows, 1), const(*gains.shape), const(width, rows),
        ],
        [slot(1, inner), const(rows, width), const(rows, width), const(width, rows), const(3, width), *specs],
        [
            jax.ShapeDtypeStruct((slots, 1, inner), F32),
            jax.ShapeDtypeStruct((rows, width), F32),
            jax.ShapeDtypeStruct((rows, width), BF),
            jax.ShapeDtypeStruct((width, rows), BF),
            jax.ShapeDtypeStruct((3, width), F32),
            *shapes,
        ],
        [pltpu.VMEM((rows, width), F32)] + held_scratch(slots, w_down) + held_scratch(slots, w_in),
    )(at, grad2, low2, *pieces(w_down), slope, *pieces(w_in), norm, recip, gains, hidden_rel)


def attend_back_kernel(first, slots, heads, scale, at_ref, x_ref, low_ref, grad_ref, *refs):
    ctx_refs = refs[:slots]
    (own_ref, mine_ref, theirs_ref, bias_ref, w_out_ref, seg_ref, x_rel_ref, grad_rel_ref,
     vec_ref, tok_ref, keep_ref, send_ref, sum_ref, q_ref, k_ref, v_ref, ctx_ref, proj_ref, held, sems) = refs[slots:]
    s = pl.program_id(0)
    half = mine_ref.shape[-1]
    mine_at = pl.ds(pl.multiple_of(at_ref[0] * half, half), half)
    theirs_at = pl.ds(pl.multiple_of((1 - at_ref[0]) * half, half), half)
    copies = []
    for i in range(slots):
        if first + i == 0:
            copies.append([
                pltpu.make_async_copy(own_ref.at[:2], held.at[i, :2], sems.at[i, 0]),
                pltpu.make_async_copy(own_ref.at[2:], held.at[i, 2:], sems.at[i, 1]),
            ])
        else:
            copies.append([
                pltpu.make_async_copy(mine_ref.at[:, first + i - 1], held.at[i, :, :, mine_at], sems.at[i, 0]),
                pltpu.make_async_copy(theirs_ref.at[:, first + i - 1], held.at[i, :, :, theirs_at], sems.at[i, 1]),
            ])

    @pl.when(s == 0)
    def _():
        for pair in copies:
            for copy in pair:
                copy.start()

    for i, pair in enumerate(copies):
        @pl.when(s == i)
        def _():
            for copy in pair:
                copy.wait()
            rows, cols = ctx_ref.shape[0] // 2, ctx_ref.shape[1]
            ctx_ref[:rows] = ctx_refs[i][:rows, :cols]
            ctx_ref[rows:] = ctx_refs[i][:rows, cols:]

    x, low = x_ref[0], low_ref[...]
    cols = w_out_ref.shape[1]
    size = cols // heads
    weight = held[s].reshape(3, cols, x.shape[1])
    q_t = (dot_t(weight[0], x) + column(bias_ref[0, 0:1])).astype(BF)
    q_scaled = (q_t * scale).astype(BF)
    q = q_t.T
    k_t = dot_t(weight[1], x).astype(BF)
    k = k_t.T
    v = (dot_t(x, weight[2]) + bias_ref[0, 1:2]).astype(BF)
    gc_t = dot_t(w_out_ref[0], low).astype(BF)
    gc = gc_t.T
    row = seg_ref[pl.ds(at_ref[3], 1)].astype(F32)
    allowed = column(row) == row
    spot = lambda h: slice(h * size, (h + 1) * size)
    first_of = lambda h: (dot(k[:, spot(h)], q_scaled[spot(h)]), dot(v[:, spot(h)], gc_t[spot(h)]))
    ready = first_of(0)
    for h in range(heads):
        at = spot(h)
        raw, grad_probs = ready
        if h + 1 < heads:
            ready = first_of(h + 1)
        if h == 0:
            whole = dot(grad_rel_ref[...], ctx_ref[...])
            store_parts(keep_ref, send_ref, s < slots // 2, proj_ref.shape[1], whole)
        grown, inv = softmax_columns(raw, allowed)
        probs = grown * inv
        inner = jnp.sum(probs * grad_probs, axis=0, keepdims=True)
        grad_scores = (probs * (grad_probs - inner) * scale).astype(BF)
        v_ref[:, at] = dot(probs.astype(BF), gc[:, at])
        q_ref[at] = dot(k_t[at], grad_scores)
        k_ref[:, at] = dot(grad_scores, q[:, at])
    grad_q = q_ref[...].T
    grad_v = v_ref[...]
    vec_ref[0, 0:1] = col_sum(grad_q)
    vec_ref[0, 1:2] = col_sum(grad_v)
    parts = [grad_q.astype(BF), k_ref[...].astype(BF), grad_v.astype(BF)]
    for c in range(3):
        proj_ref[:, c * cols : (c + 1) * cols] = parts[c]
    proj = proj_ref[...]
    share = dot(proj, weight.reshape(3 * cols, x.shape[1]))
    store_parts(keep_ref, send_ref, s < slots // 2, 0, dot(x_rel_ref[...], proj))

    @pl.when(s == 0)
    def _():
        sum_ref[...] = share + grad_ref[...]

    @pl.when(s > 0)
    def _():
        sum_ref[...] += share

    @pl.when(s == slots - 1)
    def _():
        tok_ref[...] = sum_ref[...].astype(tok_ref.dtype)


def attend_back(at, first, x, low, grad, ctx, w_qkv, bias, heads, w_out, segments, x_rel, grad_rel, kind):
    slots, cols = len(ctx), w_out.shape[1]
    rows, width = x.shape[1:]
    own, mine, theirs = w_qkv
    piece, half = mine.shape[-2:]
    split = lambda v: v.reshape(4, -1, piece, half)
    later = lambda *shape: pl.BlockSpec((1, *shape), lambda i, at: (i + first,) + (0,) * len(shape))
    specs, shapes = part_specs(slots, width // 8, 4 * cols)
    return call(
        functools.partial(attend_back_kernel, first, slots, heads, (cols // heads) ** -0.5), "attend_back", at, (slots,),
        [here(rows, width), const(rows, width), const(rows, width)]
        + [const(*ctx[0].shape)] * slots
        + [
            FAR, FAR, FAR, later(2, cols), later(cols, width), const(*segments.shape), const(width, rows), const(width, rows),
        ],
        [slot(2, cols), const(rows, width), *specs],
        [
            jax.ShapeDtypeStruct((slots, 2, cols), F32),
            jax.ShapeDtypeStruct((rows, width), kind),
            *shapes,
        ],
        [
            pltpu.VMEM((rows, width), F32), pltpu.VMEM((cols, rows), F32), pltpu.VMEM((rows, cols), F32),
            pltpu.VMEM((rows, cols), F32), pltpu.VMEM((rows, cols), BF), pltpu.VMEM((rows, 3 * cols), BF),
            pltpu.VMEM((slots, 4, piece, width), BF), pltpu.SemaphoreType.DMA((slots, 2)),
        ],
    )(at, x, low, grad, *ctx, own.reshape(4, piece, width), split(mine), split(theirs), bias, w_out, segments, x_rel, grad_rel)


def place_kernel(slots, at_ref, *refs):
    sources, (out_ref, held, sems) = refs[:-3], refs[-3:]
    here = at_ref[3]
    end = (here == 0) | (here == slots - 1)
    far = jnp.where(here < 2, slots - 1, 0)

    def each(step, act):
        wanted = (
            step == here,
            step == here + 1 - 2 * lax.rem(here, 2),
            (step == slots - 1 - here) & (here > 0) & (here < slots - 1),
            (step == far) & (here > 0) & (here < slots - 1),
            (step == jnp.where(here == 0, 2, 1)) & end,
            (step == slots - 1 - here) & end,
        )
        for source, now in zip(sources, wanted):
            @pl.when(now)
            def _():
                act(pltpu.make_async_copy(source, held.at[step], sems.at[step]))

    step = pl.program_id(0)

    @pl.when(step == 0)
    def _():
        for j in range(slots):
            each(j, lambda copy: copy.start())

    pltpu.make_async_copy(sources[0], held.at[step], sems.at[step]).wait()
    out_ref[0] = held[step].astype(out_ref.dtype)


def place_end_kernel(slots, at_ref, own_ref, last_ref, whole_ref, out_ref, held, sem):
    here = at_ref[3]
    end = (here == 0) | (here == slots - 1)
    for source, wanted in ((last_ref, end), (own_ref, jnp.logical_not(end))):
        @pl.when(wanted)
        def _():
            copy = pltpu.make_async_copy(source, held, sem)
            copy.start()
            copy.wait()

    out_ref[0] = held[...].astype(out_ref.dtype)


def place_end(at, own, last, whole):
    slots = whole.shape[0]
    spot = lambda i, at: (jnp.where(at[3] == 0, slots - 1, jnp.where(at[3] == slots - 1, 0, at[3])), 0, 0)
    return pl.pallas_call(
        functools.partial(place_end_kernel, slots),
        grid_spec=pltpu.PrefetchScalarGridSpec(
            num_scalar_prefetch=1, grid=(1,), in_specs=[FAR] * 3, out_specs=pl.BlockSpec((1, *own.shape), spot),
            scratch_shapes=[pltpu.VMEM(own.shape, own.dtype), pltpu.SemaphoreType.DMA],
        ),
        out_shape=jax.ShapeDtypeStruct(whole.shape, whole.dtype),
        input_output_aliases={3: 0},
        cost_estimate=SHORT,
        name="place_end",
    )(at, own, last, whole)


def place(at, slots, values, kind):
    own = values[0]
    return call(
        functools.partial(place_kernel, slots), "place", at, (slots,),
        [FAR] * len(values), slot(*own.shape),
        jax.ShapeDtypeStruct((slots, *own.shape), kind),
        [pltpu.VMEM((slots, *own.shape), own.dtype), pltpu.SemaphoreType.DMA((slots,))],
    )(at, *values)


def swap(value, axis, size, bit):
    return lax.ppermute(value, axis, [(i, i ^ bit) for i in range(size)])


def ordered(own, got, bit, axis):
    first = jnp.where(bit == 0, own, got)
    second = jnp.where(bit == 0, got, own)
    return jnp.stack([first, second], axis)


def in_three(value):
    high = value.astype(BF)
    rest = value - high.astype(F32)
    middle = rest.astype(BF)
    return jnp.stack([high, middle, (rest - middle.astype(F32)).astype(BF)])


class Order:
    def __init__(self):
        self.last = ()

    def hold(self, values, *waits):
        leaves, tree = jax.tree.flatten(values)
        held = lax.optimization_barrier((leaves, self.last, waits))[0]
        return jax.tree.unflatten(tree, held)

    def done(self, *values):
        self.last = tuple(values)

    def run(self, made, *waits):
        self.last = waits
        made = self.hold(made)
        self.last = tuple(jax.tree.leaves(made)[:1])
        return made


def make(sizes):
    n_outer, n_local, n_tensor = sizes["outer"], sizes["local"], sizes["tensor"]

    def local(tokens, segments, w_qkv, b_qv, w_out, w_in, b_inner, w_down, gains, shifts, cotangent):
        seq_count, seq_len, width = tokens.shape
        heads, head_size = b_qv.shape[1], b_qv.shape[2]
        head_cols = heads * head_size
        hidden_cols = w_in.shape[1]
        z = lax.axis_index("tensor")
        l_index = lax.axis_index("local")
        core, x = l_index & 1, l_index >> 1
        y = lax.axis_index("outer") & 1
        other = lambda v, s: swap(v, "tensor", n_tensor, s)
        pick = lambda v, i: lax.dynamic_index_in_dim(v, i, 0, keepdims=False)
        others = range(1, n_tensor)
        by_x = lambda v: swap(v, "local", n_local, 2)
        by_y = lambda v: swap(v, "outer", n_outer, 1)
        by_core = lambda v: swap(v, "local", n_local, 1)
        at = jnp.stack([core, x, y, z]).astype(jnp.int32)
        order = Order()
        hold, done, run = order.hold, order.done, order.run

        place8 = core * 4 + y * 2 + x
        half = width // 2

        def piece_of(weight):
            n = weight.shape[0] // 8
            return lax.dynamic_slice_in_dim(weight, place8 * n, n, 0)

        def halves(parts, rows):
            return jnp.stack([p[rows, :half] for p in parts]), jnp.stack([p[rows, half:] for p in parts])

        def plane_two(a, b, a1, b1):
            return ordered(a, a1, x, 0), ordered(b, b1, y, 0)

        def plane_three(a, b, a1, b1, rows):
            a, a1, b, b1 = (v[:, :, rows] for v in (a, a1, b, b1))
            return jnp.concatenate([ordered(a, a1, y, 0), ordered(b, b1, x, 1)], -1)

        qkv_rows = w_qkv.transpose(0, 2, 1)
        flat_qkv = qkv_rows.reshape(3 * head_cols, width)

        first = jnp.concatenate([piece_of(w_out), piece_of(w_in), piece_of(w_down)])
        first_z = [other(first, s) for s in others]
        done(first)
        biases = jnp.concatenate([b_inner.reshape(-1), b_qv.reshape(-1)])
        bias_rows = -(-biases.size // half)
        bias_pack = in_three(jnp.pad(hold(biases), (0, bias_rows * half - biases.size)).reshape(bias_rows, half))
        bias_pack = jnp.pad(bias_pack.reshape(3 * bias_rows, half), ((0, -3 * bias_rows % 16), (0, 0)))

        context = attend(at, hold(tokens), qkv_rows, b_qv.reshape(2, head_cols), segments, heads, bias_pack)
        (ctx_own, *ctx_send), first_z = run((context, first_z))
        ctx_z = [other(v, s) for v, s in zip(ctx_send, others)]
        cut, end = w_out.shape[0] // 8, (w_out.shape[0] + w_in.shape[0]) // 8
        a, b = halves(first_z, slice(0, end))
        a1, b1 = by_x(a), by_y(b)
        c, d = halves(first_z, slice(end, None))
        piece_qkv = lax.dynamic_slice(
            hold(flat_qkv), ((y * 2 + x) * (flat_qkv.shape[0] // 4), core * half), (flat_qkv.shape[0] // 4, half)
        )
        done(c, d, piece_qkv, a1, b1)
        a, b = plane_two(*hold((a, b, a1, b1)))
        a1, b1 = by_y(a), by_x(b)
        done(a, b, *ctx_z)
        ctx_z = hold(ctx_z)
        c1, d1 = by_x(hold(c)), by_y(hold(d))
        top = seq_len // 2
        bias_got = jnp.stack([p[top : top + 3 * bias_rows] for p in ctx_z]).astype(F32)
        bias_got = bias_got.reshape(n_tensor - 1, 3, bias_rows * half)
        bias_got = bias_got[:, 0] + bias_got[:, 1] + bias_got[:, 2]
        bias_all = jnp.concatenate([biases[None], bias_got[:, : biases.size]])
        b_inner_all = bias_all[:, :hidden_cols]
        b_qv_all = bias_all[:, hidden_cols:].reshape(n_tensor, 2, head_cols)
        done(b_inner_all, a1, b1)
        a, b, a1, b1, piece_qkv = hold((a, b, a1, b1, piece_qkv))
        third_z = [other(piece_qkv, s) for s in others]
        in_both = plane_three(a, b, a1, b1, slice(cut, None))
        out_both = plane_three(a, b, a1, b1, slice(0, cut))
        done(in_both, out_both, b_inner_all, c1, d1)
        in_both, out_both, c, d, c1, d1 = hold((in_both, out_both, c, d, c1, d1))
        in_core, out_core = by_core(in_both), by_core(out_both)
        c, d = plane_two(c, d, c1, d1)
        done(c, d, in_core, out_core)
        c1, d1 = by_y(hold(c)), by_x(hold(d))
        out_got = ordered(*hold((out_both, out_core)), core, 0).transpose(3, 0, 1, 2, 4, 5)
        out_all = jnp.concatenate([w_out[None], out_got.reshape(n_tensor - 1, *w_out.shape)])
        in_parts = (w_in, in_both, in_core)
        done(out_all, *third_z)
        e = jnp.stack(hold(third_z))
        e1 = by_x(e)
        done(e)
        ctx = [ctx_own, *ctx_z]
        made = rise(at, hold(ctx), out_all, tokens, gains, shifts, in_parts, b_inner_all)
        made, c1, d1, e1 = run((made, c1, d1, e1))
        hidden1, hidden_low, norm_one, recip_one, activation, slope, tokens_rel, hidden_rel = made
        down_both = plane_three(c, d, c1, d1, slice(None))
        down_core = by_core(down_both)
        e = ordered(e, e1, x, 0)
        e1 = by_y(e)
        done(down_both, down_core, e)
        down_parts = (w_down, down_both, down_core)
        made = fall(at, hold(activation), down_parts, hidden1, cotangent, gains, shifts)
        made, e1 = run((made, e1))
        output_own, grad_r2, grad_r2_low, vec_two, keep1, send1 = made

        across = lambda v: swap(v, "tensor", n_tensor, 1)
        middle = lambda v: lax.ppermute(v, "tensor", [(1, 2), (2, 1)])
        outward = lambda v: lax.ppermute(v, "tensor", [(1, 0), (2, 3)])

        def hop_one(own):
            return across(own), middle(own)

        def hop_two(partner, other):
            return middle(partner), outward(other)

        def hop_three(passed, _):
            return (outward(passed),)

        block = width // 8

        class Part:
            def __init__(self, slots, *arrays):
                self.parts = [v[:, slots].reshape(2, 2, -1, *v.shape[2:]) for v in arrays]

            def total(self, *index):
                terms = [p[index].astype(F32) for p in self.parts]
                return functools.reduce(lambda u, v: u + v, terms).astype(BF)

            def take(self, got):
                self.parts = [p[0] for p in self.parts]
                self.parts.append(got.reshape(self.parts[0].shape))

            def totals(self):
                return [self.total(i) for i in range(self.parts[0].shape[0])]

        def pair_of(keep, got):
            count = keep.shape[1]
            return Part(slice(0, count // 2), keep, got), Part(slice(count // 2, count), keep, got)

        def plane(by_first, by_second):
            flying = []
            for move, group in ((by_x, by_first), (by_y, by_second)):
                sends = [p.total(1) for p in group]
                flat = jnp.concatenate([v.reshape(-1, *v.shape[-2:]) for v in sends])
                done(*order.last, flat)
                flying.append(move(flat))
            return flying

        def landed(flying, *groups):
            for flat, group in zip(flying, groups):
                first = 0
                for p in group:
                    size = math.prod(p.parts[0].shape[:-2]) // 2
                    p.take(flat[first : first + size])
                    first += size

        z_near = lambda v: swap(v, "tensor", n_tensor, 1)
        z_far = lambda v: swap(v, "tensor", n_tensor, 2)

        def after_near(values, got):
            return values[0].astype(F32) + got[0].astype(F32), values[1].astype(F32) + got[1].astype(F32)

        def outer_rest(mine):
            bit = 2
            while bit < n_outer:
                mine = mine + swap(mine.astype(BF), "outer", n_outer, bit).astype(F32)
                bit *= 2
            return mine

        def whole_rows(mine, got):
            return ordered(mine, got.astype(F32), y, 0).reshape(2 * block, mine.shape[-1])

        out_1 = hop_one(output_own)
        core1 = by_core(send1)
        qkv_both = ordered(e, e1, y, 0)
        qkv_core = by_core(qkv_both)
        qkv_parts = (flat_qkv, qkv_both, qkv_core)
        done(qkv_both, core1)
        h1 = pair_of(*hold((keep1, core1)))
        flight = plane([h1[0]], [h1[1]])
        made = back(
            at, hold(grad_r2), grad_r2_low, down_parts, slope, in_parts, norm_one, recip_one, gains, hidden_rel
        )
        made, qkv_core, out_1, flight = run((made, qkv_core, out_1, flight))
        qkv_parts = (flat_qkv, qkv_both, qkv_core)
        grad_binner, grad_r1, grad_r1_low, grad_r1_rel, vec_one, keep2, send2 = made
        out_2 = hop_two(*out_1)
        core2 = by_core(send2)
        landed(flight, [h1[0]], [h1[1]])
        done(core2)
        h2 = pair_of(*hold((keep2, core2)))
        groups = [h2[0], h1[1]], [h2[1], h1[0]]
        flight = plane(*groups)
        two = n_tensor // 2
        made = attend_back(
            at, 0, tokens, hold(grad_r1_low), grad_r1, ctx[:two], qkv_parts, b_qv_all, heads, out_all, segments,
            tokens_rel, grad_r1_rel, F32,
        )
        made, out_2, flight = run((made, out_2, flight))
        bqv_a, tok_a, keep_a, send_a = made
        out_3 = hop_three(*out_2)
        core_a = by_core(send_a)
        landed(flight, *groups)
        total1 = h1[0].totals() + h1[1].totals()
        near1 = z_near(jnp.stack([total1[1], total1[3]]))
        done(core_a)
        ha = pair_of(*hold((keep_a, core_a)))
        groups = [ha[0], h2[1]], [ha[1], h2[0]]
        flight = plane(*groups)
        made = attend_back(
            at, two, tokens, hold(grad_r1_low), tok_a, ctx[two:], qkv_parts, b_qv_all, heads, out_all, segments,
            tokens_rel, grad_r1_rel, BF,
        )
        made, out_3, flight, near1 = run((made, out_3, flight, near1))
        bqv_b, tok_own, keep_b, send_b = made
        tok_1 = hop_one(tok_own)
        core_b = by_core(send_b)
        landed(flight, *groups)

        grad_bqv = jnp.concatenate([bqv_a, bqv_b])
        slot_vec = [
            jnp.concatenate([grad_binner[s].reshape(-1, half), grad_bqv[s].reshape(-1, half)]) for s in range(n_tensor)
        ]
        common = jnp.concatenate([vec_one, vec_two]).reshape(-1, half)
        n_slot = slot_vec[0].shape[0]
        vec_got = z_near(jnp.concatenate([slot_vec[1], slot_vec[3], common]))
        done(core_b)
        hb = pair_of(*hold((keep_b, core_b)))
        groups = [hb[0], ha[1]], [hb[1], ha[0]]
        flight = plane(*groups)
        total2 = h2[0].totals() + h2[1].totals()
        near2 = jnp.stack([total2[1], total2[3]])
        mine1, far1 = after_near((total1[0], total1[2]), near1)
        far1 = far1.astype(BF)
        done(*order.last, near2, far1, *tok_1, *flight, vec_got)
        tok_1, flight, vec_got, near2, far1 = hold((tok_1, flight, vec_got, near2, far1))
        tok_2 = hop_two(*tok_1)
        near2 = z_near(near2)
        landed(flight, *groups)
        groups = [hb[1]], [hb[0]]
        flight = plane(*groups)
        vec_got = vec_got[: 2 * n_slot].reshape(2, n_slot, half), vec_got[2 * n_slot :]
        vec_0, vec_2 = after_near((slot_vec[0], slot_vec[2]), vec_got[0])
        common = common + vec_got[1]
        vec_send = jnp.concatenate([vec_2, common])
        done(vec_send, *flight)
        landed(hold(flight), *groups)
        total3 = [t for part in (*ha, *hb) for t in part.totals()]
        near3 = z_near(jnp.stack([total3[1], total3[3]]))
        vec_got = z_far(hold(vec_send))
        done(*total3, near2)
        mine2, far2 = after_near((total2[0], total2[2]), hold(near2))
        far12 = jnp.stack([far1, far2.astype(BF)])
        done(far12, *tok_2)
        tok_2, far12 = hold((tok_2, far12))
        tok_3 = hop_three(*tok_2)
        far12 = z_far(far12)
        grad_tokens = place(at, n_tensor, (tok_own, *tok_1, *tok_2, tok_2[0]), F32)
        grad_tokens, near3 = run((grad_tokens, near3))
        mine3, far3 = after_near((total3[0], total3[2]), near3)
        far3 = z_far(far3.astype(BF))
        done(far12, far3)
        done(hold(far12))
        mine12 = outer_rest(jnp.stack([mine1, mine2]) + hold(far12).astype(F32))
        got12 = by_y(mine12.astype(BF))
        done(mine12)
        output = place(at, n_tensor, (output_own, *out_1, *out_2, hold(out_3[0])), BF)
        output = output.reshape(seq_count, seq_len, width)
        done(output, vec_got)
        vectors = jnp.concatenate([vec_0, common]) + hold(vec_got)
        vec_got = by_core(vectors)
        mine3 = outer_rest(mine3 + hold(far3).astype(F32))
        got3 = by_y(mine3.astype(BF))
        done(mine3, vec_got)
        vectors = vectors + hold(vec_got)
        vec_got = by_x(vectors)
        done(got12)
        got12 = hold(got12)
        done_wdown = whole_rows(mine12[0], got12[0])
        done_win = whole_rows(mine12[1], got12[1])
        done(done_wdown, done_win, got3, vec_got)
        got3, vec_got = hold((got3, vec_got))
        vectors = vectors + vec_got
        vec_got = by_y(vectors)
        done_last = whole_rows(mine3, got3)
        vectors = vectors + hold(vec_got)
        bit = 2
        while bit < n_outer:
            vectors = vectors + swap(vectors, "outer", n_outer, bit)
            bit *= 2
        slot_sum = vectors[:n_slot].reshape(-1)
        common = vectors[n_slot:].reshape(6, width)
        common = jnp.stack([common[i] for i in (0, 3, 1, 2, 4, 5)])
        part = lambda v, n: lax.dynamic_slice_in_dim(v, l_index * (n // n_local), n // n_local, v.ndim - 1)
        binner = part(slot_sum[:hidden_cols].reshape(b_inner.shape), head_size)
        bqv = part(slot_sum[hidden_cols:].reshape(b_qv.shape), head_size)
        common = part(common, width)
        grad_wqkv = done_last[:, : 3 * head_cols].reshape(width // n_local, 3, head_cols).transpose(1, 0, 2)
        done(grad_wqkv, common, binner, bqv, *tok_3)
        grad_tokens = place_end(at, *hold((tok_own, tok_3[0], grad_tokens)))
        grad_tokens = grad_tokens.reshape(seq_count, seq_len, width)
        return (
            output,
            grad_tokens,
            grad_wqkv,
            bqv,
            done_last[:, 3 * head_cols :].T,
            done_win,
            binner,
            done_wdown.T,
            common[:2],
            common[2:],
        )

    return local


def solution(mesh):
    placed = (
        P(("outer", "local"), None, None),
        P(("outer", "local"), None),
        P(None, None, "tensor"),
        P(None, "tensor", None),
        P("tensor", None),
        P(None, "tensor"),
        P("tensor", None),
        P("tensor", None),
        P(),
        P(),
        P(("outer", "local"), None, None),
    )
    return jax.shard_map(
        make(dict(mesh.shape)),
        mesh=mesh,
        in_specs=placed,
        out_specs=(
            P(("outer", "local"), None, None),
            P(("outer", "local"), None, None),
            P(None, "local", "tensor"),
            P(None, "tensor", "local"),
            P("tensor", "local"),
            P("local", "tensor"),
            P("tensor", "local"),
            P("tensor", "local"),
            P(None, "local"),
            P(None, "local"),
        ),
        check_vma=False,
    )
```
